32 devices in a mesh: expert: 4 (over y, x), shard: 8 (over z, core).
Axes of the slice: x: 2, y: 2, z: 4, core: 2. Of those that a mesh axis runs over, the one named last changes fastest.
Arguments:
- inputs: bfloat16 [8, 1024, 2048], P('shard', 'expert'), may hold values from -6 to 6
- cotangent: bfloat16 [8, 1024, 2048], P('shard', 'expert'), may hold values from -6 to 6
- blocks: int32 [8, 1024], P('shard', 'expert'), may hold values from 0 to 3, never falling along the last dimension, each value on 1 to 512 neighbouring positions
- attn_routes: int32 [8, 1024, 2], P('shard', 'expert'), may hold values from 0 to 3, all different within a row; in each aligned block of 256 rows (0 to 255, 256 to 511, ..., all dimensions but the last counted through in order) at most 160 rows name the same one
- ffn_routes: int32 [8, 1024, 2], P('shard', 'expert'), may hold values from 0 to 3, all different within a row; in each aligned block of 256 rows (0 to 255, 256 to 511, ..., all dimensions but the last counted through in order) at most 160 rows name the same one
- w_key: bfloat16 [2048, 2048], P(('expert', 'shard')), may hold values from -0.125 to 0.125
- w_value: bfloat16 [2048, 2048], P(('expert', 'shard')), may hold values from -0.125 to 0.125
- attn_router: bfloat16 [2048, 4], P(('expert', 'shard')), may hold values from -0.09375 to 0.09375
- ffn_router: bfloat16 [2048, 4], P(('expert', 'shard')), may hold values from -0.09375 to 0.09375
- attn_gain: bfloat16 [2048], P(('expert', 'shard')), may hold values from 0.5 to 1.5
- ffn_gain: bfloat16 [2048], P(('expert', 'shard')), may hold values from 0.5 to 1.5
- attn_bias: bfloat16 [2048], P(('expert', 'shard')), may hold values from -0.59765625 to 0.59765625
- ffn_bias: bfloat16 [2048], P(('expert', 'shard')), may hold values from -0.59765625 to 0.59765625
- w_query: bfloat16 [4, 2048, 2048], P('expert', 'shard'), may hold values from -0.125 to 0.125
- w_out: bfloat16 [4, 2048, 2048], P('expert', 'shard'), may hold values from -1.5 to 1.5
- w_gate: bfloat16 [4, 2048, 5632], P('expert', 'shard'), may hold values from -0.125 to 0.125
- w_up: bfloat16 [4, 2048, 5632], P('expert', 'shard'), may hold values from -0.125 to 0.125
- w_down: bfloat16 [4, 5632, 2048], P('expert', 'shard'), may hold values from -0.078125 to 0.078125
Outputs:
- outputs: bfloat16 [8, 1024, 2048], P('shard', 'expert')
- input_grad: bfloat16 [8, 1024, 2048], P('shard', 'expert')
- grad_w_key: float32 [2048, 2048], P(('expert', 'shard'))
- grad_w_value: float32 [2048, 2048], P(('expert', 'shard'))
- grad_attn_router: float32 [2048, 4], P(('expert', 'shard'))
- grad_ffn_router: float32 [2048, 4], P(('expert', 'shard'))
- grad_attn_gain: float32 [2048], P(('expert', 'shard'))
- grad_ffn_gain: float32 [2048], P(('expert', 'shard'))
- grad_attn_bias: float32 [2048], P(('expert', 'shard'))
- grad_ffn_bias: float32 [2048], P(('expert', 'shard'))
- grad_w_query: float32 [4, 2048, 2048], P('expert', 'shard')
- grad_w_out: float32 [4, 2048, 2048], P('expert', 'shard')
- grad_w_gate: float32 [4, 2048, 5632], P('expert', 'shard')
- grad_w_up: float32 [4, 2048, 5632], P('expert', 'shard')
- grad_w_down: float32 [4, 5632, 2048], P('expert', 'shard')
The draws below stay inside these ranges and needn't reach their ends.
Inputs may be any that keep to these rules, and one draw needn't show every extreme that they name: `attn_routes`: each token names 2 different experts. Among the 256 tokens of one device (aligned blocks of rows), no expert is named by more than 160 tokens, and in some blocks one expert is named by exactly 160. `ffn_routes`: each token names 2 different experts. Among the 256 tokens of one device (aligned blocks of rows), no expert is named by more than 160 tokens, and in some blocks one expert is named by exactly 160. `blocks`: in every sequence the block ids start at 0, never fall and rise by one at a time; a block holds 1 to 512 positions, and one holds exactly 512.
All inputs are finite; a program needn't handle non-finite values.
Results may differ from the reference program's by a relative error of at most 0.02.
Values may be sent and summed in bfloat16 or wider, within the bound.
A program may use at most 512 MiB of HBM per device.

```python
import math
import jax
import jax.numpy as jnp
import numpy as np
from jax import lax

D = 2048
KVH = 16
HD = 128
FF = 5632
TOPK = 2
TOK_DEV = 256
BLOCK = 256
EXPERTS = 4
EH = 2048
LENGTH = 1024
SEQS = 8
CAP = 160
N_EXPERT = 4


def block_scale(rng, extent, pieces, smallest, top_value):
    def one(dim, shards_of):
        steps = jax.random.uniform(jax.random.fold_in(jax.random.fold_in(rng, 6), dim), (shards_of,), jnp.float32, smallest / len(pieces), top_value / len(pieces))
        return jnp.repeat(jnp.exp(steps), extent[dim] // shards_of).reshape((-1,) + (1,) * (len(extent) - dim - 1))

    level = one(*pieces[0])
    for cut in pieces[1:]:
        level = level * one(*cut)
    return level


def split_up(number_of, total, reach, skew):
    weights = [(1 << 20) // math.isqrt(rank ** skew) + 1 for rank in range(2, number_of + 1)]
    surplus, counts = total - reach - (number_of - 1), [1] * (number_of - 1)
    while surplus > 0:
        candidates = [i for i in range(number_of - 1) if counts[i] < reach]
        pool, budget = sum([weights[i] for i in candidates]), surplus
        for i in candidates:
            addition = min(reach - counts[i], max(1, budget * weights[i] // pool), surplus)
            counts[i] = counts[i] + addition
            surplus = surplus - addition
    return np.array([reach] + counts)


def ragged(key, number_of, total, bound, lean):
    if number_of == 2:
        one = jax.random.randint(key, (), max(1, total - bound), min(bound, total - 1) + 1)
        return jnp.stack([one, total - one])
    lengths = jnp.asarray(split_up(number_of, total, bound, lean), jnp.int32)
    couples = (number_of - 1) // 2
    giver, sink = lengths[1:1 + 2 * couples:2], lengths[2:2 + 2 * couples:2]
    room = jnp.minimum(giver - 1, bound - sink)
    passed = jax.random.randint(jax.random.fold_in(key, 1), (couples,), 0, 1 << 20) % (room + 1)
    lengths = lengths.at[1:1 + 2 * couples:2].set(giver - passed).at[2:2 + 2 * couples:2].set(sink + passed)
    return lengths[jax.random.permutation(jax.random.fold_in(key, 2), number_of)]


def assign_block(stream_key, own, number, rows, count, top, reach, skew):
    order = jax.random.permutation(stream_key, count)
    crowded, common = shares(count, rows * top, reach, skew, True), shares(count, rows * top, reach, skew, False)
    places = jnp.arange(count)

    def named(lengths, rotation):
        used = int((lengths > 0).sum())
        fixed = max(1, used // 4)
        moved = fixed + (places - fixed + rotation * (used - fixed)) % max(1, count - fixed)
        return jnp.zeros((count,), jnp.int32).at[order[jnp.where(places < fixed, places, moved)]].set(jnp.asarray(lengths, jnp.int32))

    lengths = jnp.where(number % 4 == 0, named(crowded, number // 4), named(common, number - number // 4 - 1))
    mixed = jax.random.permutation(jax.random.fold_in(own, 3), count)
    donor, receiver = mixed[0:count // 2 * 2:2], mixed[1:count // 2 * 2:2]
    slack = jnp.minimum(lengths[donor] - 1, reach - lengths[receiver]) // 2
    slack = jnp.where((donor == order[0]) | (receiver == order[0]) | (lengths[receiver] == 0), 0, jnp.maximum(slack, 0))
    moved = jax.random.randint(jax.random.fold_in(own, 4), (count // 2,), 0, 1 << 20) % (slack + 1)
    lengths = lengths.at[donor].add(-moved).at[receiver].add(moved)
    labels = jnp.searchsorted(jnp.cumsum(lengths), jnp.arange(rows * top), side="right").astype(jnp.int32)
    grid = labels.reshape(top, rows).T
    grid = grid[jax.random.permutation(jax.random.fold_in(own, 1), rows)]
    rotation = jax.random.randint(jax.random.fold_in(own, 2), (rows, 1), 0, top)
    return jnp.take_along_axis(grid, (jnp.arange(top)[None, :] + rotation) % top, axis=1)


def shares(amount, total, bound, skew, full):
    portions = [(1 << 20) // math.isqrt(rank ** skew) + 1 for rank in range(1, amount + 1)]
    largest = bound if full else min(bound, max(-(-total // amount), total * portions[0] // sum(portions)))
    least = 1 if total - largest >= amount - 1 else 0
    given, surplus = [largest] + [least] * (amount - 1), total - largest - least * (amount - 1)
    while surplus > 0:
        free = [i for i in range(1, amount) if given[i] < largest] or [i for i in range(1, amount) if given[i] < bound]
        whole, left = sum([portions[i] for i in free]), surplus
        for i in free:
            addition = min(bound - given[i], max(1, left * portions[i] // whole), surplus)
            given[i] = given[i] + addition
            surplus = surplus - addition
    return np.array(given)


def scatter_about(own_key, dims, width, bound, split=(), kind=jnp.bfloat16):
    values = jax.random.normal(own_key, dims, jnp.float32) * width
    if len(split) > 0:
        values = block_scale(own_key, dims, split, -0.22, 0.18) * values
    return jnp.clip(values, min=-bound, max=bound).astype(kind)


def setup_inputs(seed: int = 0) -> dict:
    key_list = jax.random.split(jax.random.key(seed), 19)
    inputs = scatter_about(key_list[0], (SEQS, LENGTH, D), 1.0, 6.0, ((0, 8), (1, 4)))
    cotangent = scatter_about(key_list[1], (SEQS, LENGTH, D), 1.0, 6.0, ((0, 8), (1, 4)))
    blocks = jax.vmap(lambda own: jnp.searchsorted(jnp.cumsum(ragged(own, LENGTH // BLOCK, LENGTH, 2 * BLOCK, 1)), jnp.arange(LENGTH), side="right"))(jax.random.split(key_list[2], SEQS)).reshape((SEQS, LENGTH)).astype(jnp.int32)
    attn_routes_keys = jax.random.split(jax.random.fold_in(key_list[3], 1), SEQS * LENGTH // TOK_DEV)
    attn_routes_turns = jax.random.permutation(jax.random.fold_in(key_list[3], 3), SEQS * LENGTH // TOK_DEV)
    attn_routes = jax.vmap(lambda own, number: assign_block(jax.random.fold_in(key_list[3], 2), own, number, TOK_DEV, EXPERTS, TOPK, CAP, 2))(attn_routes_keys, attn_routes_turns).reshape((SEQS, LENGTH, TOPK))
    ffn_routes_keys = jax.random.split(jax.random.fold_in(key_list[4], 1), SEQS * LENGTH // TOK_DEV)
    ffn_routes_turns = jax.random.permutation(jax.random.fold_in(key_list[4], 3), SEQS * LENGTH // TOK_DEV)
    ffn_routes = jax.vmap(lambda own, number: assign_block(jax.random.fold_in(key_list[4], 2), own, number, TOK_DEV, EXPERTS, TOPK, CAP, 2))(ffn_routes_keys, ffn_routes_turns).reshape((SEQS, LENGTH, TOPK))
    w_key = scatter_about(key_list[5], (D, EH), D ** -0.5, 0.125, ((0, 32),))
    w_value = scatter_about(key_list[6], (D, EH), D ** -0.5, 0.125, ((0, 32),))
    attn_router = scatter_about(key_list[7], (D, EXPERTS), (2 * D) ** -0.5, 0.09375, ((0, 32),))
    ffn_router = scatter_about(key_list[8], (D, EXPERTS), (2 * D) ** -0.5, 0.09375, ((0, 32),))
    attn_gain = jnp.clip(1.0 + 0.1 * jax.random.normal(key_list[9], (D,), jnp.float32), 0.5, 1.5).astype(jnp.bfloat16)
    ffn_gain = jnp.clip(1.0 + 0.1 * jax.random.normal(key_list[10], (D,), jnp.float32), 0.5, 1.5).astype(jnp.bfloat16)
    attn_bias = scatter_about(key_list[11], (D,), 0.1, 0.59765625, ((0, 32),))
    ffn_bias = scatter_about(key_list[12], (D,), 0.1, 0.59765625, ((0, 32),))
    w_query = scatter_about(key_list[13], (EXPERTS, D, EH), D ** -0.5, 0.125, ((0, 4), (1, 8)))
    w_out = scatter_about(key_list[14], (EXPERTS, EH, D), (max(EH * 8 // LENGTH, 1)) ** -0.5, 1.5, ((0, 4), (1, 8)))
    w_gate = scatter_about(key_list[15], (EXPERTS, D, FF), D ** -0.5, 0.125, ((0, 4), (1, 8)))
    w_up = scatter_about(key_list[16], (EXPERTS, D, FF), D ** -0.5, 0.125, ((0, 4), (1, 8)))
    w_down = scatter_about(key_list[17], (EXPERTS, FF, D), FF ** -0.5, 0.078125, ((0, 4), (1, 8)))
    return {"inputs": inputs, "cotangent": cotangent, "blocks": blocks, "attn_routes": attn_routes, "ffn_routes": ffn_routes, "w_key": w_key, "w_value": w_value, "attn_router": attn_router, "ffn_router": ffn_router, "attn_gain": attn_gain, "ffn_gain": ffn_gain, "attn_bias": attn_bias, "ffn_bias": ffn_bias, "w_query": w_query, "w_out": w_out, "w_gate": w_gate, "w_up": w_up, "w_down": w_down}


EPSILON = 1e-06
NEGATIVE = -1e+30
ROPE_BASE = 10000.0
PRECISE = lax.Precision.HIGHEST

@jax.custom_vjp
def low(v):
    return lax.optimization_barrier(v.astype(jnp.bfloat16)).astype(jnp.float32)

@jax.custom_vjp
def low_back(v):
    return v

def low_keep(v):
    return (low(v), None)

def low_pass(kept, grad):
    return (grad,)

def back_keep(v):
    return (v, None)

def back_low(kept, grad):
    return (low(grad),)
low.defvjp(low_keep, low_pass)
low_back.defvjp(back_keep, back_low)

def rms_norm(values, scaling):
    return values * lax.rsqrt(lax.optimization_barrier(jnp.mean(values * values, axis=-1, keepdims=True)) + EPSILON) * scaling

def rotary(tensor, position):
    half_width = tensor.shape[-1] // 2
    frequency = jnp.exp(-math.log(ROPE_BASE) * jnp.arange(half_width, dtype=jnp.float32) / half_width)
    angles = position[..., None, None] * frequency
    cosine = jnp.cos(angles)
    sine_part = jnp.sin(angles)
    first_half = tensor[..., :half_width]
    second_half = tensor[..., half_width:]
    return jnp.concatenate([first_half * cosine - second_half * sine_part, second_half * cosine + first_half * sine_part], axis=-1)

def gate_weights(logits, routes):
    picked = jnp.take_along_axis(logits, routes, axis=-1)
    return jax.nn.softmax(picked, axis=-1)

def matmul(left_side, right_side):
    return jnp.dot(left_side, right_side, precision=PRECISE)

def pick_rows(table, index_table):
    return jax.vmap(lambda matrix, picker: matrix[picker])(table, index_table)

def slot_tables(routes):
    spread = routes.reshape(SEQS, N_EXPERT, TOK_DEV * TOPK)
    onehot = (spread[..., None] == jnp.arange(EXPERTS, dtype=jnp.int32)).astype(jnp.int32)
    ranking = lax.optimization_barrier(jnp.sum(onehot * (jnp.cumsum(onehot, axis=2) - 1), axis=-1))
    source = jnp.arange(N_EXPERT, dtype=jnp.int32)[None, :, None]
    slot_index = (source * (EXPERTS * CAP) + spread * CAP + ranking).reshape(SEQS, LENGTH * TOPK)
    route_ids = jnp.broadcast_to(jnp.arange(LENGTH * TOPK, dtype=jnp.int32)[None, :], (SEQS, LENGTH * TOPK))
    sequence_index = jnp.broadcast_to(jnp.arange(SEQS, dtype=jnp.int32)[:, None], (SEQS, LENGTH * TOPK))
    total_slots = N_EXPERT * EXPERTS * CAP
    route_of_slot = jnp.zeros((SEQS, total_slots), jnp.int32).at[sequence_index, slot_index].set(route_ids)
    filled = jnp.zeros((SEQS, total_slots), jnp.int32).at[sequence_index, slot_index].set(1)
    return (slot_index.reshape(SEQS, LENGTH, TOPK), route_of_slot // TOPK, filled)

def slot_rows(hidden_rows, token_of_slot, filled):
    picked = pick_rows(hidden_rows, token_of_slot)
    return jnp.where(filled[..., None] > 0, picked, 0.0)

def to_experts(slots):
    trailing = slots.shape[2:]
    grouped = slots.reshape((SEQS, N_EXPERT, EXPERTS, CAP) + trailing)
    axes_order = (2, 0, 1, 3) + tuple(range(4, 4 + len(trailing)))
    return grouped.transpose(axes_order).reshape((EXPERTS * SEQS, N_EXPERT * CAP) + trailing)

def from_experts(results):
    grouped = results.reshape(EXPERTS, SEQS, N_EXPERT, CAP, -1)
    return grouped.transpose(1, 2, 0, 3, 4).reshape(SEQS, N_EXPERT * EXPERTS * CAP, -1)

def combine(returned, slot_index, gates):
    picked = pick_rows(returned, slot_index.reshape(SEQS, LENGTH * TOPK)).reshape(SEQS, LENGTH, TOPK, -1)
    return lax.optimization_barrier(jnp.sum(gates[..., None] * picked, axis=2))

def attend(query_rows, query_place, query_block, query_weight, out_weight, keys, values, key_blocks):
    row_count = query_rows.shape[0]
    queries = low(rotary(low_back(matmul(query_rows, query_weight)).reshape(row_count, KVH, HD), query_place.astype(jnp.float32)))
    raw_scores = jnp.einsum('rhd,lhd->hrl', queries, keys, precision=PRECISE) * HD ** (-0.5)
    allowed = key_blocks[None, None, :] <= query_block[None, :, None]
    scores = jnp.where(allowed, low_back(raw_scores), NEGATIVE)
    row_peak = lax.optimization_barrier(jnp.max(scores, axis=-1, keepdims=True))
    exponent = jnp.exp(scores - row_peak)
    probabilities = low(exponent / lax.optimization_barrier(jnp.sum(exponent, axis=-1, keepdims=True)))
    mixed_heads = jnp.einsum('hrl,lhd->rhd', probabilities, values, precision=PRECISE)
    mixed_heads = low(low_back(mixed_heads)).reshape(row_count, KVH * HD)
    return low(low_back(matmul(mixed_heads, out_weight)))

def expert_ffn(ffn_in, gate_weight, up_weight, down_weight):
    gate_pre = low_back(matmul(ffn_in, gate_weight))
    up_pre = low_back(matmul(ffn_in, up_weight))
    hidden = low(jax.nn.silu(gate_pre) * up_pre)
    return low(low_back(matmul(hidden, down_weight)))

def reference(inputs, cotangent, blocks, attn_routes, ffn_routes, w_key, w_value, attn_router, ffn_router, attn_gain, ffn_gain, attn_bias, ffn_bias, w_query, w_out, w_gate, w_up, w_down):
    params = tuple((weight.astype(jnp.float32) for weight in (w_key, w_value, attn_router, ffn_router, attn_gain, ffn_gain, attn_bias, ffn_bias, w_query, w_out, w_gate, w_up, w_down)))
    attn_slot, attn_token, attn_filled = slot_tables(attn_routes)
    ffn_slot, ffn_token, ffn_filled = slot_tables(ffn_routes)
    positions = jnp.broadcast_to(jnp.arange(LENGTH, dtype=jnp.int32).astype(jnp.float32)[None, :], (SEQS, LENGTH))
    query_place = to_experts(jnp.where(attn_filled > 0, attn_token, 0))
    query_block = to_experts(jnp.where(attn_filled > 0, pick_rows(blocks, attn_token), 0))

    def forward(block_in, weights):
        key_w, value_w, router_a, router_f, gain_a, gain_f, bias_a, bias_f, query_w, out_w, gate_w, up_w, down_w = weights
        h_attn = low(rms_norm(block_in, gain_a))
        gates_a = gate_weights(matmul(h_attn, router_a), attn_routes)
        keys = low(rotary(low_back(matmul(h_attn, key_w)).reshape(SEQS, LENGTH, KVH, HD), positions))
        values = low(low_back(matmul(h_attn, value_w))).reshape(SEQS, LENGTH, KVH, HD)
        attn_in = to_experts(low_back(slot_rows(h_attn, attn_token, attn_filled)))

        def attend_pair(pair_index):
            expert = pair_index // SEQS
            sequence = pair_index % SEQS
            return attend(attn_in[pair_index], query_place[pair_index], query_block[pair_index], query_w[expert], out_w[expert], keys[sequence], values[sequence], blocks[sequence])
        attn_back = from_experts(lax.map(jax.checkpoint(attend_pair), jnp.arange(EXPERTS * SEQS, dtype=jnp.int32)))
        middle = block_in + combine(attn_back, attn_slot, gates_a) + bias_a
        h_ffn = low(rms_norm(middle, gain_f))
        gates_f = gate_weights(matmul(h_ffn, router_f), ffn_routes)
        ffn_in = to_experts(low_back(slot_rows(h_ffn, ffn_token, ffn_filled))).reshape(EXPERTS, SEQS * N_EXPERT * CAP, D)

        def ffn_expert(expert):
            return expert_ffn(ffn_in[expert], gate_w[expert], up_w[expert], down_w[expert])
        ffn_out = lax.map(jax.checkpoint(ffn_expert), jnp.arange(EXPERTS, dtype=jnp.int32))
        ffn_back = from_experts(ffn_out.reshape(EXPERTS * SEQS, N_EXPERT * CAP, D))
        return middle + combine(ffn_back, ffn_slot, gates_f) + bias_f
    output_rows, pull_back = jax.vjp(forward, inputs.astype(jnp.float32), params)
    grad_in, all_grads = pull_back(cotangent.astype(jnp.float32))
    return (output_rows.astype(jnp.bfloat16), grad_in.astype(jnp.bfloat16), all_grads[0], all_grads[1], all_grads[2], all_grads[3], all_grads[4], all_grads[5], all_grads[6], all_grads[7], all_grads[8], all_grads[9], all_grads[10], all_grads[11], all_grads[12])
```

```python
import functools
import math

import jax
import jax.numpy as jnp
from jax import lax
from jax.experimental import pallas as pl
from jax.experimental.pallas import tpu as pltpu
from jax.sharding import PartitionSpec as P

HD = 128
TOPK = 2
EPSILON = 1e-06
NEGATIVE = -1e30
ROPE_BASE = 10000.0
PRECISE = lax.Precision.HIGHEST
BF = jnp.bfloat16
F32 = jnp.float32
LOG2E = 1.4426950408889634


def dot(a, b):
    return jnp.dot(a, b, preferred_element_type=F32)


def dot_tn(a, b, precision=None):
    return lax.dot_general(a, b, (((0,), (0,)), ((), ())), precision=precision, preferred_element_type=F32)


def dot_nt(a, b):
    return lax.dot_general(a, b, (((1,), (1,)), ((), ())), preferred_element_type=F32)


def inverse_rms(values):
    return lax.rsqrt(jnp.mean(values * values, axis=-1, keepdims=True) + EPSILON)


def norm_back(grad, values, inv, gain):
    u = grad * gain
    centre = jnp.mean(u * values, axis=-1, keepdims=True)
    return inv * (u - values * (inv * inv) * centre), jnp.sum(grad * values * inv, axis=0)


def rope_tables(position):
    half = HD // 2
    frequency = jnp.exp(-math.log(ROPE_BASE) * jnp.arange(half, dtype=F32) / half)
    angles = position[:, None] * frequency
    cosine, sine = jnp.cos(angles), jnp.sin(angles)
    return jnp.concatenate([cosine, cosine], -1), jnp.concatenate([-sine, sine], -1)


def rotate(tensor, cosine, sine):
    heads = tensor.reshape(tensor.shape[:-1] + (-1, HD))
    swapped = jnp.concatenate([heads[..., HD // 2:], heads[..., :HD // 2]], -1)
    return (heads * cosine[:, None, :] + swapped * sine[:, None, :]).reshape(tensor.shape)


def attend_kernel(scale, q_ref, k_ref, v_ref, qb_ref, kb_ref, o_ref, l_ref):
    s = dot_nt(k_ref[...], q_ref[...])
    s = jnp.where(kb_ref[...] <= qb_ref[0], s * (scale * LOG2E), NEGATIVE)
    peak = jnp.max(s, axis=0, keepdims=True)
    p = jnp.exp2(s - peak)
    total = jnp.sum(p, axis=0, keepdims=True)
    o = dot_tn(v_ref[...], p.astype(BF))
    o_ref[...] = (o / total).T.astype(BF)
    l_ref[0] = peak + jnp.log2(total)


def attend(q, k, v, q_blocks, k_blocks):
    rows, width = q.shape
    length = k.shape[0]
    heads = width // HD
    tile = 256
    return pl.pallas_call(
        functools.partial(attend_kernel, HD ** -0.5),
        grid=(heads, rows // tile),
        in_specs=[
            pl.BlockSpec((tile, HD), lambda h, i: (i, h)),
            pl.BlockSpec((length, HD), lambda h, i: (0, h)),
            pl.BlockSpec((length, HD), lambda h, i: (0, h)),
            pl.BlockSpec((1, 1, tile), lambda h, i: (0, 0, i)),
            pl.BlockSpec((length, 1), lambda h, i: (0, 0)),
        ],
        out_specs=[
            pl.BlockSpec((tile, HD), lambda h, i: (i, h)),
            pl.BlockSpec((1, 1, tile), lambda h, i: (h, 0, i)),
        ],
        out_shape=[
            jax.ShapeDtypeStruct((rows, width), BF),
            jax.ShapeDtypeStruct((heads, 1, rows), F32),
        ],
        cost_estimate=pl.CostEstimate(
            flops=4 * rows * length * width,
            transcendentals=rows * length * heads,
            bytes_accessed=4 * rows * width + 4 * length * width,
        ),
        name="attend",
    )(q, k, v, q_blocks.reshape(1, 1, rows), k_blocks.reshape(length, 1))


def attend_back_kernel(scale, q_ref, k_ref, v_ref, d_ref, o_ref, l_ref, qb_ref, kb_ref, dq_ref, dk_ref, dv_ref):
    q, k, d = q_ref[...], k_ref[...], d_ref[...]
    s = dot_nt(k, q)
    p = jnp.exp2(s * (scale * LOG2E) - l_ref[0])
    p = jnp.where(kb_ref[...] <= qb_ref[0], p, 0.0)
    centre = jnp.sum((d.astype(F32) * o_ref[...].astype(F32)).T, axis=0, keepdims=True)
    grad_p = dot_nt(v_ref[...], d)
    grad_s = (p * (grad_p - centre)).astype(BF)
    dq_ref[...] = (dot_tn(k, grad_s) * scale).T
    new_k = dot(grad_s, q) * scale
    new_v = dot(p.astype(BF), d)

    @pl.when(pl.program_id(1) == 0)
    def _():
        dk_ref[...] = new_k
        dv_ref[...] = new_v

    @pl.when(pl.program_id(1) > 0)
    def _():
        dk_ref[...] += new_k
        dv_ref[...] += new_v


def attend_back(q, k, v, d, o, total, q_blocks, k_blocks):
    rows, width = q.shape
    length = k.shape[0]
    heads = width // HD
    tile = 256
    row_spec = pl.BlockSpec((tile, HD), lambda h, i: (i, h))
    key_spec = pl.BlockSpec((length, HD), lambda h, i: (0, h))
    return pl.pallas_call(
        functools.partial(attend_back_kernel, HD ** -0.5),
        grid=(heads, rows // tile),
        in_specs=[
            row_spec, key_spec, key_spec, row_spec, row_spec,
            pl.BlockSpec((1, 1, tile), lambda h, i: (h, 0, i)),
            pl.BlockSpec((1, 1, tile), lambda h, i: (0, 0, i)),
            pl.BlockSpec((length, 1), lambda h, i: (0, 0)),
        ],
        out_specs=[row_spec, key_spec, key_spec],
        out_shape=[
            jax.ShapeDtypeStruct((rows, width), F32),
            jax.ShapeDtypeStruct((length, width), F32),
            jax.ShapeDtypeStruct((length, width), F32),
        ],
        cost_estimate=pl.CostEstimate(
            flops=10 * rows * length * width,
            transcendentals=rows * length * heads,
            bytes_accessed=10 * rows * width + 12 * length * width,
        ),
        name="attend_back",
    )(q, k, v, d, o, total, q_blocks.reshape(1, 1, rows), k_blocks.reshape(length, 1))


def pick(table, routes, ids):
    parts = jnp.split(table, len(ids), axis=1)
    return [sum(jnp.where(routes[:, j:j + 1] == e, part, 0.0) for e, part in zip(ids, parts)) for j in range(TOPK)]


def place(pieces, routes, ids):
    return jnp.concatenate(
        [sum(jnp.where(routes[:, j:j + 1] == e, pieces[j], 0.0) for j in range(TOPK)) for e in ids], axis=1
    )


def pair_softmax(logits):
    peak = jnp.maximum(logits[0], logits[1])
    powers = [jnp.exp(v - peak) for v in logits]
    total = powers[0] + powers[1]
    return [v / total for v in powers]


def local(
    inputs, cotangent, blocks, attn_routes, ffn_routes, w_key, w_value, attn_router, ffn_router, attn_gain, ffn_gain,
    attn_bias, ffn_bias, w_query, w_out, w_gate, w_up, w_down,
):
    n_e, n_s = lax.axis_size("expert"), lax.axis_size("shard")
    me = lax.axis_index("expert")
    tokens, width = inputs.shape[1:]
    ids = list(range(n_e))
    capacity = 5 * tokens * TOPK // (4 * n_e)
    group = w_key.shape[1] // n_e
    length = n_e * tokens
    small_rows = w_key.shape[0]

    def swap(value, k):
        return lax.ppermute(value, "expert", [(i, i ^ k) for i in range(n_e)])

    def spread(value):
        return jnp.concatenate([value] + [swap(value, k) for k in range(1, n_e)], axis=0)

    def collect(value):
        parts = jnp.split(value, n_e, axis=0)
        return sum([parts[0].astype(F32)] + [swap(parts[k], k).astype(F32) for k in range(1, n_e)])

    def shuffle(value, axis):
        return lax.all_to_all(value, axis, split_axis=0, concat_axis=0, tiled=True)

    def gather_shard(value):
        return lax.all_gather(value, "shard", axis=0, tiled=True)

    def scatter_shard(value):
        return lax.psum_scatter(value, "shard", scatter_dimension=0, tiled=True)

    small = jnp.concatenate(
        [attn_router, ffn_router, attn_gain[:, None], ffn_gain[:, None], attn_bias[:, None], ffn_bias[:, None]], axis=1
    )
    small_width = small.shape[1]
    small = jnp.pad(small, ((0, 0), (0, 128 - small_width)))
    packed = jnp.concatenate(
        [
            w_key.reshape(small_rows, n_e, group).transpose(1, 0, 2),
            w_value.reshape(small_rows, n_e, group).transpose(1, 0, 2),
            jnp.broadcast_to(small[None], (n_e,) + small.shape),
        ],
        axis=2,
    )
    packed = gather_shard(shuffle(packed, "expert")[None])
    packed = packed.transpose(1, 0, 2, 3).reshape(width, -1)
    key_value_w = packed[:, :2 * group]
    small = packed[:, 2 * group:2 * group + small_width].astype(F32)
    router_a, router_f = small[:, :n_e], small[:, n_e:2 * n_e]
    gain_a, gain_f, bias_a, bias_f = (small[:, 2 * n_e + i] for i in range(4))

    def to_heads(value):
        rows = value.shape[0]
        value = shuffle(value.reshape(rows, n_e, group).transpose(1, 0, 2), "expert")
        return gather_shard(value.transpose(1, 0, 2).reshape(rows, n_e * group))

    def from_heads(value):
        value = scatter_shard(value)
        rows = value.shape[0]
        value = shuffle(value.reshape(rows, n_e, group).transpose(1, 0, 2), "expert")
        return value.transpose(1, 0, 2).reshape(rows, n_e * group)

    query_w = to_heads(w_query[0])
    out_rows = w_out.shape[1]
    turned = shuffle(w_out[0].T, "shard").reshape(n_s, width // n_s, out_rows).transpose(1, 0, 2)
    out_wt = to_heads(turned.reshape(width // n_s, n_s * out_rows))

    def to_columns(value):
        rows = value.shape[0]
        return shuffle(value.reshape(rows, n_s, -1).transpose(1, 0, 2), "shard").reshape(rows * n_s, -1)

    def from_columns(value):
        rows = value.shape[0] // n_s
        value = shuffle(value, "shard").reshape(n_s, rows, -1)
        return value.transpose(1, 0, 2).reshape(rows, -1)

    gate_own, up_own, down_own = to_columns(w_gate[0]), to_columns(w_up[0]), w_down[0]
    gate_w = [gate_own] + [swap(gate_own, k) for k in range(1, n_e)]
    up_w = [up_own] + [swap(up_own, k) for k in range(1, n_e)]
    down_w = [down_own] + [swap(down_own, k) for k in range(1, n_e)]

    own = inputs[0].astype(F32)
    cot = cotangent[0]
    seq_in = spread(inputs[0]).astype(F32)
    meta = spread(jnp.concatenate([blocks, attn_routes[0].T], axis=0)[None])
    seq_blocks = meta[:, 0].reshape(-1)
    routes_a = meta[:, 1:].transpose(0, 2, 1).reshape(-1, TOPK)
    position = jnp.concatenate([(me ^ k) * tokens + jnp.arange(tokens, dtype=jnp.int32) for k in range(n_e)]).astype(F32)
    cosine, sine = rope_tables(position)
    h_attn = (seq_in * inverse_rms(seq_in) * gain_a).astype(BF)
    logits_a = dot(h_attn, router_a.astype(BF))
    gates_a = pair_softmax(pick(logits_a, routes_a, ids))
    key_value = dot(h_attn, key_value_w)
    keys = rotate(key_value[:, :group], cosine, sine).astype(BF)
    values = key_value[:, group:].astype(BF)
    queries = pick(dot(h_attn, query_w), routes_a, ids)
    queries = jnp.concatenate([rotate(v, cosine, sine).astype(BF) for v in queries], axis=0)
    row_blocks = jnp.concatenate([seq_blocks, seq_blocks])
    mixed_rows, log_total = attend(queries, keys, values, row_blocks, seq_blocks)
    mixed = [v.astype(F32) for v in jnp.split(mixed_rows, TOPK, axis=0)]
    mixed_all = place([gates_a[j] * mixed[j] for j in range(TOPK)], routes_a, ids).astype(BF)
    middle = own + collect(dot_nt(mixed_all, out_wt).astype(BF)) + bias_a

    inv_f = inverse_rms(middle)
    h_ffn = (middle * inv_f * gain_f).astype(BF)
    h_all = gather_shard(h_ffn)
    cot_all = gather_shard(cot)
    routes_f = gather_shard(ffn_routes[0].T[None])
    logits_f = dot(h_all, router_f.astype(BF))
    flat_routes = routes_f.transpose(0, 2, 1).reshape(-1, TOPK)
    gates_f = pair_softmax(pick(logits_f, flat_routes, ids))
    h_blocks = h_all.reshape(n_s, tokens, width)
    cot_blocks = cot_all.reshape(n_s, tokens, width)
    triangle = (jnp.arange(tokens)[:, None] <= jnp.arange(tokens)[None, :]).astype(BF)

    def rows_of(select, source):
        return lax.dot_general(
            select, source, (((2,), (1,)), ((0,), (0,))), preferred_element_type=F32
        ).astype(BF).reshape(n_s * capacity, width)

    selects, out_rows_f, back_rows_f = [], [], []
    grad_gate_f = [0.0] * TOPK
    weight_grads = []
    for k in range(n_e):
        expert = me ^ k
        named = [routes_f[:, j] == expert for j in range(TOPK)]
        any_named = named[0] | named[1]
        rank = dot(any_named.astype(BF), triangle).astype(jnp.int32) - 1
        hit = (rank[:, None, :] == jnp.arange(capacity, dtype=jnp.int32)[None, :, None]) & any_named[:, None, :]
        select = hit.astype(BF)
        gate_token = sum(jnp.where(named[j], gates_f[j].reshape(n_s, tokens), 0.0) for j in range(TOPK))
        gate_slot = jnp.sum(jnp.where(hit, gate_token[:, None, :], 0.0), axis=2).reshape(-1, 1)
        rows, cot_rows = rows_of(select, h_blocks), rows_of(select, cot_blocks)
        gate_pre, up_pre = dot(rows, gate_w[k]), dot(rows, up_w[k])
        grad_hidden = dot_nt(cot_rows, down_w[k])
        sigma = 1.0 / (1.0 + jnp.exp(-gate_pre))
        silu = gate_pre * sigma
        hidden = silu * up_pre
        grad_slot = jnp.sum(grad_hidden * hidden, axis=1).reshape(n_s, capacity)
        grad_hidden = grad_hidden * gate_slot
        hidden = (hidden * gate_slot).astype(BF)
        grad_gate = (grad_hidden * up_pre * sigma * (1.0 + gate_pre * (1.0 - sigma))).astype(BF)
        grad_up = (grad_hidden * silu).astype(BF)
        back = (dot_nt(grad_gate, gate_w[k]) + dot_nt(grad_up, up_w[k])).astype(BF)
        selects.append(select)
        back_rows_f.append(back.reshape(n_s, capacity, width))
        out_rows_f.append(dot(hidden, down_w[k]).astype(BF).reshape(n_s, capacity, width))
        grad_token = jnp.sum(jnp.where(hit, grad_slot[:, :, None], 0.0), axis=1)
        grad_gate_f = [grad_gate_f[j] + jnp.where(named[j], grad_token, 0.0) for j in range(TOPK)]
        weight_grads.append(
            (dot_tn(rows, grad_gate).astype(BF), dot_tn(rows, grad_up).astype(BF), dot_tn(hidden, cot_rows).astype(BF))
        )
    select = jnp.concatenate(selects, axis=1)

    def tokens_of(row_list):
        return lax.dot_general(
            select, jnp.concatenate(row_list, axis=1), (((1,), (1,)), ((0,), (0,))), preferred_element_type=F32
        ).astype(BF).reshape(n_s * tokens, width)

    back_f = scatter_shard(tokens_of(back_rows_f)).astype(F32)
    ffn_out = scatter_shard(tokens_of(out_rows_f)).astype(F32)
    outputs = (middle + ffn_out + bias_f).astype(BF)[None]
    grad_gates_f = jnp.sum(
        shuffle(jnp.stack(grad_gate_f, axis=1).reshape(n_s, TOPK * tokens), "shard"), axis=0
    ).reshape(TOPK, tokens, 1)

    def expert_sum(which):
        return weight_grads[0][which].astype(F32) + sum(
            swap(weight_grads[k][which], k).astype(F32) for k in range(1, n_e)
        )

    grad_gate_w = from_columns(expert_sum(0).astype(BF)).astype(F32)[None]
    grad_up_w = from_columns(expert_sum(1).astype(BF)).astype(F32)[None]
    grad_down_w = expert_sum(2)[None]

    grad_out = cot.astype(F32)
    own_routes_f = ffn_routes[0]
    own_gates_f = pair_softmax(pick(dot(h_ffn, router_f.astype(BF)), own_routes_f, ids))

    def logit_grads(gates, grads, routes):
        centre = sum(gates[j] * grads[j] for j in range(TOPK))
        return place([gates[j] * (grads[j] - centre) for j in range(TOPK)], routes, ids)

    grad_logits_f = logit_grads(own_gates_f, grad_gates_f, own_routes_f)
    grad_router_f = dot_tn(h_ffn.astype(F32), grad_logits_f, PRECISE)
    grad_h_ffn = back_f + jnp.dot(grad_logits_f, router_f.T, precision=PRECISE)
    grad_norm, grad_gain_f = norm_back(grad_h_ffn, middle, inv_f, gain_f)
    grad_middle = grad_out + grad_norm
    grad_bias_f = jnp.sum(grad_out, axis=0)
    grad_bias_a = jnp.sum(grad_middle, axis=0)

    seq_grad = spread(grad_middle.astype(BF))
    grad_mixed = pick(dot(seq_grad, out_wt), routes_a, ids)
    grad_gates_a = [collect(jnp.sum(grad_mixed[j] * mixed[j], axis=1, keepdims=True)) for j in range(TOPK)]
    grad_mixed = jnp.concatenate([(gates_a[j] * grad_mixed[j]).astype(BF) for j in range(TOPK)], axis=0)
    grad_out_wt = dot_tn(seq_grad, mixed_all).astype(BF)
    grad_q, grad_k, grad_v = attend_back(queries, keys, values, grad_mixed, mixed_rows, log_total, row_blocks, seq_blocks)
    grad_q = [rotate(v, cosine, -sine) for v in jnp.split(grad_q, TOPK, axis=0)]
    grad_query_all = place(grad_q, routes_a, ids).astype(BF)
    grad_key_value = jnp.concatenate([rotate(grad_k, cosine, -sine), grad_v], axis=1).astype(BF)
    back_a = collect((dot_nt(grad_query_all, query_w) + dot_nt(grad_key_value, key_value_w)).astype(BF))
    grad_query_w = from_heads(dot_tn(h_attn, grad_query_all).astype(BF)).astype(F32)[None]
    value = from_heads(grad_out_wt)
    value = value.reshape(width // n_s, n_s, out_rows).transpose(1, 0, 2)
    grad_out_w = shuffle(value, "shard").reshape(width, out_rows).T.astype(F32)[None]
    value = dot_tn(h_attn, grad_key_value).astype(BF).reshape(n_e, n_s, small_rows, 2 * group).transpose(1, 0, 2, 3)
    value = shuffle(scatter_shard(value)[0], "expert")
    grad_key_w = value[:, :, :group].transpose(1, 0, 2).reshape(small_rows, -1).astype(F32)
    grad_value_w = value[:, :, group:].transpose(1, 0, 2).reshape(small_rows, -1).astype(F32)

    h_own = h_attn[:tokens]
    own_routes_a = attn_routes[0]
    own_gates_a = [v[:tokens] for v in gates_a]
    grad_logits_a = logit_grads(own_gates_a, grad_gates_a, own_routes_a)
    grad_router_a = dot_tn(h_own.astype(F32), grad_logits_a, PRECISE)
    grad_h_attn = back_a + jnp.dot(grad_logits_a, router_a.T, precision=PRECISE)
    grad_norm, grad_gain_a = norm_back(grad_h_attn, own, inverse_rms(own), gain_a)
    input_grad = (grad_middle + grad_norm).astype(BF)[None]

    shared = jnp.concatenate(
        [grad_router_a, grad_router_f]
        + [v[:, None] for v in (grad_gain_a, grad_gain_f, grad_bias_a, grad_bias_f)],
        axis=1,
    )
    shared = shuffle(shared.reshape(n_e * n_s, -1), ("expert", "shard"))
    shared = jnp.sum(shared, axis=0).reshape(small_rows, small_width)
    return (
        outputs,
        input_grad,
        grad_key_w,
        grad_value_w,
        shared[:, :n_e],
        shared[:, n_e:2 * n_e],
        shared[:, 2 * n_e],
        shared[:, 2 * n_e + 1],
        shared[:, 2 * n_e + 2],
        shared[:, 2 * n_e + 3],
        grad_query_w,
        grad_out_w,
        grad_gate_w,
        grad_up_w,
        grad_down_w,
    )


def solution(mesh):
    rows = P("shard", "expert", None)
    shared, vector = P(("expert", "shard"), None), P(("expert", "shard"))
    weight = P("expert", "shard", None)
    in_specs = (rows, rows, P("shard", "expert"), rows, rows) + (shared,) * 4 + (vector,) * 4 + (weight,) * 5
    out_specs = (rows, rows) + (shared,) * 4 + (vector,) * 4 + (weight,) * 5
    return jax.shard_map(local, mesh=mesh, in_specs=in_specs, out_specs=out_specs, check_vma=False)
```

```python
import functools
import math

import jax
import jax.numpy as jnp
from jax import lax
from jax.experimental import pallas as pl
from jax.experimental.pallas import tpu as pltpu
from jax.sharding import PartitionSpec as P

HD = 128
TOPK = 2
EPSILON = 1e-06
NEGATIVE = -1e30
ROPE_BASE = 10000.0
PRECISE = lax.Precision.HIGHEST
BF = jnp.bfloat16
F32 = jnp.float32
LOG2E = 1.4426950408889634


def dot(a, b):
    return jnp.dot(a, b, preferred_element_type=F32)


def dot_tn(a, b, precision=None):
    return lax.dot_general(a, b, (((0,), (0,)), ((), ())), precision=precision, preferred_element_type=F32)


def dot_nt(a, b):
    return lax.dot_general(a, b, (((1,), (1,)), ((), ())), preferred_element_type=F32)


def inverse_rms(values):
    return lax.rsqrt(jnp.mean(values * values, axis=-1, keepdims=True) + EPSILON)


def norm_back(grad, values, inv, gain):
    u = grad * gain
    centre = jnp.mean(u * values, axis=-1, keepdims=True)
    return inv * (u - values * (inv * inv) * centre), jnp.sum(grad * values * inv, axis=0)


def rope_tables(position):
    half = HD // 2
    frequency = jnp.exp(-math.log(ROPE_BASE) * jnp.arange(half, dtype=F32) / half)
    angles = position[:, None] * frequency
    cosine, sine = jnp.cos(angles), jnp.sin(angles)
    return jnp.concatenate([cosine, cosine], -1), jnp.concatenate([-sine, sine], -1)


def rotate(tensor, cosine, sine):
    heads = tensor.reshape(tensor.shape[:-1] + (-1, HD))
    swapped = jnp.concatenate([heads[..., HD // 2:], heads[..., :HD // 2]], -1)
    return (heads * cosine[:, None, :] + swapped * sine[:, None, :]).reshape(tensor.shape)


def attend_kernel(scale, q_ref, k_ref, v_ref, qb_ref, kb_ref, o_ref, l_ref):
    s = dot_nt(k_ref[...], q_ref[...])
    s = jnp.where(kb_ref[...] <= qb_ref[0], s * (scale * LOG2E), NEGATIVE)
    peak = jnp.max(s, axis=0, keepdims=True)
    p = jnp.exp2(s - peak)
    total = jnp.sum(p, axis=0, keepdims=True)
    o = dot_tn(v_ref[...], p.astype(BF))
    o_ref[...] = (o / total).T.astype(BF)
    l_ref[0] = peak + jnp.log2(total)


def attend(q, k, v, q_blocks, k_blocks):
    rows, width = q.shape
    length = k.shape[0]
    heads = width // HD
    tile = 256
    return pl.pallas_call(
        functools.partial(attend_kernel, HD ** -0.5),
        grid=(heads, rows // tile),
        in_specs=[
            pl.BlockSpec((tile, HD), lambda h, i: (i, h)),
            pl.BlockSpec((length, HD), lambda h, i: (0, h)),
            pl.BlockSpec((length, HD), lambda h, i: (0, h)),
            pl.BlockSpec((1, 1, tile), lambda h, i: (0, 0, i)),
            pl.BlockSpec((length, 1), lambda h, i: (0, 0)),
        ],
        out_specs=[
            pl.BlockSpec((tile, HD), lambda h, i: (i, h)),
            pl.BlockSpec((1, 1, tile), lambda h, i: (h, 0, i)),
        ],
        out_shape=[
            jax.ShapeDtypeStruct((rows, width), BF),
            jax.ShapeDtypeStruct((heads, 1, rows), F32),
        ],
        cost_estimate=pl.CostEstimate(
            flops=rows * length, transcendentals=0, bytes_accessed=4 * rows * width
        ),
        name="attend",
    )(q, k, v, q_blocks.reshape(1, 1, rows), k_blocks.reshape(length, 1))


def attend_back_kernel(scale, q_ref, k_ref, v_ref, d_ref, o_ref, l_ref, qb_ref, kb_ref, dq_ref, dk_ref, dv_ref):
    q, k, d = q_ref[...], k_ref[...], d_ref[...]
    s = dot_nt(k, q)
    p = jnp.exp2(s * (scale * LOG2E) - l_ref[0])
    p = jnp.where(kb_ref[...] <= qb_ref[0], p, 0.0)
    centre = jnp.sum((d.astype(F32) * o_ref[...].astype(F32)).T, axis=0, keepdims=True)
    grad_p = dot_nt(v_ref[...], d)
    grad_s = (p * (grad_p - centre)).astype(BF)
    dq_ref[...] = (dot_tn(k, grad_s) * scale).T
    new_k = dot(grad_s, q) * scale
    new_v = dot(p.astype(BF), d)

    @pl.when(pl.program_id(1) == 0)
    def _():
        dk_ref[...] = new_k
        dv_ref[...] = new_v

    @pl.when(pl.program_id(1) > 0)
    def _():
        dk_ref[...] += new_k
        dv_ref[...] += new_v


def attend_back(q, k, v, d, o, total, q_blocks, k_blocks):
    rows, width = q.shape
    length = k.shape[0]
    heads = width // HD
    tile = 256
    row_spec = pl.BlockSpec((tile, HD), lambda h, i: (i, h))
    key_spec = pl.BlockSpec((length, HD), lambda h, i: (0, h))
    return pl.pallas_call(
        functools.partial(attend_back_kernel, HD ** -0.5),
        grid=(heads, rows // tile),
        in_specs=[
            row_spec, key_spec, key_spec, row_spec, row_spec,
            pl.BlockSpec((1, 1, tile), lambda h, i: (h, 0, i)),
            pl.BlockSpec((1, 1, tile), lambda h, i: (0, 0, i)),
            pl.BlockSpec((length, 1), lambda h, i: (0, 0)),
        ],
        out_specs=[row_spec, key_spec, key_spec],
        out_shape=[
            jax.ShapeDtypeStruct((rows, width), F32),
            jax.ShapeDtypeStruct((length, width), F32),
            jax.ShapeDtypeStruct((length, width), F32),
        ],
        cost_estimate=pl.CostEstimate(
            flops=rows * length, transcendentals=0, bytes_accessed=4 * rows * width
        ),
        name="attend_back",
    )(q, k, v, d, o, total, q_blocks.reshape(1, 1, rows), k_blocks.reshape(length, 1))


def pick(table, routes, ids):
    parts = jnp.split(table, len(ids), axis=1)
    return [sum(jnp.where(routes[:, j:j + 1] == e, part, 0.0) for e, part in zip(ids, parts)) for j in range(TOPK)]


def place(pieces, routes, ids):
    return jnp.concatenate(
        [sum(jnp.where(routes[:, j:j + 1] == e, pieces[j], 0.0) for j in range(TOPK)) for e in ids], axis=1
    )


def pair_softmax(logits):
    peak = jnp.maximum(logits[0], logits[1])
    powers = [jnp.exp(v - peak) for v in logits]
    total = powers[0] + powers[1]
    return [v / total for v in powers]


def local(
    inputs, cotangent, blocks, attn_routes, ffn_routes, w_key, w_value, attn_router, ffn_router, attn_gain, ffn_gain,
    attn_bias, ffn_bias, w_query, w_out, w_gate, w_up, w_down,
):
    n_e, n_s = lax.axis_size("expert"), lax.axis_size("shard")
    me = lax.axis_index("expert")
    tokens, width = inputs.shape[1:]
    ids = list(range(n_e))
    capacity = 5 * tokens * TOPK // (4 * n_e)
    group = w_key.shape[1] // n_e
    length = n_e * tokens
    small_rows = w_key.shape[0]

    def swap(value, k):
        return lax.ppermute(value, "expert", [(i, i ^ k) for i in range(n_e)])

    def after(value, *others):
        return lax.optimization_barrier((value,) + others)[0]

    def spread(value):
        return jnp.concatenate([value] + [swap(value, k) for k in range(1, n_e)], axis=0)

    def fetch(block):
        return [block] + [swap(block, k) for k in range(1, 3 if n_e == 4 else n_e)]

    def fetch_rest(blocks, *others):
        if n_e != 4:
            return blocks
        half = blocks[0].shape[0] // 2
        one, two = after(blocks[1], *others), after(blocks[2], *others)
        return blocks + [jnp.concatenate([swap(one[:half], 2), swap(two[half:], 1)], axis=0)]

    def add_low(a, b):
        return (a.astype(F32) + b.astype(F32)).astype(BF)

    def deliver_first(far):
        half = far.shape[0] // 2
        return [swap(far[:half], 1), swap(far[half:], 2)] if n_e == 4 else []

    def deliver_near(parts):
        if n_e != 4:
            return [swap(parts[k], k) for k in range(1, n_e)]
        half = parts[0].shape[0] // 2
        return [swap(parts[1][:half], 1), swap(parts[2][half:], 2)]

    def deliver_last(parts, halves):
        if n_e != 4:
            return []
        half = parts[0].shape[0] // 2
        return [swap(add_low(parts[2][:half], halves[0]), 2), swap(add_low(parts[1][half:], halves[1]), 1)]

    def total(own, near, last):
        own = own.astype(F32)
        if n_e != 4:
            return sum([own] + [v.astype(F32) for v in near])
        half = own.shape[0] // 2
        near, last = [v.astype(F32) for v in near], [v.astype(F32) for v in last]
        return jnp.concatenate([own[:half] + near[0] + last[0], own[half:] + near[1] + last[1]], axis=0)

    def collect(value):
        parts = jnp.split(value, n_e, axis=0)
        return sum([parts[0].astype(F32)] + [swap(parts[k], k).astype(F32) for k in range(1, n_e)])

    def shuffle(value, axis):
        return lax.all_to_all(value, axis, split_axis=0, concat_axis=0, tiled=True)

    def gather_shard(value):
        return lax.all_gather(value, "shard", axis=0, tiled=True)

    def scatter_shard(value):
        return lax.psum_scatter(value, "shard", scatter_dimension=0, tiled=True)

    small = jnp.concatenate(
        [attn_router, ffn_router, attn_gain[:, None], ffn_gain[:, None], attn_bias[:, None], ffn_bias[:, None]], axis=1
    )
    small_width = small.shape[1]
    route_width = tokens * TOPK // (n_e * small_rows)
    small = jnp.pad(small, ((0, 0), (0, 128 - small_width)))
    packed = jnp.concatenate(
        [
            w_key.reshape(small_rows, n_e, group).transpose(1, 0, 2),
            w_value.reshape(small_rows, n_e, group).transpose(1, 0, 2),
            jnp.broadcast_to(small[None], (n_e,) + small.shape),
        ],
        axis=2,
    )
    packed = shuffle(packed, "expert")
    route_at = 2 * group + small_width
    packed = packed.at[:, :, route_at:route_at + route_width].set(
        ffn_routes[0].astype(BF).reshape(n_e, small_rows, route_width)
    )
    packed = gather_shard(packed[None])
    routes_f = packed[:, :, :, route_at:route_at + route_width].reshape(n_s * tokens, TOPK).astype(jnp.int32)
    packed = packed.transpose(1, 0, 2, 3).reshape(width, -1)
    key_value_w = packed[:, :2 * group]
    small = packed[:, 2 * group:2 * group + small_width].astype(F32)
    router_a, router_f = small[:, :n_e], small[:, n_e:2 * n_e]
    gain_a, gain_f, bias_a, bias_f = (small[:, 2 * n_e + i] for i in range(4))

    def to_heads(value):
        rows = value.shape[0]
        value = shuffle(value.reshape(rows, n_e, group).transpose(1, 0, 2), "expert")
        return value.transpose(1, 0, 2).reshape(rows, n_e * group)

    def from_heads(value):
        rows = value.shape[0]
        value = shuffle(value.reshape(rows, n_e, group).transpose(1, 0, 2), "expert")
        return value.transpose(1, 0, 2).reshape(rows, n_e * group)

    notes = jnp.concatenate([blocks[0][:, None], attn_routes[0]], axis=1).astype(BF)
    carried = jnp.concatenate([inputs[0], jnp.pad(notes, ((0, 0), (0, 128 - 1 - TOPK)))], axis=1)
    carried = spread(carried)
    query_w = gather_shard(to_heads(w_query[0]))
    out_rows = w_out.shape[1]
    turned = shuffle(after(w_out[0], carried).T, "shard").reshape(n_s, width // n_s, out_rows).transpose(1, 0, 2)
    out_wt = gather_shard(to_heads(turned.reshape(width // n_s, n_s * out_rows)))

    hidden_units = w_down.shape[1]
    turned = jnp.stack([w_gate[0].T.reshape(n_s, hidden_units, -1), w_up[0].T.reshape(n_s, hidden_units, -1)], axis=1)
    turned = shuffle(after(turned, query_w), "shard").reshape(n_s, 2 * hidden_units, -1)
    gate_up_own = turned.transpose(1, 0, 2).reshape(2 * hidden_units, width)
    down_w = fetch(w_down[0])

    own = inputs[0].astype(F32)
    cot = cotangent[0]
    seq_in = carried[:, :width].astype(F32)
    notes = carried[:, width:width + 1 + TOPK].astype(jnp.int32)
    seq_blocks, routes_a = notes[:, 0], notes[:, 1:]
    position = jnp.concatenate([(me ^ k) * tokens + jnp.arange(tokens, dtype=jnp.int32) for k in range(n_e)]).astype(F32)
    cosine, sine = rope_tables(position)
    h_attn = (seq_in * inverse_rms(seq_in) * gain_a).astype(BF)
    logits_a = dot(h_attn, router_a.astype(BF))
    gates_a = pair_softmax(pick(logits_a, routes_a, ids))
    key_value = dot(h_attn, key_value_w)
    keys = rotate(key_value[:, :group], cosine, sine).astype(BF)
    values = key_value[:, group:].astype(BF)
    queries = pick(dot(h_attn, query_w), routes_a, ids)
    queries = jnp.concatenate([rotate(v, cosine, sine).astype(BF) for v in queries], axis=0)
    row_blocks = jnp.concatenate([seq_blocks, seq_blocks])
    queries, *down_w = lax.optimization_barrier((queries, *down_w))
    down_w = fetch_rest(down_w)
    mixed_rows, log_total = attend(queries, keys, values, row_blocks, seq_blocks)
    mixed = [v.astype(F32) for v in jnp.split(mixed_rows, TOPK, axis=0)]
    mixed_all = place([gates_a[j] * mixed[j] for j in range(TOPK)], routes_a, ids).astype(BF)
    mixed_out, *down_w = lax.optimization_barrier((mixed_all, *down_w))
    middle = own + collect(dot_nt(mixed_out, out_wt).astype(BF)) + bias_a

    inv_f = inverse_rms(middle)
    h_ffn = (middle * inv_f * gain_f).astype(BF)
    h_ffn, gate_up_own = lax.optimization_barrier((h_ffn, gate_up_own))
    gate_up_w = fetch(gate_up_own)
    h_all = gather_shard(h_ffn)
    cot_all = gather_shard(after(cot, h_ffn))
    logits_f = dot(h_all, router_f.astype(BF))
    gates_f = pair_softmax(pick(logits_f, routes_f, ids))
    routes_blocks = routes_f.reshape(n_s, tokens, TOPK)
    h_blocks = h_all.reshape(n_s, tokens, width)
    triangle = (jnp.arange(tokens)[:, None] <= jnp.arange(tokens)[None, :]).astype(BF)

    def rows_of(select, source):
        return lax.dot_general(
            select, source, (((2,), (1,)), ((0,), (0,))), preferred_element_type=F32
        ).astype(BF).reshape(n_s * capacity, width)

    selects, hiddens, back_rows_f = [], [], []
    grad_gate_f = [0.0] * TOPK
    grad_pieces = []
    for k in range(n_e):
        if k == 1:
            gate_up_w = fetch_rest(gate_up_w, hiddens[0])
        expert = me ^ k
        gate_w, up_w = gate_up_w[k][:hidden_units], gate_up_w[k][hidden_units:]
        named = [routes_blocks[:, :, j] == expert for j in range(TOPK)]
        any_named = named[0] | named[1]
        rank = dot(any_named.astype(BF), triangle).astype(jnp.int32) - 1
        hit = (rank[:, None, :] == jnp.arange(capacity, dtype=jnp.int32)[None, :, None]) & any_named[:, None, :]
        select = hit.astype(BF)
        gate_token = sum(jnp.where(named[j], gates_f[j].reshape(n_s, tokens), 0.0) for j in range(TOPK))
        gate_slot = jnp.sum(jnp.where(hit, gate_token[:, None, :], 0.0), axis=2).reshape(-1, 1)
        rows = rows_of(select, h_blocks)
        gate_pre, up_pre = dot_nt(rows, gate_w), dot_nt(rows, up_w)
        if k == 0:
            cot_blocks = after(cot_all, gate_pre, up_pre).reshape(n_s, tokens, width)
        cot_rows = rows_of(select, cot_blocks)
        grad_hidden = dot_nt(cot_rows, down_w[k])
        sigma = 1.0 / (1.0 + jnp.exp(-gate_pre))
        silu = gate_pre * sigma
        hidden = silu * up_pre
        grad_slot = jnp.sum(grad_hidden * hidden, axis=1).reshape(n_s, capacity)
        grad_hidden = grad_hidden * gate_slot
        hidden = (hidden * gate_slot).astype(BF)
        grad_gate = (grad_hidden * up_pre * sigma * (1.0 + gate_pre * (1.0 - sigma))).astype(BF)
        grad_up = (grad_hidden * silu).astype(BF)
        back = (dot(grad_gate, gate_w) + dot(grad_up, up_w)).astype(BF)
        selects.append(select)
        back_rows_f.append(back.reshape(n_s, capacity, width))
        hiddens.append(hidden)
        grad_token = jnp.sum(jnp.where(hit, grad_slot[:, :, None], 0.0), axis=1)
        grad_gate_f = [grad_gate_f[j] + jnp.where(named[j], grad_token, 0.0) for j in range(TOPK)]
        grad_pieces.append((rows, cot_rows, grad_gate, grad_up))
    select = jnp.concatenate(selects, axis=1)

    def tokens_of(row_list):
        return lax.dot_general(
            select, jnp.concatenate(row_list, axis=1), (((1,), (1,)), ((0,), (0,))), preferred_element_type=F32
        ).astype(BF).reshape(n_s * tokens, width)

    back_sum = tokens_of(back_rows_f)
    back_f = scatter_shard(back_sum)

    def gate_up_grads(k, *others):
        rows, _, grad_gate, grad_up = grad_pieces[k]
        rows = after(rows, *others)
        return jnp.concatenate([dot_tn(grad_gate, rows).astype(BF), dot_tn(grad_up, rows).astype(BF)], axis=0)

    grad_gate_up = [None] * n_e
    grad_gate_up[n_e - 1] = gate_up_grads(n_e - 1, back_sum)
    halves = deliver_first(grad_gate_up[n_e - 1])
    out_rows_f = []
    for k in range(n_e):
        hidden = after(hiddens[k], grad_gate_up[n_e - 1])
        out_rows_f.append(dot(hidden, down_w[k]).astype(BF).reshape(n_s, capacity, width))
    out_sum = tokens_of(out_rows_f)
    ffn_out = scatter_shard(out_sum)
    back_f, out_sum, *halves = lax.optimization_barrier((back_f, out_sum, *halves))
    back_f = back_f.astype(F32)
    grad_gates_f = jnp.sum(
        shuffle(jnp.stack(grad_gate_f, axis=1).reshape(n_s, TOPK * tokens), "shard"), axis=0
    ).reshape(TOPK, tokens, 1)


    grad_out = cot.astype(F32)
    own_routes_f = ffn_routes[0]
    own_gates_f = pair_softmax(pick(dot(h_ffn, router_f.astype(BF)), own_routes_f, ids))

    def logit_grads(gates, grads, routes):
        centre = sum(gates[j] * grads[j] for j in range(TOPK))
        return place([gates[j] * (grads[j] - centre) for j in range(TOPK)], routes, ids)

    grad_logits_f = logit_grads(own_gates_f, grad_gates_f, own_routes_f)
    grad_router_f = dot_tn(h_ffn.astype(F32), grad_logits_f, PRECISE)
    grad_h_ffn = back_f + jnp.dot(grad_logits_f, router_f.T, precision=PRECISE)
    grad_norm, grad_gain_f = norm_back(grad_h_ffn, middle, inv_f, gain_f)
    grad_middle = grad_out + grad_norm
    grad_bias_f = jnp.sum(grad_out, axis=0)
    grad_bias_a = jnp.sum(grad_middle, axis=0)

    grad_middle_low = grad_middle.astype(BF)
    for k in range(n_e - 1):
        grad_gate_up[k] = gate_up_grads(k, back_f)
    seq_grad = spread(grad_middle_low)
    seq_grad, *grad_gate_up = lax.optimization_barrier((seq_grad, *grad_gate_up))
    near = deliver_near(grad_gate_up)
    last = deliver_last(grad_gate_up, halves)
    grad_mixed = pick(dot(seq_grad, out_wt), routes_a, ids)
    gate_grads = jnp.concatenate([jnp.sum(grad_mixed[j] * mixed[j], axis=1, keepdims=True) for j in range(TOPK)], axis=1)
    gate_grads_high = gate_grads.astype(BF)
    gate_grads_low = (gate_grads - gate_grads_high.astype(F32)).astype(BF)
    grad_mixed = jnp.concatenate([(gates_a[j] * grad_mixed[j]).astype(BF) for j in range(TOPK)], axis=0)
    grad_out_wt = dot_tn(seq_grad, mixed_all).astype(BF)
    grad_mixed, grad_out_wt = lax.optimization_barrier((grad_mixed, grad_out_wt))
    grad_q, grad_k, grad_v = attend_back(queries, keys, values, grad_mixed, mixed_rows, log_total, row_blocks, seq_blocks)
    grad_q, *near = lax.optimization_barrier((grad_q, *near))
    grad_q = [rotate(v, cosine, -sine) for v in jnp.split(grad_q, TOPK, axis=0)]
    grad_query_all = place(grad_q, routes_a, ids).astype(BF)
    grad_key_value = jnp.concatenate([rotate(grad_k, cosine, -sine), grad_v], axis=1).astype(BF)
    back_a = (dot_nt(grad_query_all, query_w) + dot_nt(grad_key_value, key_value_w)).astype(BF)
    back_a = jnp.concatenate(
        [back_a, jnp.pad(jnp.concatenate([gate_grads_high, gate_grads_low], axis=1), ((0, 0), (0, 128 - 2 * TOPK)))], axis=1
    )
    back_a, ffn_out, *last = lax.optimization_barrier((back_a, ffn_out, *last))
    value = total(grad_gate_up[0], near, last).astype(BF).reshape(2 * hidden_units, n_s, width // n_s).transpose(1, 0, 2)
    gate_up_turned = shuffle(value, "shard").reshape(n_s, 2, hidden_units, width // n_s)
    outputs = (middle + ffn_out.astype(F32) + bias_f).astype(BF)[None]
    grad_down = [dot_tn(after(hiddens[k], back_a), grad_pieces[k][1]).astype(BF) for k in range(n_e)]
    halves = deliver_first(grad_down[n_e - 1])
    value = scatter_shard(grad_out_wt)
    value, key_value_grad = lax.optimization_barrier((value, dot_tn(h_attn, grad_key_value).astype(BF)))
    value = from_heads(value).reshape(width // n_s, n_s, out_rows).transpose(1, 0, 2)
    grad_out_w = shuffle(value, "shard").reshape(width, out_rows)
    key_value_grad = key_value_grad.reshape(n_e, n_s, small_rows, 2 * group).transpose(1, 0, 2, 3)
    key_value_grad = scatter_shard(key_value_grad.reshape(n_s * n_e * small_rows, 2 * group))
    key_value_grad = shuffle(key_value_grad.reshape(n_e, small_rows, -1), "expert")
    back_a = collect(back_a)
    near, last = deliver_near(grad_down), deliver_last(grad_down, halves)
    back_a, grad_out_w, key_value_grad, *near = lax.optimization_barrier((back_a, grad_out_w, key_value_grad, *near))
    grad_down_w = total(grad_down[0], near, last)[None]
    grad_out_w = grad_out_w.T.astype(F32)[None]
    grad_key_w = key_value_grad[:, :, :group].transpose(1, 0, 2).reshape(small_rows, -1).astype(F32)
    grad_value_w = key_value_grad[:, :, group:].transpose(1, 0, 2).reshape(small_rows, -1).astype(F32)
    gate_grads = back_a[:, width:width + TOPK] + back_a[:, width + TOPK:width + 2 * TOPK]
    grad_gates_a = [gate_grads[:, j:j + 1] for j in range(TOPK)]
    back_a = back_a[:, :width]
    value = after(scatter_shard(dot_tn(h_attn, grad_query_all).astype(BF)), gate_up_turned)
    grad_query_w = from_heads(value).astype(F32)[None]
    grad_gate_w = gate_up_turned[:, 0].reshape(n_s * hidden_units, -1).T.astype(F32)[None]
    grad_up_w = gate_up_turned[:, 1].reshape(n_s * hidden_units, -1).T.astype(F32)[None]

    h_own = h_attn[:tokens]
    own_routes_a = attn_routes[0]
    own_gates_a = [v[:tokens] for v in gates_a]
    grad_logits_a = logit_grads(own_gates_a, grad_gates_a, own_routes_a)
    grad_router_a = dot_tn(h_own.astype(F32), grad_logits_a, PRECISE)
    grad_h_attn = back_a + jnp.dot(grad_logits_a, router_a.T, precision=PRECISE)
    grad_norm, grad_gain_a = norm_back(grad_h_attn, own, inverse_rms(own), gain_a)
    input_grad = (grad_middle + grad_norm).astype(BF)[None]

    shared = jnp.concatenate(
        [grad_router_a, grad_router_f]
        + [v[:, None] for v in (grad_gain_a, grad_gain_f, grad_bias_a, grad_bias_f)],
        axis=1,
    )
    shared = shuffle(shared.reshape(n_e * n_s, -1), ("expert", "shard"))
    shared = jnp.sum(shared, axis=0).reshape(small_rows, small_width)
    return (
        outputs,
        input_grad,
        grad_key_w,
        grad_value_w,
        shared[:, :n_e],
        shared[:, n_e:2 * n_e],
        shared[:, 2 * n_e],
        shared[:, 2 * n_e + 1],
        shared[:, 2 * n_e + 2],
        shared[:, 2 * n_e + 3],
        grad_query_w,
        grad_out_w,
        grad_gate_w,
        grad_up_w,
        grad_down_w,
    )


def solution(mesh):
    rows = P("shard", "expert", None)
    shared, vector = P(("expert", "shard"), None), P(("expert", "shard"))
    weight = P("expert", "shard", None)
    in_specs = (rows, rows, P("shard", "expert"), rows, rows) + (shared,) * 4 + (vector,) * 4 + (weight,) * 5
    out_specs = (rows, rows) + (shared,) * 4 + (vector,) * 4 + (weight,) * 5
    return jax.shard_map(local, mesh=mesh, in_specs=in_specs, out_specs=out_specs, check_vma=False)
```

```python
import functools
import math

import jax
import jax.numpy as jnp
from jax import lax
from jax.experimental import pallas as pl
from jax.experimental.pallas import tpu as pltpu
from jax.sharding import PartitionSpec as P

HD = 128
TOPK = 2
EPSILON = 1e-06
NEGATIVE = -1e30
ROPE_BASE = 10000.0
PRECISE = lax.Precision.HIGHEST
BF = jnp.bfloat16
F32 = jnp.float32
LOG2E = 1.4426950408889634


def dot(a, b):
    return jnp.dot(a, b, preferred_element_type=F32)


def dot_tn(a, b, precision=None):
    return lax.dot_general(a, b, (((0,), (0,)), ((), ())), precision=precision, preferred_element_type=F32)


def dot_nt(a, b):
    return lax.dot_general(a, b, (((1,), (1,)), ((), ())), preferred_element_type=F32)


def inverse_rms(values):
    return lax.rsqrt(jnp.mean(values * values, axis=-1, keepdims=True) + EPSILON)


def norm_back(grad, values, inv, gain):
    u = grad * gain
    centre = jnp.mean(u * values, axis=-1, keepdims=True)
    return inv * (u - values * (inv * inv) * centre), jnp.sum(grad * values * inv, axis=0)


def rope_tables(position):
    half = HD // 2
    frequency = jnp.exp(-math.log(ROPE_BASE) * jnp.arange(half, dtype=F32) / half)
    angles = position[:, None] * frequency
    cosine, sine = jnp.cos(angles), jnp.sin(angles)
    return jnp.concatenate([cosine, cosine], -1), jnp.concatenate([-sine, sine], -1)


def rotate(tensor, cosine, sine):
    heads = tensor.reshape(tensor.shape[:-1] + (-1, HD))
    swapped = jnp.concatenate([heads[..., HD // 2:], heads[..., :HD // 2]], -1)
    return (heads * cosine[:, None, :] + swapped * sine[:, None, :]).reshape(tensor.shape)


def attend_kernel(scale, q_ref, k_ref, v_ref, qb_ref, kb_ref, o_ref, l_ref):
    s = dot_nt(k_ref[...], q_ref[...])
    s = jnp.where(kb_ref[...] <= qb_ref[0], s * (scale * LOG2E), NEGATIVE)
    peak = jnp.max(s, axis=0, keepdims=True)
    p = jnp.exp2(s - peak)
    total = jnp.sum(p, axis=0, keepdims=True)
    o = dot_tn(v_ref[...], p.astype(BF))
    o_ref[...] = (o / total).T.astype(BF)
    l_ref[0] = peak + jnp.log2(total)


def attend(q, k, v, q_blocks, k_blocks):
    rows, width = q.shape
    length = k.shape[0]
    heads = width // HD
    tile = 256
    return pl.pallas_call(
        functools.partial(attend_kernel, HD ** -0.5),
        grid=(heads, rows // tile),
        in_specs=[
            pl.BlockSpec((tile, HD), lambda h, i: (i, h)),
            pl.BlockSpec((length, HD), lambda h, i: (0, h)),
            pl.BlockSpec((length, HD), lambda h, i: (0, h)),
            pl.BlockSpec((1, 1, tile), lambda h, i: (0, 0, i)),
            pl.BlockSpec((length, 1), lambda h, i: (0, 0)),
        ],
        out_specs=[
            pl.BlockSpec((tile, HD), lambda h, i: (i, h)),
            pl.BlockSpec((1, 1, tile), lambda h, i: (h, 0, i)),
        ],
        out_shape=[
            jax.ShapeDtypeStruct((rows, width), BF),
            jax.ShapeDtypeStruct((heads, 1, rows), F32),
        ],
        cost_estimate=pl.CostEstimate(
            flops=rows * length, transcendentals=0, bytes_accessed=4 * rows * width
        ),
        name="attend",
    )(q, k, v, q_blocks.reshape(1, 1, rows), k_blocks.reshape(length, 1))


def attend_back_kernel(scale, q_ref, k_ref, v_ref, d_ref, o_ref, l_ref, qb_ref, kb_ref, dq_ref, dk_ref, dv_ref):
    q, k, d = q_ref[...], k_ref[...], d_ref[...]
    s = dot_nt(k, q)
    p = jnp.exp2(s * (scale * LOG2E) - l_ref[0])
    p = jnp.where(kb_ref[...] <= qb_ref[0], p, 0.0)
    centre = jnp.sum((d.astype(F32) * o_ref[...].astype(F32)).T, axis=0, keepdims=True)
    grad_p = dot_nt(v_ref[...], d)
    grad_s = (p * (grad_p - centre)).astype(BF)
    dq_ref[...] = (dot_tn(k, grad_s) * scale).T
    new_k = dot(grad_s, q) * scale
    new_v = dot(p.astype(BF), d)

    @pl.when(pl.program_id(1) == 0)
    def _():
        dk_ref[...] = new_k
        dv_ref[...] = new_v

    @pl.when(pl.program_id(1) > 0)
    def _():
        dk_ref[...] += new_k
        dv_ref[...] += new_v


def attend_back(q, k, v, d, o, total, q_blocks, k_blocks):
    rows, width = q.shape
    length = k.shape[0]
    heads = width // HD
    tile = 256
    row_spec = pl.BlockSpec((tile, HD), lambda h, i: (i, h))
    key_spec = pl.BlockSpec((length, HD), lambda h, i: (0, h))
    return pl.pallas_call(
        functools.partial(attend_back_kernel, HD ** -0.5),
        grid=(heads, rows // tile),
        in_specs=[
            row_spec, key_spec, key_spec, row_spec, row_spec,
            pl.BlockSpec((1, 1, tile), lambda h, i: (h, 0, i)),
            pl.BlockSpec((1, 1, tile), lambda h, i: (0, 0, i)),
            pl.BlockSpec((length, 1), lambda h, i: (0, 0)),
        ],
        out_specs=[row_spec, key_spec, key_spec],
        out_shape=[
            jax.ShapeDtypeStruct((rows, width), F32),
            jax.ShapeDtypeStruct((length, width), F32),
            jax.ShapeDtypeStruct((length, width), F32),
        ],
        cost_estimate=pl.CostEstimate(
            flops=rows * length, transcendentals=0, bytes_accessed=4 * rows * width
        ),
        name="attend_back",
    )(q, k, v, d, o, total, q_blocks.reshape(1, 1, rows), k_blocks.reshape(length, 1))


def pick(table, routes, ids):
    parts = jnp.split(table, len(ids), axis=1)
    return [sum(jnp.where(routes[:, j:j + 1] == e, part, 0.0) for e, part in zip(ids, parts)) for j in range(TOPK)]


def place(pieces, routes, ids):
    return jnp.concatenate(
        [sum(jnp.where(routes[:, j:j + 1] == e, pieces[j], 0.0) for j in range(TOPK)) for e in ids], axis=1
    )


def pair_softmax(logits):
    peak = jnp.maximum(logits[0], logits[1])
    powers = [jnp.exp(v - peak) for v in logits]
    total = powers[0] + powers[1]
    return [v / total for v in powers]


def local(
    inputs, cotangent, blocks, attn_routes, ffn_routes, w_key, w_value, attn_router, ffn_router, attn_gain, ffn_gain,
    attn_bias, ffn_bias, w_query, w_out, w_gate, w_up, w_down,
):
    n_e, n_s = lax.axis_size("expert"), lax.axis_size("shard")
    me = lax.axis_index("expert")
    tokens, width = inputs.shape[1:]
    ids = list(range(n_e))
    capacity = 5 * tokens * TOPK // (4 * n_e)
    group = w_key.shape[1] // n_e
    length = n_e * tokens
    small_rows = w_key.shape[0]

    def swap(value, k):
        return lax.ppermute(value, "expert", [(i, i ^ k) for i in range(n_e)])

    def after(value, *others):
        return lax.optimization_barrier((value,) + others)[0]

    def spread(value):
        return jnp.concatenate([value] + [swap(value, k) for k in range(1, n_e)], axis=0)

    def fetch(block):
        return [block] + [swap(block, k) for k in range(1, 3 if n_e == 4 else n_e)]

    def fetch_rest(blocks, *others):
        if n_e != 4:
            return blocks
        half = blocks[0].shape[0] // 2
        one, two = after(blocks[1], *others), after(blocks[2], *others)
        return blocks + [jnp.concatenate([swap(one[:half], 2), swap(two[half:], 1)], axis=0)]

    def add_low(a, b):
        return (a.astype(F32) + b.astype(F32)).astype(BF)

    def deliver_first(far):
        return [swap(far[0], 1), swap(far[1], 2)] if n_e == 4 else []

    def deliver_near(parts):
        if n_e != 4:
            return [swap(parts[k][i], k) for i in range(2) for k in range(1, n_e)]
        return [swap(parts[1][0], 1), swap(parts[2][1], 2)]

    def deliver_last(parts, halves):
        if n_e != 4:
            return []
        return [swap(add_low(parts[2][0], halves[0]), 2), swap(add_low(parts[1][1], halves[1]), 1)]

    def total(own, near, last):
        count = len(near) // 2
        return [
            sum(v.astype(F32) for v in [own[i]] + near[i * count:(i + 1) * count] + last[i:i + 1]) for i in range(2)
        ]

    def collect(value):
        parts = jnp.split(value, n_e, axis=0)
        return sum([parts[0].astype(F32)] + [swap(parts[k], k).astype(F32) for k in range(1, n_e)])

    def shuffle(value, axis):
        return lax.all_to_all(value, axis, split_axis=0, concat_axis=0, tiled=True)

    def trade(value):
        out = jnp.zeros_like(value)
        for k in range(n_e):
            piece = lax.dynamic_index_in_dim(value, me ^ k, 0, False)
            out = lax.dynamic_update_index_in_dim(out, swap(piece, k) if k else piece, me ^ k, 0)
        return out

    def gather_shard(value):
        return lax.all_gather(value, "shard", axis=0, tiled=True)

    def scatter_shard(value):
        return lax.psum_scatter(value, "shard", scatter_dimension=0, tiled=True)

    small = jnp.concatenate(
        [attn_router, ffn_router, attn_gain[:, None], ffn_gain[:, None], attn_bias[:, None], ffn_bias[:, None]], axis=1
    )
    small_width = small.shape[1]
    route_width = tokens * TOPK // (n_e * small_rows)
    small = jnp.pad(small, ((0, 0), (0, 128 - small_width)))
    packed = jnp.concatenate(
        [
            w_key.reshape(small_rows, n_e, group).transpose(1, 0, 2),
            w_value.reshape(small_rows, n_e, group).transpose(1, 0, 2),
            jnp.broadcast_to(small[None], (n_e,) + small.shape),
        ],
        axis=2,
    )
    packed = shuffle(packed, "expert")
    route_at = 2 * group + small_width
    packed = packed.at[:, :, route_at:route_at + route_width].set(
        ffn_routes[0].astype(BF).reshape(n_e, small_rows, route_width)
    )
    packed = gather_shard(packed[None])
    routes_f = packed[:, :, :, route_at:route_at + route_width].reshape(n_s * tokens, TOPK).astype(jnp.int32)
    packed = packed.transpose(1, 0, 2, 3).reshape(width, -1)
    key_value_w = packed[:, :2 * group]
    small = packed[:, 2 * group:2 * group + small_width].astype(F32)
    router_a, router_f = small[:, :n_e], small[:, n_e:2 * n_e]
    gain_a, gain_f, bias_a, bias_f = (small[:, 2 * n_e + i] for i in range(4))

    def to_heads(value):
        rows = value.shape[0]
        value = shuffle(value.reshape(rows, n_e, group).transpose(1, 0, 2), "expert")
        return value.transpose(1, 0, 2).reshape(rows, n_e * group)

    def from_heads(value):
        rows = value.shape[0]
        value = trade(value.reshape(rows, n_e, group).transpose(1, 0, 2))
        return value.transpose(1, 0, 2).reshape(rows, n_e * group)

    notes = jnp.concatenate([blocks[0][:, None], attn_routes[0]], axis=1).astype(BF)
    carried = jnp.concatenate([inputs[0], jnp.pad(notes, ((0, 0), (0, 128 - 1 - TOPK)))], axis=1)
    carried = [carried] + [swap(carried, k) for k in range(1, n_e)]
    query_w = to_heads(w_query[0])
    out_w, query_w, carried[1] = lax.optimization_barrier((w_out[0], query_w, carried[1]))
    carried = jnp.concatenate(carried, axis=0)
    query_w = gather_shard(query_w)
    out_rows = out_w.shape[0]
    turned = shuffle(out_w.T, "shard").reshape(n_s, width // n_s, out_rows).transpose(1, 0, 2)
    out_wt = gather_shard(to_heads(turned.reshape(width // n_s, n_s * out_rows)))

    hidden_units = w_down.shape[1]
    turned = jnp.stack([w_gate[0].T.reshape(n_s, hidden_units, -1), w_up[0].T.reshape(n_s, hidden_units, -1)], axis=1)
    turned = shuffle(after(turned, query_w), "shard").reshape(n_s, 2 * hidden_units, -1)
    gate_up_own = turned.transpose(1, 0, 2).reshape(2 * hidden_units, width)
    down_w = fetch(w_down[0])

    own = inputs[0].astype(F32)
    cot = cotangent[0]
    seq_in = carried[:, :width].astype(F32)
    notes = carried[:, width:width + 1 + TOPK].astype(jnp.int32)
    seq_blocks, routes_a = notes[:, 0], notes[:, 1:]
    position = jnp.concatenate([(me ^ k) * tokens + jnp.arange(tokens, dtype=jnp.int32) for k in range(n_e)]).astype(F32)
    cosine, sine = rope_tables(position)
    h_attn = (seq_in * inverse_rms(seq_in) * gain_a).astype(BF)
    logits_a = dot(h_attn, router_a.astype(BF))
    gates_a = pair_softmax(pick(logits_a, routes_a, ids))
    key_value = dot(h_attn, key_value_w)
    keys = rotate(key_value[:, :group], cosine, sine).astype(BF)
    values = key_value[:, group:].astype(BF)
    queries = pick(dot(h_attn, query_w), routes_a, ids)
    queries = jnp.concatenate([rotate(v, cosine, sine).astype(BF) for v in queries], axis=0)
    row_blocks = jnp.concatenate([seq_blocks, seq_blocks])
    queries, *down_w = lax.optimization_barrier((queries, *down_w))
    down_w = fetch_rest(down_w)
    mixed_rows, log_total = attend(queries, keys, values, row_blocks, seq_blocks)
    mixed = [v.astype(F32) for v in jnp.split(mixed_rows, TOPK, axis=0)]
    mixed_all = place([gates_a[j] * mixed[j] for j in range(TOPK)], routes_a, ids).astype(BF)
    mixed_out, *down_w = lax.optimization_barrier((mixed_all, *down_w))
    middle = own + collect(dot_nt(mixed_out, out_wt).astype(BF)) + bias_a

    inv_f = inverse_rms(middle)
    h_ffn = (middle * inv_f * gain_f).astype(BF)
    h_ffn, gate_up_own = lax.optimization_barrier((h_ffn, gate_up_own))
    gate_up_w = fetch(gate_up_own)
    h_all = gather_shard(h_ffn)
    cot_all = gather_shard(after(cot, h_ffn))
    logits_f = dot(h_all, router_f.astype(BF))
    gates_f = pair_softmax(pick(logits_f, routes_f, ids))
    routes_blocks = routes_f.reshape(n_s, tokens, TOPK)
    h_blocks = h_all.reshape(n_s, tokens, width)
    triangle = (jnp.arange(tokens)[:, None] <= jnp.arange(tokens)[None, :]).astype(BF)

    def rows_of(select, source):
        return lax.dot_general(
            select, source, (((2,), (1,)), ((0,), (0,))), preferred_element_type=F32
        ).astype(BF).reshape(n_s * capacity, width)

    selects, hiddens, back_rows_f = [], [], []
    grad_gate_f = [0.0] * TOPK
    grad_pieces = []
    for k in range(n_e):
        if k == 1:
            gate_up_w = fetch_rest(gate_up_w, hiddens[0])
        expert = me ^ k
        named = [routes_blocks[:, :, j] == expert for j in range(TOPK)]
        any_named = named[0] | named[1]
        rank = dot(any_named.astype(BF), triangle).astype(jnp.int32) - 1
        hit = (rank[:, None, :] == jnp.arange(capacity, dtype=jnp.int32)[None, :, None]) & any_named[:, None, :]
        select = hit.astype(BF)
        gate_token = sum(jnp.where(named[j], gates_f[j].reshape(n_s, tokens), 0.0) for j in range(TOPK))
        gate_slot = jnp.sum(jnp.where(hit, gate_token[:, None, :], 0.0), axis=2).reshape(1, -1)
        rows = rows_of(select, h_blocks)
        pre = dot_nt(gate_up_w[k], rows)
        if k == 0:
            cot_blocks = after(cot_all, pre).reshape(n_s, tokens, width)
        gate_pre, up_pre = pre[:hidden_units], pre[hidden_units:]
        cot_rows = rows_of(select, cot_blocks)
        grad_hidden = dot_nt(down_w[k], cot_rows)
        sigma = 1.0 / (1.0 + jnp.exp(-gate_pre))
        silu = gate_pre * sigma
        hidden = silu * up_pre
        grad_slot = jnp.sum(grad_hidden * hidden, axis=0).reshape(n_s, capacity)
        grad_hidden = grad_hidden * gate_slot
        hidden = (hidden * gate_slot).astype(BF)
        grad_gate = (grad_hidden * up_pre * sigma * (1.0 + gate_pre * (1.0 - sigma))).astype(BF)
        grad_pre = jnp.concatenate([grad_gate, (grad_hidden * silu).astype(BF)], axis=0)
        back = dot_tn(grad_pre, gate_up_w[k]).astype(BF)
        selects.append(select)
        back_rows_f.append(back.reshape(n_s, capacity, width))
        hiddens.append(hidden)
        grad_token = jnp.sum(jnp.where(hit, grad_slot[:, :, None], 0.0), axis=1)
        grad_gate_f = [grad_gate_f[j] + jnp.where(named[j], grad_token, 0.0) for j in range(TOPK)]
        grad_pieces.append((rows, cot_rows, grad_pre))
    select = jnp.concatenate(selects, axis=1)

    def tokens_of(row_list):
        return lax.dot_general(
            select, jnp.concatenate(row_list, axis=1), (((1,), (1,)), ((0,), (0,))), preferred_element_type=F32
        ).astype(BF).reshape(n_s * tokens, width)

    back_sum = tokens_of(back_rows_f)
    back_f = scatter_shard(back_sum)

    def gate_up_grads(k, *others):
        rows, _, grad_pre = grad_pieces[k]
        rows = after(rows, *others)
        return [dot(v, rows).astype(BF) for v in jnp.split(grad_pre, 2, axis=0)]

    grad_gate_up = [None] * n_e
    grad_gate_up[n_e - 1] = gate_up_grads(n_e - 1, back_sum)
    halves = deliver_first(grad_gate_up[n_e - 1])
    out_rows_f = []
    for k in range(n_e):
        hidden = after(hiddens[k], *grad_gate_up[n_e - 1])
        out_rows_f.append(dot_tn(hidden, down_w[k]).astype(BF).reshape(n_s, capacity, width))
    out_sum = tokens_of(out_rows_f)
    ffn_out = scatter_shard(out_sum)
    back_f, out_sum, *halves = lax.optimization_barrier((back_f, out_sum, *halves))
    back_f = back_f.astype(F32)
    grad_gates_f = jnp.sum(
        shuffle(jnp.stack(grad_gate_f, axis=1).reshape(n_s, TOPK * tokens), "shard"), axis=0
    ).reshape(TOPK, tokens, 1)


    grad_out = cot.astype(F32)
    own_routes_f = ffn_routes[0]
    own_gates_f = pair_softmax(pick(dot(h_ffn, router_f.astype(BF)), own_routes_f, ids))

    def logit_grads(gates, grads, routes):
        centre = sum(gates[j] * grads[j] for j in range(TOPK))
        return place([gates[j] * (grads[j] - centre) for j in range(TOPK)], routes, ids)

    grad_logits_f = logit_grads(own_gates_f, grad_gates_f, own_routes_f)
    grad_router_f = dot_tn(h_ffn.astype(F32), grad_logits_f, PRECISE)
    grad_h_ffn = back_f + jnp.dot(grad_logits_f, router_f.T, precision=PRECISE)
    grad_norm, grad_gain_f = norm_back(grad_h_ffn, middle, inv_f, gain_f)
    grad_middle = grad_out + grad_norm
    grad_bias_f = jnp.sum(grad_out, axis=0)
    grad_bias_a = jnp.sum(grad_middle, axis=0)

    grad_middle_low = grad_middle.astype(BF)
    for k in range(n_e - 1):
        grad_gate_up[k] = gate_up_grads(k, back_f)
    seq_grad = spread(grad_middle_low)
    seq_grad, grad_gate_up = lax.optimization_barrier((seq_grad, grad_gate_up))
    near = deliver_near(grad_gate_up)
    last = deliver_last(grad_gate_up, halves)
    grad_mixed = pick(dot(seq_grad, out_wt), routes_a, ids)
    gate_grads = jnp.concatenate([jnp.sum(grad_mixed[j] * mixed[j], axis=1, keepdims=True) for j in range(TOPK)], axis=1)
    gate_grads_high = gate_grads.astype(BF)
    gate_grads_low = (gate_grads - gate_grads_high.astype(F32)).astype(BF)
    grad_mixed = jnp.concatenate([(gates_a[j] * grad_mixed[j]).astype(BF) for j in range(TOPK)], axis=0)
    grad_out_wt = dot_tn(seq_grad, mixed_all).astype(BF)
    grad_mixed, grad_out_wt = lax.optimization_barrier((grad_mixed, grad_out_wt))
    grad_q, grad_k, grad_v = attend_back(queries, keys, values, grad_mixed, mixed_rows, log_total, row_blocks, seq_blocks)
    grad_q, *near = lax.optimization_barrier((grad_q, *near))
    grad_q = [rotate(v, cosine, -sine) for v in jnp.split(grad_q, TOPK, axis=0)]
    grad_query_all = place(grad_q, routes_a, ids).astype(BF)
    grad_key_value = jnp.concatenate([rotate(grad_k, cosine, -sine), grad_v], axis=1).astype(BF)
    back_a = (dot_nt(grad_query_all, query_w) + dot_nt(grad_key_value, key_value_w)).astype(BF)
    back_a = jnp.concatenate(
        [back_a, jnp.pad(jnp.concatenate([gate_grads_high, gate_grads_low], axis=1), ((0, 0), (0, 128 - 2 * TOPK)))], axis=1
    )
    value = scatter_shard(grad_out_wt)
    back_a, ffn_out, *last = lax.optimization_barrier((back_a, ffn_out, *last))
    gate_up_total = [v.astype(BF) for v in total(grad_gate_up[0], near, last)]
    outputs = (middle + ffn_out.astype(F32) + bias_f).astype(BF)[None]
    key_value_grad = after(dot_tn(h_attn, grad_key_value).astype(BF), back_a)
    key_value_grad = key_value_grad.reshape(n_e, n_s, small_rows, 2 * group).transpose(1, 0, 2, 3)
    key_value_grad = scatter_shard(key_value_grad.reshape(n_s * n_e * small_rows, 2 * group))
    query_grad = dot_tn(h_attn, grad_query_all).astype(BF)
    query_grad, value = lax.optimization_barrier((query_grad, value))
    query_grad = scatter_shard(query_grad)
    value = from_heads(value).reshape(width // n_s, n_s, out_rows).transpose(1, 0, 2)

    def to_rows(value):
        value = shuffle(value.reshape(hidden_units, n_s, width // n_s).transpose(1, 0, 2), "shard")
        return value.reshape(n_s * hidden_units, width // n_s)

    gate_turned = to_rows(gate_up_total[0])
    grad_down = []
    for k in range(n_e):
        hidden = after(hiddens[k], back_a)
        grad_down.append([dot(v, grad_pieces[k][1]).astype(BF) for v in jnp.split(hidden, 2, axis=0)])
    halves = deliver_first(grad_down[n_e - 1])
    back_a = collect(back_a)
    near, last = deliver_near(grad_down), deliver_last(grad_down, halves)
    back_a, gate_turned, *near = lax.optimization_barrier((back_a, gate_turned, *near))
    up_total, key_value_grad = lax.optimization_barrier((after(gate_up_total[1], gate_turned), key_value_grad))
    up_turned = to_rows(up_total)
    grad_out_w = shuffle(after(value, gate_turned), "shard").reshape(width, out_rows).T.astype(F32)[None]
    grad_down_w = jnp.concatenate(total(grad_down[0], near, last), axis=0)[None]
    key_value_grad = trade(key_value_grad.reshape(n_e, small_rows, -1))
    grad_key_w = key_value_grad[:, :, :group].transpose(1, 0, 2).reshape(small_rows, -1).astype(F32)
    grad_value_w = key_value_grad[:, :, group:].transpose(1, 0, 2).reshape(small_rows, -1).astype(F32)
    gate_grads = back_a[:, width:width + TOPK] + back_a[:, width + TOPK:width + 2 * TOPK]
    grad_gates_a = [gate_grads[:, j:j + 1] for j in range(TOPK)]
    back_a = back_a[:, :width]
    grad_query_w = from_heads(query_grad).astype(F32)[None]
    grad_gate_w = gate_turned.T.astype(F32)[None]
    grad_up_w = up_turned.T.astype(F32)[None]

    h_own = h_attn[:tokens]
    own_routes_a = attn_routes[0]
    own_gates_a = [v[:tokens] for v in gates_a]
    grad_logits_a = logit_grads(own_gates_a, grad_gates_a, own_routes_a)
    grad_router_a = dot_tn(h_own.astype(F32), grad_logits_a, PRECISE)
    grad_h_attn = back_a + jnp.dot(grad_logits_a, router_a.T, precision=PRECISE)
    grad_norm, grad_gain_a = norm_back(grad_h_attn, own, inverse_rms(own), gain_a)
    input_grad = (grad_middle + grad_norm).astype(BF)[None]

    shared = jnp.concatenate(
        [grad_router_a, grad_router_f]
        + [v[:, None] for v in (grad_gain_a, grad_gain_f, grad_bias_a, grad_bias_f)],
        axis=1,
    )
    shared = shuffle(shared.reshape(n_e * n_s, -1), ("expert", "shard"))
    shared = jnp.sum(shared, axis=0).reshape(small_rows, small_width)
    return (
        outputs,
        input_grad,
        grad_key_w,
        grad_value_w,
        shared[:, :n_e],
        shared[:, n_e:2 * n_e],
        shared[:, 2 * n_e],
        shared[:, 2 * n_e + 1],
        shared[:, 2 * n_e + 2],
        shared[:, 2 * n_e + 3],
        grad_query_w,
        grad_out_w,
        grad_gate_w,
        grad_up_w,
        grad_down_w,
    )


def solution(mesh):
    rows = P("shard", "expert", None)
    shared, vector = P(("expert", "shard"), None), P(("expert", "shard"))
    weight = P("expert", "shard", None)
    in_specs = (rows, rows, P("shard", "expert"), rows, rows) + (shared,) * 4 + (vector,) * 4 + (weight,) * 5
    out_specs = (rows, rows) + (shared,) * 4 + (vector,) * 4 + (weight,) * 5
    return jax.shard_map(local, mesh=mesh, in_specs=in_specs, out_specs=out_specs, check_vma=False)
```

```python
import functools
import math

import jax
import jax.numpy as jnp
from jax import lax
from jax.experimental import pallas as pl
from jax.experimental.pallas import tpu as pltpu
from jax.sharding import PartitionSpec as P

HD = 128
TOPK = 2
EPSILON = 1e-06
NEGATIVE = -1e30
ROPE_BASE = 10000.0
PRECISE = lax.Precision.HIGHEST
BF = jnp.bfloat16
F32 = jnp.float32
LOG2E = 1.4426950408889634


def dot(a, b):
    return jnp.dot(a, b, preferred_element_type=F32)


def dot_tn(a, b, precision=None):
    return lax.dot_general(a, b, (((0,), (0,)), ((), ())), precision=precision, preferred_element_type=F32)


def dot_nt(a, b):
    return lax.dot_general(a, b, (((1,), (1,)), ((), ())), preferred_element_type=F32)


def inverse_rms(values):
    return lax.rsqrt(jnp.mean(values * values, axis=-1, keepdims=True) + EPSILON)


def norm_back(grad, values, inv, gain):
    u = grad * gain
    centre = jnp.mean(u * values, axis=-1, keepdims=True)
    return inv * (u - values * (inv * inv) * centre), jnp.sum(grad * values * inv, axis=0)


def rope_tables(position):
    half = HD // 2
    frequency = jnp.exp(-math.log(ROPE_BASE) * jnp.arange(half, dtype=F32) / half)
    angles = position[:, None] * frequency
    cosine, sine = jnp.cos(angles), jnp.sin(angles)
    return jnp.concatenate([cosine, cosine], -1), jnp.concatenate([-sine, sine], -1)


def turn(tile, cosine, sine):
    return tile * cosine + pltpu.roll(tile, HD // 2, 1) * sine


def chosen(ref, route, n_e, width, at):
    parts = [jnp.where(route == e, ref[:, e * width + at:e * width + at + HD], 0.0) for e in range(n_e)]
    return functools.reduce(lambda a, b: a + b, parts)


def attend_kernel(
    n_e, scale, q_ref, kv_ref, route_ref, gate_ref, cos_ref, sin_ref, qb_ref, kb_ref,
    query_ref, key_ref, value_ref, o_ref, l_ref, mixed_ref,
):
    width = key_ref.shape[1]
    tile = q_ref.shape[0]
    step = pl.program_id(0)

    @pl.when(step == 0)
    def _():
        for at in range(0, width, HD):
            key_ref[:, at:at + HD] = turn(kv_ref[:, at:at + HD], cos_ref[...], sin_ref[...]).astype(BF)
        value_ref[...] = kv_ref[:, width:].astype(BF)

    here = pl.ds(pl.multiple_of(step * tile, tile), tile)
    cosine, sine = cos_ref[here, :], sin_ref[here, :]
    routes = [route_ref[:, j:j + 1] for j in range(TOPK)]
    gates = [gate_ref[:, j:j + 1] for j in range(TOPK)]
    allowed = kb_ref[...] <= jnp.concatenate([qb_ref[...]] * TOPK, axis=1)
    for head in range(width // HD):
        at = head * HD
        q = [turn(chosen(q_ref, routes[j], n_e, width, at), cosine, sine).astype(BF) for j in range(TOPK)]
        for j in range(TOPK):
            query_ref[j, :, at:at + HD] = q[j]
        s = dot_nt(key_ref[:, at:at + HD], jnp.concatenate(q, axis=0))
        s = jnp.where(allowed, s * (scale * LOG2E), NEGATIVE)
        peak = jnp.max(s, axis=0, keepdims=True)
        p = jnp.exp2(s - peak)
        total = jnp.sum(p, axis=0, keepdims=True)
        o = (dot_tn(value_ref[:, at:at + HD], p.astype(BF)) / total).T.astype(BF)
        l_ref[0, head:head + 1, :] = peak + jnp.log2(total)
        o = [o[j * tile:(j + 1) * tile] for j in range(TOPK)]
        for j in range(TOPK):
            o_ref[j, :, at:at + HD] = o[j]
        o = [gates[j] * o[j].astype(F32) for j in range(TOPK)]
        for e in range(n_e):
            parts = [jnp.where(routes[j] == e, o[j], 0.0) for j in range(TOPK)]
            mixed_ref[:, e * width + at:e * width + at + HD] = (parts[0] + parts[1]).astype(BF)


def attend(q_raw, kv_raw, routes, gates, cosine, sine, q_blocks, k_blocks):
    length, wide = q_raw.shape
    width = kv_raw.shape[1] // 2
    n_e, heads = wide // width, width // HD
    tile = 256
    whole = lambda *shape: pl.BlockSpec(shape, lambda i: (0,) * len(shape))
    tiled = lambda cols: pl.BlockSpec((tile, cols), lambda i: (i, 0))
    pair = pl.BlockSpec((TOPK, tile, width), lambda i: (0, i, 0))
    return pl.pallas_call(
        functools.partial(attend_kernel, n_e, HD ** -0.5),
        grid=(length // tile,),
        in_specs=[
            tiled(wide), whole(length, 2 * width), tiled(TOPK), tiled(TOPK), whole(length, HD), whole(length, HD),
            pl.BlockSpec((1, tile), lambda i: (0, i)), whole(length, 1),
        ],
        out_specs=[
            pair, whole(length, width), whole(length, width), pair,
            pl.BlockSpec((1, heads, TOPK * tile), lambda i: (i, 0, 0)), tiled(wide),
        ],
        out_shape=[
            jax.ShapeDtypeStruct((TOPK, length, width), BF),
            jax.ShapeDtypeStruct((length, width), BF),
            jax.ShapeDtypeStruct((length, width), BF),
            jax.ShapeDtypeStruct((TOPK, length, width), BF),
            jax.ShapeDtypeStruct((length // tile, heads, TOPK * tile), F32),
            jax.ShapeDtypeStruct((length, wide), BF),
        ],
        cost_estimate=pl.CostEstimate(flops=length * length, transcendentals=0, bytes_accessed=8 * length * width),
        name="attend",
    )(q_raw, kv_raw, routes, gates, cosine, sine, q_blocks, k_blocks)


def attend_back_kernel(
    n_e, scale, g_ref, route_ref, gate_ref, query_ref, key_ref, value_ref, o_ref, l_ref, cos_ref, sin_ref, qb_ref,
    kb_ref, dq_ref, dkv_ref, note_ref, dk_ref, dv_ref,
):
    width = key_ref.shape[1]
    tile = g_ref.shape[0]
    step = pl.program_id(0)

    @pl.when(step == 0)
    def _():
        dk_ref[...] = jnp.zeros_like(dk_ref)
        dv_ref[...] = jnp.zeros_like(dv_ref)

    here = pl.ds(pl.multiple_of(step * tile, tile), tile)
    cosine, sine = cos_ref[here, :], sin_ref[here, :]
    routes = [route_ref[:, j:j + 1] for j in range(TOPK)]
    gates = [gate_ref[:, j:j + 1] for j in range(TOPK)]
    allowed = kb_ref[...] <= jnp.concatenate([qb_ref[...]] * TOPK, axis=1)
    gate_grads = [jnp.zeros((tile, 1), F32) for _ in range(TOPK)]
    for head in range(width // HD):
        at = head * HD
        k, v = key_ref[:, at:at + HD], value_ref[:, at:at + HD]
        g = [chosen(g_ref, routes[j], n_e, width, at) for j in range(TOPK)]
        o = [o_ref[j, :, at:at + HD].astype(F32) for j in range(TOPK)]
        gate_grads = [gate_grads[j] + jnp.sum(g[j] * o[j], axis=1, keepdims=True) for j in range(TOPK)]
        d = jnp.concatenate([(gates[j] * g[j]).astype(BF) for j in range(TOPK)], axis=0)
        q = jnp.concatenate([query_ref[j, :, at:at + HD] for j in range(TOPK)], axis=0)
        centre = jnp.sum((d.astype(F32) * jnp.concatenate(o, axis=0)).T, axis=0, keepdims=True)
        s = dot_nt(k, q)
        p = jnp.where(allowed, jnp.exp2(s * (scale * LOG2E) - l_ref[0, head:head + 1, :]), 0.0)
        grad_s = (p * (dot_nt(v, d) - centre)).astype(BF)
        dq = (dot_tn(k, grad_s) * scale).T
        dq = [turn(dq[j * tile:(j + 1) * tile], cosine, -sine) for j in range(TOPK)]
        for e in range(n_e):
            parts = [jnp.where(routes[j] == e, dq[j], 0.0) for j in range(TOPK)]
            dq_ref[:, e * width + at:e * width + at + HD] = (parts[0] + parts[1]).astype(BF)
        dk_ref[:, at:at + HD] += dot(grad_s, q) * scale
        dv_ref[:, at:at + HD] += dot(p.astype(BF), d)
    lane = lax.broadcasted_iota(jnp.int32, (tile, HD), 1)
    note = jnp.zeros((tile, HD), F32)
    for j in range(TOPK):
        high = gate_grads[j].astype(BF).astype(F32)
        note = jnp.where(lane == j, high, note)
        note = jnp.where(lane == TOPK + j, gate_grads[j] - high, note)
    note_ref[...] = note.astype(BF)

    @pl.when(step == pl.num_programs(0) - 1)
    def _():
        for at in range(0, width, HD):
            dkv_ref[:, at:at + HD] = turn(dk_ref[:, at:at + HD], cos_ref[...], -sin_ref[...]).astype(BF)
        dkv_ref[:, width:] = dv_ref[...].astype(BF)


def attend_back(g_raw, routes, gates, queries, keys, values, mixed, log_total, cosine, sine, q_blocks, k_blocks):
    length, wide = g_raw.shape
    width = keys.shape[1]
    n_e, heads = wide // width, width // HD
    tile = 256
    whole = lambda *shape: pl.BlockSpec(shape, lambda i: (0,) * len(shape))
    tiled = lambda cols: pl.BlockSpec((tile, cols), lambda i: (i, 0))
    pair = pl.BlockSpec((TOPK, tile, width), lambda i: (0, i, 0))
    return pl.pallas_call(
        functools.partial(attend_back_kernel, n_e, HD ** -0.5),
        grid=(length // tile,),
        in_specs=[
            tiled(wide), tiled(TOPK), tiled(TOPK), pair, whole(length, width), whole(length, width), pair,
            pl.BlockSpec((1, heads, TOPK * tile), lambda i: (i, 0, 0)), whole(length, HD), whole(length, HD),
            pl.BlockSpec((1, tile), lambda i: (0, i)), whole(length, 1),
        ],
        out_specs=[tiled(wide), whole(length, 2 * width), tiled(HD)],
        out_shape=[
            jax.ShapeDtypeStruct((length, wide), BF),
            jax.ShapeDtypeStruct((length, 2 * width), BF),
            jax.ShapeDtypeStruct((length, HD), BF),
        ],
        scratch_shapes=[pltpu.VMEM((length, width), F32), pltpu.VMEM((length, width), F32)],
        cost_estimate=pl.CostEstimate(flops=length * length, transcendentals=0, bytes_accessed=8 * length * width),
        name="attend_back",
    )(g_raw, routes, gates, queries, keys, values, mixed, log_total, cosine, sine, q_blocks, k_blocks)


def pick(table, routes, ids):
    parts = jnp.split(table, len(ids), axis=1)
    return [sum(jnp.where(routes[:, j:j + 1] == e, part, 0.0) for e, part in zip(ids, parts)) for j in range(TOPK)]


def place(pieces, routes, ids):
    return jnp.concatenate(
        [sum(jnp.where(routes[:, j:j + 1] == e, pieces[j], 0.0) for j in range(TOPK)) for e in ids], axis=1
    )


def pair_softmax(logits):
    peak = jnp.maximum(logits[0], logits[1])
    powers = [jnp.exp(v - peak) for v in logits]
    total = powers[0] + powers[1]
    return [v / total for v in powers]


def local(
    inputs, cotangent, blocks, attn_routes, ffn_routes, w_key, w_value, attn_router, ffn_router, attn_gain, ffn_gain,
    attn_bias, ffn_bias, w_query, w_out, w_gate, w_up, w_down,
):
    n_e, n_s = lax.axis_size("expert"), lax.axis_size("shard")
    me = lax.axis_index("expert")
    tokens, width = inputs.shape[1:]
    ids = list(range(n_e))
    capacity = 5 * tokens * TOPK // (4 * n_e)
    group = w_key.shape[1] // n_e
    length = n_e * tokens
    small_rows = w_key.shape[0]

    def swap(value, k):
        return lax.ppermute(value, "expert", [(i, i ^ k) for i in range(n_e)])

    def after(value, *others):
        return lax.optimization_barrier((value,) + others)[0]

    def spread(value):
        return jnp.concatenate([value] + [swap(value, k) for k in range(1, n_e)], axis=0)

    def fetch(block):
        return [block] + [swap(block, k) for k in range(1, 3 if n_e == 4 else n_e)]

    def fetch_rest(blocks, *others):
        if n_e != 4:
            return blocks
        half = blocks[0].shape[0] // 2
        one, two = after(blocks[1], *others), after(blocks[2], *others)
        return blocks + [jnp.concatenate([swap(one[:half], 2), swap(two[half:], 1)], axis=0)]

    def add_low(a, b):
        return (a.astype(F32) + b.astype(F32)).astype(BF)

    def deliver_first(far):
        return [swap(far[0], 1), swap(far[1], 2)] if n_e == 4 else []

    def deliver_near(parts):
        if n_e != 4:
            return [swap(parts[k][i], k) for i in range(2) for k in range(1, n_e)]
        return [swap(parts[1][0], 1), swap(parts[2][1], 2)]

    def deliver_last(parts, halves):
        if n_e != 4:
            return []
        return [swap(add_low(parts[2][0], halves[0]), 2), swap(add_low(parts[1][1], halves[1]), 1)]

    def total(own, near, last):
        count = len(near) // 2
        return [
            sum(v.astype(F32) for v in [own[i]] + near[i * count:(i + 1) * count] + last[i:i + 1]) for i in range(2)
        ]

    def collect(value):
        parts = jnp.split(value, n_e, axis=0)
        return sum([parts[0].astype(F32)] + [swap(parts[k], k).astype(F32) for k in range(1, n_e)])

    def shuffle(value, axis):
        return lax.all_to_all(value, axis, split_axis=0, concat_axis=0, tiled=True)

    def trade(value):
        out = jnp.zeros_like(value)
        for k in range(n_e):
            piece = lax.dynamic_index_in_dim(value, me ^ k, 0, False)
            out = lax.dynamic_update_index_in_dim(out, swap(piece, k) if k else piece, me ^ k, 0)
        return out

    def gather_shard(value):
        return lax.all_gather(value, "shard", axis=0, tiled=True)

    def scatter_shard(value):
        return lax.psum_scatter(value, "shard", scatter_dimension=0, tiled=True)

    small = jnp.concatenate(
        [attn_router, ffn_router, attn_gain[:, None], ffn_gain[:, None], attn_bias[:, None], ffn_bias[:, None]], axis=1
    )
    small_width = small.shape[1]
    route_width = tokens * TOPK // (n_e * small_rows)
    small = jnp.pad(small, ((0, 0), (0, 128 - small_width)))
    packed = jnp.concatenate(
        [
            w_key.reshape(small_rows, n_e, group).transpose(1, 0, 2),
            w_value.reshape(small_rows, n_e, group).transpose(1, 0, 2),
            jnp.broadcast_to(small[None], (n_e,) + small.shape),
        ],
        axis=2,
    )
    packed = shuffle(packed, "expert")
    route_at = 2 * group + small_width
    packed = packed.at[:, :, route_at:route_at + route_width].set(
        ffn_routes[0].astype(BF).reshape(n_e, small_rows, route_width)
    )
    packed = gather_shard(packed[None])
    routes_f = packed[:, :, :, route_at:route_at + route_width].reshape(n_s * tokens, TOPK).astype(jnp.int32)
    packed = packed.transpose(1, 0, 2, 3).reshape(width, -1)
    key_value_w = packed[:, :2 * group]
    small = packed[:, 2 * group:2 * group + small_width].astype(F32)
    router_a, router_f = small[:, :n_e], small[:, n_e:2 * n_e]
    gain_a, gain_f, bias_a, bias_f = (small[:, 2 * n_e + i] for i in range(4))

    def to_heads(value):
        rows = value.shape[0]
        value = shuffle(value.reshape(rows, n_e, group).transpose(1, 0, 2), "expert")
        return value.transpose(1, 0, 2).reshape(rows, n_e * group)

    def from_heads(value):
        rows = value.shape[0]
        value = trade(value.reshape(rows, n_e, group).transpose(1, 0, 2))
        return value.transpose(1, 0, 2).reshape(rows, n_e * group)

    notes = jnp.concatenate([blocks[0][:, None], attn_routes[0]], axis=1).astype(BF)
    carried = jnp.concatenate([inputs[0], jnp.pad(notes, ((0, 0), (0, 128 - 1 - TOPK)))], axis=1)
    carried = lax.optimization_barrier(spread(carried))
    query_w = gather_shard(to_heads(w_query[0]))

    hidden_units = w_down.shape[1]
    turned = jnp.stack([w_gate[0].T.reshape(n_s, hidden_units, -1), w_up[0].T.reshape(n_s, hidden_units, -1)], axis=1)
    turned = shuffle(after(turned, query_w), "shard").reshape(n_s, 2 * hidden_units, -1)
    gate_up_own = turned.transpose(1, 0, 2).reshape(2 * hidden_units, width)
    down_w = fetch(w_down[0])

    own = inputs[0].astype(F32)
    cot = cotangent[0]
    seq_in = carried[:, :width].astype(F32)
    notes = carried[:, width:width + 1 + TOPK].astype(jnp.int32)
    seq_blocks, routes_a = notes[:, 0], notes[:, 1:]
    position = jnp.concatenate([(me ^ k) * tokens + jnp.arange(tokens, dtype=jnp.int32) for k in range(n_e)]).astype(F32)
    cosine, sine = rope_tables(position)
    h_attn = (seq_in * inverse_rms(seq_in) * gain_a).astype(BF)
    logits_a = dot(h_attn, router_a.astype(BF))
    gates_a = pair_softmax(pick(logits_a, routes_a, ids))
    key_value = dot(h_attn, key_value_w)
    key_value, out_w = lax.optimization_barrier((key_value, w_out[0]))
    out_rows = out_w.shape[0]
    turned = shuffle(out_w.T, "shard").reshape(n_s, width // n_s, out_rows).transpose(1, 0, 2)
    out_wt = gather_shard(to_heads(turned.reshape(width // n_s, n_s * out_rows)))
    gate_pair = jnp.concatenate(gates_a, axis=1)
    row_blocks, key_blocks = seq_blocks.reshape(1, -1), seq_blocks.reshape(-1, 1)
    query_raw = dot(h_attn, query_w)
    query_raw, *down_w = lax.optimization_barrier((query_raw, *down_w))
    down_w = fetch_rest(down_w)
    queries, keys, values, mixed, log_total, mixed_all = attend(
        query_raw, key_value, routes_a, gate_pair, cosine, sine, row_blocks, key_blocks
    )
    mixed_out, *down_w = lax.optimization_barrier((mixed_all, *down_w))
    middle = own + collect(dot_nt(mixed_out, out_wt).astype(BF)) + bias_a

    inv_f = inverse_rms(middle)
    h_ffn = (middle * inv_f * gain_f).astype(BF)
    h_ffn, gate_up_own = lax.optimization_barrier((h_ffn, gate_up_own))
    gate_up_w = fetch(gate_up_own)
    h_all = gather_shard(h_ffn)
    cot_all = gather_shard(after(cot, h_ffn))
    logits_f = dot(h_all, router_f.astype(BF))
    gates_f = pair_softmax(pick(logits_f, routes_f, ids))
    routes_blocks = routes_f.reshape(n_s, tokens, TOPK)
    h_blocks = h_all.reshape(n_s, tokens, width)
    triangle = (jnp.arange(tokens)[:, None] <= jnp.arange(tokens)[None, :]).astype(BF)

    def rows_of(select, source):
        return lax.dot_general(
            select, source, (((2,), (1,)), ((0,), (0,))), preferred_element_type=F32
        ).astype(BF).reshape(n_s * capacity, width)

    selects, hiddens, back_rows_f = [], [], []
    grad_gate_f = [0.0] * TOPK
    grad_pieces = []
    for k in range(n_e):
        if k == 1:
            gate_up_w = fetch_rest(gate_up_w, hiddens[0])
        expert = me ^ k
        named = [routes_blocks[:, :, j] == expert for j in range(TOPK)]
        any_named = named[0] | named[1]
        rank = dot(any_named.astype(BF), triangle).astype(jnp.int32) - 1
        hit = (rank[:, None, :] == jnp.arange(capacity, dtype=jnp.int32)[None, :, None]) & any_named[:, None, :]
        select = hit.astype(BF)
        gate_token = sum(jnp.where(named[j], gates_f[j].reshape(n_s, tokens), 0.0) for j in range(TOPK))
        gate_slot = jnp.sum(jnp.where(hit, gate_token[:, None, :], 0.0), axis=2).reshape(1, -1)
        rows = rows_of(select, h_blocks)
        pre = dot_nt(gate_up_w[k], rows)
        if k == 0:
            cot_blocks = after(cot_all, pre).reshape(n_s, tokens, width)
        gate_pre, up_pre = pre[:hidden_units], pre[hidden_units:]
        cot_rows = rows_of(select, cot_blocks)
        grad_hidden = dot_nt(down_w[k], cot_rows)
        sigma = 1.0 / (1.0 + jnp.exp(-gate_pre))
        silu = gate_pre * sigma
        hidden = silu * up_pre
        grad_slot = jnp.sum(grad_hidden * hidden, axis=0).reshape(n_s, capacity)
        grad_hidden = grad_hidden * gate_slot
        hidden = (hidden * gate_slot).astype(BF)
        grad_gate = (grad_hidden * up_pre * sigma * (1.0 + gate_pre * (1.0 - sigma))).astype(BF)
        grad_pre = jnp.concatenate([grad_gate, (grad_hidden * silu).astype(BF)], axis=0)
        back = dot_tn(grad_pre, gate_up_w[k]).astype(BF)
        selects.append(select)
        back_rows_f.append(back.reshape(n_s, capacity, width))
        hiddens.append(hidden)
        grad_token = jnp.sum(jnp.where(hit, grad_slot[:, :, None], 0.0), axis=1)
        grad_gate_f = [grad_gate_f[j] + jnp.where(named[j], grad_token, 0.0) for j in range(TOPK)]
        grad_pieces.append((rows, cot_rows, grad_pre))
    select = jnp.concatenate(selects, axis=1)

    def tokens_of(row_list):
        return lax.dot_general(
            select, jnp.concatenate(row_list, axis=1), (((1,), (1,)), ((0,), (0,))), preferred_element_type=F32
        ).astype(BF).reshape(n_s * tokens, width)

    back_sum = tokens_of(back_rows_f)
    back_f = scatter_shard(back_sum)

    def gate_up_grads(k, *others):
        rows, _, grad_pre = grad_pieces[k]
        rows = after(rows, *others)
        return [dot(v, rows).astype(BF) for v in jnp.split(grad_pre, 2, axis=0)]

    grad_gate_up = [None] * n_e
    grad_gate_up[n_e - 1] = gate_up_grads(n_e - 1, back_sum)
    halves = deliver_first(grad_gate_up[n_e - 1])
    out_rows_f = []
    for k in range(n_e):
        hidden = after(hiddens[k], *(grad_gate_up[n_e - 1] if k < 2 else halves))
        out_rows_f.append(dot_tn(hidden, down_w[k]).astype(BF).reshape(n_s, capacity, width))
    out_sum = tokens_of(out_rows_f)
    ffn_out = scatter_shard(out_sum)
    back_f, out_sum = lax.optimization_barrier((back_f, out_sum))
    back_f = back_f.astype(F32)
    grad_gates_f = jnp.sum(
        shuffle(jnp.stack(grad_gate_f, axis=1).reshape(n_s, TOPK * tokens), "shard"), axis=0
    ).reshape(TOPK, tokens, 1)


    grad_out = cot.astype(F32)
    own_routes_f = ffn_routes[0]
    own_gates_f = pair_softmax(pick(dot(h_ffn, router_f.astype(BF)), own_routes_f, ids))

    def logit_grads(gates, grads, routes):
        centre = sum(gates[j] * grads[j] for j in range(TOPK))
        return place([gates[j] * (grads[j] - centre) for j in range(TOPK)], routes, ids)

    grad_logits_f = logit_grads(own_gates_f, grad_gates_f, own_routes_f)
    grad_router_f = dot_tn(h_ffn.astype(F32), grad_logits_f, PRECISE)
    grad_h_ffn = back_f + jnp.dot(grad_logits_f, router_f.T, precision=PRECISE)
    grad_norm, grad_gain_f = norm_back(grad_h_ffn, middle, inv_f, gain_f)
    grad_middle = grad_out + grad_norm
    grad_bias_f = jnp.sum(grad_out, axis=0)
    grad_bias_a = jnp.sum(grad_middle, axis=0)

    grad_middle_low = grad_middle.astype(BF)
    for k in range(n_e - 1):
        grad_gate_up[k] = gate_up_grads(k, back_f)
    seq_grad = spread(grad_middle_low)
    seq_grad, grad_gate_up = lax.optimization_barrier((seq_grad, grad_gate_up))
    near = deliver_near(grad_gate_up)
    last = deliver_last(grad_gate_up, halves)
    grad_mixed = dot(seq_grad, out_wt)
    grad_out_wt = dot_tn(seq_grad, mixed_all).astype(BF)
    grad_mixed, grad_out_wt = lax.optimization_barrier((grad_mixed, grad_out_wt))
    grad_query_all, grad_key_value, gate_notes = attend_back(
        grad_mixed, routes_a, gate_pair, queries, keys, values, mixed, log_total, cosine, sine, row_blocks, key_blocks
    )
    grad_query_all, *near = lax.optimization_barrier((grad_query_all, *near))
    back_a = (dot_nt(grad_query_all, query_w) + dot_nt(grad_key_value, key_value_w)).astype(BF)
    back_a = jnp.concatenate([back_a, gate_notes], axis=1)
    value = scatter_shard(grad_out_wt)
    back_a, ffn_out, *last = lax.optimization_barrier((back_a, ffn_out, *last))
    gate_up_total = [v.astype(BF) for v in total(grad_gate_up[0], near, last)]
    outputs = (middle + ffn_out.astype(F32) + bias_f).astype(BF)[None]
    key_value_grad = after(dot_tn(h_attn, grad_key_value).astype(BF), back_a)
    key_value_grad = key_value_grad.reshape(n_e, n_s, small_rows, 2 * group).transpose(1, 0, 2, 3)
    key_value_grad = scatter_shard(key_value_grad.reshape(n_s * n_e * small_rows, 2 * group))
    query_grad = dot_tn(h_attn, grad_query_all).astype(BF)
    query_grad, value = lax.optimization_barrier((query_grad, value))
    query_grad = scatter_shard(query_grad)
    value = from_heads(value).reshape(width // n_s, n_s, out_rows).transpose(1, 0, 2)

    def to_rows(value):
        value = shuffle(value.reshape(hidden_units, n_s, width // n_s).transpose(1, 0, 2), "shard")
        return value.reshape(n_s * hidden_units, width // n_s)

    grad_out_w = shuffle(value, "shard").reshape(width, out_rows)
    grad_out_w, gate_total = lax.optimization_barrier((grad_out_w, gate_up_total[0]))
    grad_out_w = grad_out_w.T.astype(F32)[None]
    gate_turned = to_rows(gate_total)
    grad_down = []
    for k in range(n_e):
        hidden = after(hiddens[k], back_a)
        grad_down.append([dot(v, grad_pieces[k][1]).astype(BF) for v in jnp.split(hidden, 2, axis=0)])
    halves = deliver_first(grad_down[n_e - 1])
    back_a = collect(back_a)
    near, last = deliver_near(grad_down), deliver_last(grad_down, halves)
    back_a, gate_turned, *near = lax.optimization_barrier((back_a, gate_turned, *near))
    up_total, key_value_grad = lax.optimization_barrier((after(gate_up_total[1], gate_turned), key_value_grad))
    up_turned = to_rows(up_total)
    grad_down_w = jnp.concatenate(total(grad_down[0], near, last), axis=0)[None]
    key_value_grad = trade(key_value_grad.reshape(n_e, small_rows, -1))
    grad_key_w = key_value_grad[:, :, :group].transpose(1, 0, 2).reshape(small_rows, -1).astype(F32)
    grad_value_w = key_value_grad[:, :, group:].transpose(1, 0, 2).reshape(small_rows, -1).astype(F32)
    gate_grads = back_a[:, width:width + TOPK] + back_a[:, width + TOPK:width + 2 * TOPK]
    grad_gates_a = [gate_grads[:, j:j + 1] for j in range(TOPK)]
    back_a = back_a[:, :width]
    grad_query_w = from_heads(query_grad).astype(F32)[None]
    grad_gate_w = gate_turned.T.astype(F32)[None]

    h_own = h_attn[:tokens]
    own_routes_a = attn_routes[0]
    own_gates_a = [v[:tokens] for v in gates_a]
    grad_logits_a = logit_grads(own_gates_a, grad_gates_a, own_routes_a)
    grad_router_a = dot_tn(h_own.astype(F32), grad_logits_a, PRECISE)
    grad_h_attn = back_a + jnp.dot(grad_logits_a, router_a.T, precision=PRECISE)
    grad_norm, grad_gain_a = norm_back(grad_h_attn, own, inverse_rms(own), gain_a)
    input_grad = (grad_middle + grad_norm).astype(BF)[None]

    shared = jnp.concatenate(
        [grad_router_a, grad_router_f]
        + [v[:, None] for v in (grad_gain_a, grad_gain_f, grad_bias_a, grad_bias_f)],
        axis=1,
    )
    shared, up_turned = lax.optimization_barrier((shared, up_turned))
    grad_up_w = up_turned.T.astype(F32)[None]
    shared = shuffle(shared.reshape(n_e * n_s, -1), ("expert", "shard"))
    shared = jnp.sum(shared, axis=0).reshape(small_rows, small_width)
    return (
        outputs,
        input_grad,
        grad_key_w,
        grad_value_w,
        shared[:, :n_e],
        shared[:, n_e:2 * n_e],
        shared[:, 2 * n_e],
        shared[:, 2 * n_e + 1],
        shared[:, 2 * n_e + 2],
        shared[:, 2 * n_e + 3],
        grad_query_w,
        grad_out_w,
        grad_gate_w,
        grad_up_w,
        grad_down_w,
    )


def solution(mesh):
    rows = P("shard", "expert", None)
    shared, vector = P(("expert", "shard"), None), P(("expert", "shard"))
    weight = P("expert", "shard", None)
    in_specs = (rows, rows, P("shard", "expert"), rows, rows) + (shared,) * 4 + (vector,) * 4 + (weight,) * 5
    out_specs = (rows, rows) + (shared,) * 4 + (vector,) * 4 + (weight,) * 5
    return jax.shard_map(local, mesh=mesh, in_specs=in_specs, out_specs=out_specs, check_vma=False)
```

```python
import functools
import math

import jax
import jax.numpy as jnp
from jax import lax
from jax.experimental import pallas as pl
from jax.experimental.pallas import tpu as pltpu
from jax.sharding import PartitionSpec as P

HD = 128
TOPK = 2
EPSILON = 1e-06
NEGATIVE = -1e30
ROPE_BASE = 10000.0
PRECISE = lax.Precision.HIGHEST
BF = jnp.bfloat16
F32 = jnp.float32
LOG2E = 1.4426950408889634


def dot(a, b):
    return jnp.dot(a, b, preferred_element_type=F32)


def dot_tn(a, b, precision=None):
    return lax.dot_general(a, b, (((0,), (0,)), ((), ())), precision=precision, preferred_element_type=F32)


def dot_nt(a, b):
    return lax.dot_general(a, b, (((1,), (1,)), ((), ())), preferred_element_type=F32)


def inverse_rms(values):
    return lax.rsqrt(jnp.mean(values * values, axis=-1, keepdims=True) + EPSILON)


def norm_back(grad, values, inv, gain):
    u = grad * gain
    centre = jnp.mean(u * values, axis=-1, keepdims=True)
    return inv * (u - values * (inv * inv) * centre), jnp.sum(grad * values * inv, axis=0)


def rope_tables(position):
    half = HD // 2
    frequency = jnp.exp(-math.log(ROPE_BASE) * jnp.arange(half, dtype=F32) / half)
    angles = position[:, None] * frequency
    cosine, sine = jnp.cos(angles), jnp.sin(angles)
    return jnp.concatenate([cosine, cosine], -1), jnp.concatenate([-sine, sine], -1)


def turn(tile, cosine, sine):
    return tile * cosine + pltpu.roll(tile, HD // 2, 1) * sine


def chosen(ref, route, n_e, width, at):
    parts = [jnp.where(route == e, ref[:, e * width + at:e * width + at + HD], 0.0) for e in range(n_e)]
    return functools.reduce(lambda a, b: a + b, parts)


def attend_kernel(
    n_e, scale, q_ref, kv_ref, route_ref, gate_ref, cos_ref, sin_ref, qb_ref, kb_ref,
    query_ref, key_ref, value_ref, o_ref, l_ref, mixed_ref,
):
    width = key_ref.shape[1]
    tile = q_ref.shape[0]
    step = pl.program_id(0)

    @pl.when(step == 0)
    def _():
        for at in range(0, width, HD):
            key_ref[:, at:at + HD] = turn(kv_ref[:, at:at + HD], cos_ref[...], sin_ref[...]).astype(BF)
        value_ref[...] = kv_ref[:, width:].astype(BF)

    here = pl.ds(pl.multiple_of(step * tile, tile), tile)
    cosine, sine = cos_ref[here, :], sin_ref[here, :]
    routes = [route_ref[:, j:j + 1] for j in range(TOPK)]
    gates = [gate_ref[:, j:j + 1] for j in range(TOPK)]
    allowed = kb_ref[...] <= jnp.concatenate([qb_ref[...]] * TOPK, axis=1)
    for head in range(width // HD):
        at = head * HD
        q = [turn(chosen(q_ref, routes[j], n_e, width, at), cosine, sine).astype(BF) for j in range(TOPK)]
        for j in range(TOPK):
            query_ref[j, :, at:at + HD] = q[j]
        s = dot_nt(key_ref[:, at:at + HD], jnp.concatenate(q, axis=0))
        s = jnp.where(allowed, s * (scale * LOG2E), NEGATIVE)
        peak = jnp.max(s, axis=0, keepdims=True)
        p = jnp.exp2(s - peak)
        total = jnp.sum(p, axis=0, keepdims=True)
        o = (dot_tn(value_ref[:, at:at + HD], p.astype(BF)) / total).T.astype(BF)
        l_ref[0, head:head + 1, :] = peak + jnp.log2(total)
        o = [o[j * tile:(j + 1) * tile] for j in range(TOPK)]
        for j in range(TOPK):
            o_ref[j, :, at:at + HD] = o[j]
        o = [gates[j] * o[j].astype(F32) for j in range(TOPK)]
        for e in range(n_e):
            parts = [jnp.where(routes[j] == e, o[j], 0.0) for j in range(TOPK)]
            mixed_ref[:, e * width + at:e * width + at + HD] = (parts[0] + parts[1]).astype(BF)


def attend(q_raw, kv_raw, routes, gates, cosine, sine, q_blocks, k_blocks):
    length, wide = q_raw.shape
    width = kv_raw.shape[1] // 2
    n_e, heads = wide // width, width // HD
    tile = 256
    whole = lambda *shape: pl.BlockSpec(shape, lambda i: (0,) * len(shape))
    tiled = lambda cols: pl.BlockSpec((tile, cols), lambda i: (i, 0))
    pair = pl.BlockSpec((TOPK, tile, width), lambda i: (0, i, 0))
    return pl.pallas_call(
        functools.partial(attend_kernel, n_e, HD ** -0.5),
        grid=(length // tile,),
        in_specs=[
            tiled(wide), whole(length, 2 * width), tiled(TOPK), tiled(TOPK), whole(length, HD), whole(length, HD),
            pl.BlockSpec((1, tile), lambda i: (0, i)), whole(length, 1),
        ],
        out_specs=[
            pair, whole(length, width), whole(length, width), pair,
            pl.BlockSpec((1, heads, TOPK * tile), lambda i: (i, 0, 0)), tiled(wide),
        ],
        out_shape=[
            jax.ShapeDtypeStruct((TOPK, length, width), BF),
            jax.ShapeDtypeStruct((length, width), BF),
            jax.ShapeDtypeStruct((length, width), BF),
            jax.ShapeDtypeStruct((TOPK, length, width), BF),
            jax.ShapeDtypeStruct((length // tile, heads, TOPK * tile), F32),
            jax.ShapeDtypeStruct((length, wide), BF),
        ],
        cost_estimate=pl.CostEstimate(flops=length * length, transcendentals=0, bytes_accessed=8 * length * width),
        name="attend",
    )(q_raw, kv_raw, routes, gates, cosine, sine, q_blocks, k_blocks)


def attend_back_kernel(
    n_e, scale, g_ref, route_ref, gate_ref, query_ref, key_ref, value_ref, o_ref, l_ref, cos_ref, sin_ref, qb_ref,
    kb_ref, dq_ref, dkv_ref, note_ref, dk_ref, dv_ref,
):
    width = key_ref.shape[1]
    tile = g_ref.shape[0]
    step = pl.program_id(0)

    @pl.when(step == 0)
    def _():
        dk_ref[...] = jnp.zeros_like(dk_ref)
        dv_ref[...] = jnp.zeros_like(dv_ref)

    here = pl.ds(pl.multiple_of(step * tile, tile), tile)
    cosine, sine = cos_ref[here, :], sin_ref[here, :]
    routes = [route_ref[:, j:j + 1] for j in range(TOPK)]
    gates = [gate_ref[:, j:j + 1] for j in range(TOPK)]
    allowed = kb_ref[...] <= jnp.concatenate([qb_ref[...]] * TOPK, axis=1)
    gate_grads = [jnp.zeros((tile, 1), F32) for _ in range(TOPK)]
    for head in range(width // HD):
        at = head * HD
        k, v = key_ref[:, at:at + HD], value_ref[:, at:at + HD]
        g = [chosen(g_ref, routes[j], n_e, width, at) for j in range(TOPK)]
        o = [o_ref[j, :, at:at + HD].astype(F32) for j in range(TOPK)]
        gate_grads = [gate_grads[j] + jnp.sum(g[j] * o[j], axis=1, keepdims=True) for j in range(TOPK)]
        d = jnp.concatenate([(gates[j] * g[j]).astype(BF) for j in range(TOPK)], axis=0)
        q = jnp.concatenate([query_ref[j, :, at:at + HD] for j in range(TOPK)], axis=0)
        centre = jnp.sum((d.astype(F32) * jnp.concatenate(o, axis=0)).T, axis=0, keepdims=True)
        s = dot_nt(k, q)
        p = jnp.where(allowed, jnp.exp2(s * (scale * LOG2E) - l_ref[0, head:head + 1, :]), 0.0)
        grad_s = (p * (dot_nt(v, d) - centre)).astype(BF)
        dq = (dot_tn(k, grad_s) * scale).T
        dq = [turn(dq[j * tile:(j + 1) * tile], cosine, -sine) for j in range(TOPK)]
        for e in range(n_e):
            parts = [jnp.where(routes[j] == e, dq[j], 0.0) for j in range(TOPK)]
            dq_ref[:, e * width + at:e * width + at + HD] = (parts[0] + parts[1]).astype(BF)
        dk_ref[:, at:at + HD] += dot(grad_s, q) * scale
        dv_ref[:, at:at + HD] += dot(p.astype(BF), d)
    lane = lax.broadcasted_iota(jnp.int32, (tile, HD), 1)
    note = jnp.zeros((tile, HD), F32)
    for j in range(TOPK):
        high = gate_grads[j].astype(BF).astype(F32)
        note = jnp.where(lane == j, high, note)
        note = jnp.where(lane == TOPK + j, gate_grads[j] - high, note)
    note_ref[...] = note.astype(BF)

    @pl.when(step == pl.num_programs(0) - 1)
    def _():
        for at in range(0, width, HD):
            dkv_ref[:, at:at + HD] = turn(dk_ref[:, at:at + HD], cos_ref[...], -sin_ref[...]).astype(BF)
        dkv_ref[:, width:] = dv_ref[...].astype(BF)


def attend_back(g_raw, routes, gates, queries, keys, values, mixed, log_total, cosine, sine, q_blocks, k_blocks):
    length, wide = g_raw.shape
    width = keys.shape[1]
    n_e, heads = wide // width, width // HD
    tile = 256
    whole = lambda *shape: pl.BlockSpec(shape, lambda i: (0,) * len(shape))
    tiled = lambda cols: pl.BlockSpec((tile, cols), lambda i: (i, 0))
    pair = pl.BlockSpec((TOPK, tile, width), lambda i: (0, i, 0))
    return pl.pallas_call(
        functools.partial(attend_back_kernel, n_e, HD ** -0.5),
        grid=(length // tile,),
        in_specs=[
            tiled(wide), tiled(TOPK), tiled(TOPK), pair, whole(length, width), whole(length, width), pair,
            pl.BlockSpec((1, heads, TOPK * tile), lambda i: (i, 0, 0)), whole(length, HD), whole(length, HD),
            pl.BlockSpec((1, tile), lambda i: (0, i)), whole(length, 1),
        ],
        out_specs=[tiled(wide), whole(length, 2 * width), tiled(HD)],
        out_shape=[
            jax.ShapeDtypeStruct((length, wide), BF),
            jax.ShapeDtypeStruct((length, 2 * width), BF),
            jax.ShapeDtypeStruct((length, HD), BF),
        ],
        scratch_shapes=[pltpu.VMEM((length, width), F32), pltpu.VMEM((length, width), F32)],
        cost_estimate=pl.CostEstimate(flops=length * length, transcendentals=0, bytes_accessed=8 * length * width),
        name="attend_back",
    )(g_raw, routes, gates, queries, keys, values, mixed, log_total, cosine, sine, q_blocks, k_blocks)


def expert_kernel(row_ref, cot_ref, gate_ref, wide_ref, down_ref, hidden_ref, grad_ref, back_ref, slot_ref):
    half = down_ref.shape[0]
    rows = row_ref[...]
    gate_pre, up_pre = dot_nt(wide_ref[:half], rows), dot_nt(wide_ref[half:], rows)
    grad_hidden = dot_nt(down_ref[...], cot_ref[...])
    sigma = 1.0 / (1.0 + jnp.exp(-gate_pre))
    silu = gate_pre * sigma
    hidden = silu * up_pre
    slot_ref[...] = jnp.sum(grad_hidden * hidden, axis=0, keepdims=True)
    gate = gate_ref[...]
    grad_hidden = grad_hidden * gate
    hidden_ref[...] = (hidden * gate).astype(BF)
    grad_ref[:half] = (grad_hidden * up_pre * sigma * (1.0 + gate_pre * (1.0 - sigma))).astype(BF)
    grad_ref[half:] = (grad_hidden * silu).astype(BF)
    back_ref[...] = dot_tn(grad_ref[...], wide_ref[...]).astype(BF)


def expert_pass(rows, cot_rows, gates, wide, down):
    count, width = rows.shape
    half = down.shape[0]
    tile = 256
    kept = lambda shape: pl.BlockSpec(shape, lambda i: (0, 0), pipeline_mode=pl.Buffered(1))
    tiled = pl.BlockSpec((tile, width), lambda i: (i, 0))
    turned = lambda size: pl.BlockSpec((size, tile), lambda i: (0, i))
    return pl.pallas_call(
        expert_kernel,
        grid=(count // tile,),
        in_specs=[tiled, tiled, turned(1), kept(wide.shape), kept(down.shape)],
        out_specs=[turned(half), turned(2 * half), tiled, turned(1)],
        out_shape=[
            jax.ShapeDtypeStruct((half, count), BF),
            jax.ShapeDtypeStruct((2 * half, count), BF),
            jax.ShapeDtypeStruct((count, width), BF),
            jax.ShapeDtypeStruct((1, count), F32),
        ],
        cost_estimate=pl.CostEstimate(
            flops=10 * count * width * half, transcendentals=count * half, bytes_accessed=6 * count * width + 6 * half * width
        ),
        name="expert_pass",
    )(rows, cot_rows, gates, wide, down)


def pick(table, routes, ids):
    parts = jnp.split(table, len(ids), axis=1)
    return [sum(jnp.where(routes[:, j:j + 1] == e, part, 0.0) for e, part in zip(ids, parts)) for j in range(TOPK)]


def place(pieces, routes, ids):
    return jnp.concatenate(
        [sum(jnp.where(routes[:, j:j + 1] == e, pieces[j], 0.0) for j in range(TOPK)) for e in ids], axis=1
    )


def pair_softmax(logits):
    peak = jnp.maximum(logits[0], logits[1])
    powers = [jnp.exp(v - peak) for v in logits]
    total = powers[0] + powers[1]
    return [v / total for v in powers]


def local(
    inputs, cotangent, blocks, attn_routes, ffn_routes, w_key, w_value, attn_router, ffn_router, attn_gain, ffn_gain,
    attn_bias, ffn_bias, w_query, w_out, w_gate, w_up, w_down,
):
    n_e, n_s = lax.axis_size("expert"), lax.axis_size("shard")
    me = lax.axis_index("expert")
    tokens, width = inputs.shape[1:]
    ids = list(range(n_e))
    capacity = 5 * tokens * TOPK // (4 * n_e)
    group = w_key.shape[1] // n_e
    length = n_e * tokens
    small_rows = w_key.shape[0]

    def swap(value, k):
        return lax.ppermute(value, "expert", [(i, i ^ k) for i in range(n_e)])

    def after(value, *others):
        return lax.optimization_barrier((value,) + others)[0]

    def spread(value):
        return jnp.concatenate([value] + [swap(value, k) for k in range(1, n_e)], axis=0)

    def fetch(block):
        return [block] + [swap(block, k) for k in range(1, 3 if n_e == 4 else n_e)]

    def fetch_rest(blocks, *others):
        if n_e != 4:
            return blocks
        half = blocks[0].shape[0] // 2
        one, two = after(blocks[1], *others), after(blocks[2], *others)
        return blocks + [jnp.concatenate([swap(one[:half], 2), swap(two[half:], 1)], axis=0)]

    def add_low(a, b):
        return (a.astype(F32) + b.astype(F32)).astype(BF)

    def deliver_first(far):
        return [swap(far[0], 1), swap(far[1], 2)] if n_e == 4 else []

    def deliver_near(parts):
        if n_e != 4:
            return [swap(parts[k][i], k) for i in range(2) for k in range(1, n_e)]
        return [swap(parts[1][0], 1), swap(parts[2][1], 2)]

    def deliver_last(parts, halves):
        if n_e != 4:
            return []
        return [swap(add_low(parts[2][0], halves[0]), 2), swap(add_low(parts[1][1], halves[1]), 1)]

    def total(own, near, last):
        count = len(near) // 2
        return [
            sum(v.astype(F32) for v in [own[i]] + near[i * count:(i + 1) * count] + last[i:i + 1]) for i in range(2)
        ]

    def collect(value):
        parts = jnp.split(value, n_e, axis=0)
        return sum([parts[0].astype(F32)] + [swap(parts[k], k).astype(F32) for k in range(1, n_e)])

    def shuffle(value, axis):
        return lax.all_to_all(value, axis, split_axis=0, concat_axis=0, tiled=True)

    def trade(value):
        out = jnp.zeros_like(value)
        for k in range(n_e):
            piece = lax.dynamic_index_in_dim(value, me ^ k, 0, False)
            out = lax.dynamic_update_index_in_dim(out, swap(piece, k) if k else piece, me ^ k, 0)
        return out

    def gather_shard(value):
        return lax.all_gather(value, "shard", axis=0, tiled=True)

    def scatter_shard(value):
        return lax.psum_scatter(value, "shard", scatter_dimension=0, tiled=True)

    small = jnp.concatenate(
        [attn_router, ffn_router, attn_gain[:, None], ffn_gain[:, None], attn_bias[:, None], ffn_bias[:, None]], axis=1
    )
    small_width = small.shape[1]
    route_width = tokens * TOPK // (n_e * small_rows)
    small = jnp.pad(small, ((0, 0), (0, 128 - small_width)))
    packed = jnp.concatenate(
        [
            w_key.reshape(small_rows, n_e, group).transpose(1, 0, 2),
            w_value.reshape(small_rows, n_e, group).transpose(1, 0, 2),
            jnp.broadcast_to(small[None], (n_e,) + small.shape),
        ],
        axis=2,
    )
    packed = shuffle(packed, "expert")
    route_at = 2 * group + small_width
    packed = packed.at[:, :, route_at:route_at + route_width].set(
        ffn_routes[0].astype(BF).reshape(n_e, small_rows, route_width)
    )
    packed = gather_shard(packed[None])
    routes_f = packed[:, :, :, route_at:route_at + route_width].reshape(n_s * tokens, TOPK).astype(jnp.int32)
    packed = packed.transpose(1, 0, 2, 3).reshape(width, -1)
    key_value_w = packed[:, :2 * group]
    small = packed[:, 2 * group:2 * group + small_width].astype(F32)
    router_a, router_f = small[:, :n_e], small[:, n_e:2 * n_e]
    gain_a, gain_f, bias_a, bias_f = (small[:, 2 * n_e + i] for i in range(4))

    def to_heads(value):
        rows = value.shape[0]
        value = shuffle(value.reshape(rows, n_e, group).transpose(1, 0, 2), "expert")
        return value.transpose(1, 0, 2).reshape(rows, n_e * group)

    def from_heads(value):
        rows = value.shape[0]
        value = trade(value.reshape(rows, n_e, group).transpose(1, 0, 2))
        return value.transpose(1, 0, 2).reshape(rows, n_e * group)

    notes = jnp.concatenate([blocks[0][:, None], attn_routes[0]], axis=1).astype(BF)
    carried = jnp.concatenate([inputs[0], jnp.pad(notes, ((0, 0), (0, 128 - 1 - TOPK)))], axis=1)
    carried, down_w = lax.optimization_barrier((spread(carried), w_down[0]))
    query_w = gather_shard(to_heads(w_query[0]))

    hidden_units = w_down.shape[1]
    turned = jnp.stack([w_gate[0].T.reshape(n_s, hidden_units, -1), w_up[0].T.reshape(n_s, hidden_units, -1)], axis=1)
    down_w = fetch(down_w)
    turned, query_w = lax.optimization_barrier((turned, query_w))
    turned = shuffle(turned, "shard").reshape(n_s, 2 * hidden_units, -1)
    gate_up_own = turned.transpose(1, 0, 2).reshape(2 * hidden_units, width)

    own = inputs[0].astype(F32)
    cot = cotangent[0]
    seq_in = carried[:, :width].astype(F32)
    notes = carried[:, width:width + 1 + TOPK].astype(jnp.int32)
    seq_blocks, routes_a = notes[:, 0], notes[:, 1:]
    position = jnp.concatenate([(me ^ k) * tokens + jnp.arange(tokens, dtype=jnp.int32) for k in range(n_e)]).astype(F32)
    cosine, sine = rope_tables(position)
    h_attn = (seq_in * inverse_rms(seq_in) * gain_a).astype(BF)
    logits_a = dot(h_attn, router_a.astype(BF))
    gates_a = pair_softmax(pick(logits_a, routes_a, ids))
    key_value = dot(h_attn, key_value_w)
    key_value, out_w = lax.optimization_barrier((key_value, w_out[0]))
    out_rows = out_w.shape[0]
    turned = shuffle(out_w.T, "shard").reshape(n_s, width // n_s, out_rows).transpose(1, 0, 2)
    turned = to_heads(turned.reshape(width // n_s, n_s * out_rows))
    turned, *down_w = lax.optimization_barrier((turned, *down_w))
    down_w = fetch_rest(down_w)
    out_wt = gather_shard(turned)
    gate_pair = jnp.concatenate(gates_a, axis=1)
    row_blocks, key_blocks = seq_blocks.reshape(1, -1), seq_blocks.reshape(-1, 1)
    query_raw = dot(h_attn, query_w)
    queries, keys, values, mixed, log_total, mixed_all = attend(
        query_raw, key_value, routes_a, gate_pair, cosine, sine, row_blocks, key_blocks
    )
    mixed_out, *down_w = lax.optimization_barrier((mixed_all, *down_w))
    middle = own + collect(dot_nt(mixed_out, out_wt).astype(BF)) + bias_a

    inv_f = inverse_rms(middle)
    h_ffn = (middle * inv_f * gain_f).astype(BF)
    h_ffn, gate_up_own = lax.optimization_barrier((h_ffn, gate_up_own))
    gate_up_w = fetch(gate_up_own)
    h_all = gather_shard(h_ffn)
    cot_all = gather_shard(after(cot, h_ffn))
    logits_f = dot(h_all, router_f.astype(BF))
    gates_f = pair_softmax(pick(logits_f, routes_f, ids))
    routes_blocks = routes_f.reshape(n_s, tokens, TOPK)
    h_blocks = h_all.reshape(n_s, tokens, width)
    triangle = (jnp.arange(tokens)[:, None] <= jnp.arange(tokens)[None, :]).astype(BF)

    def rows_of(select, source):
        return lax.dot_general(
            select, source, (((2,), (1,)), ((0,), (0,))), preferred_element_type=F32
        ).astype(BF).reshape(n_s * capacity, width)

    selects, hiddens, back_rows_f = [], [], []
    grad_gate_f = [0.0] * TOPK
    grad_pieces = []
    all_rows = []
    for k in range(n_e):
        expert = me ^ k
        named = [routes_blocks[:, :, j] == expert for j in range(TOPK)]
        any_named = named[0] | named[1]
        rank = dot(any_named.astype(BF), triangle).astype(jnp.int32) - 1
        hit = (rank[:, None, :] == jnp.arange(capacity, dtype=jnp.int32)[None, :, None]) & any_named[:, None, :]
        gate_token = sum(jnp.where(named[j], gates_f[j].reshape(n_s, tokens), 0.0) for j in range(TOPK))
        gate_slot = jnp.sum(jnp.where(hit, gate_token[:, None, :], 0.0), axis=2).reshape(1, -1)
        all_rows.append((named, hit, gate_slot, rows_of(hit.astype(BF), h_blocks)))
    cot_all, all_rows, gate_up_w = lax.optimization_barrier((cot_all, all_rows, gate_up_w))
    cot_blocks = cot_all.reshape(n_s, tokens, width)
    gate_up_w = fetch_rest(gate_up_w)
    for k in range(n_e):
        named, hit, gate_slot, rows = all_rows[k]
        select = hit.astype(BF)
        cot_rows = rows_of(select, cot_blocks)
        if k == 2 and n_e == 4:
            cot_rows, gate_up_w[3] = lax.optimization_barrier((cot_rows, gate_up_w[3]))
        hidden, grad_pre, back, grad_slot = expert_pass(rows, cot_rows, gate_slot, gate_up_w[k], down_w[k])
        grad_slot = grad_slot.reshape(n_s, capacity)
        selects.append(select)
        back_rows_f.append(back.reshape(n_s, capacity, width))
        hiddens.append(hidden)
        grad_token = jnp.sum(jnp.where(hit, grad_slot[:, :, None], 0.0), axis=1)
        grad_gate_f = [grad_gate_f[j] + jnp.where(named[j], grad_token, 0.0) for j in range(TOPK)]
        grad_pieces.append((rows, cot_rows, grad_pre))
    select = jnp.concatenate(selects, axis=1)

    def tokens_of(row_list):
        return lax.dot_general(
            select, jnp.concatenate(row_list, axis=1), (((1,), (1,)), ((0,), (0,))), preferred_element_type=F32
        ).astype(BF).reshape(n_s * tokens, width)

    back_sum = tokens_of(back_rows_f)
    back_f = scatter_shard(back_sum)

    def gate_up_grads(k, *others):
        rows, _, grad_pre = grad_pieces[k]
        rows = after(rows, *others)
        return [dot(v, rows).astype(BF) for v in jnp.split(grad_pre, 2, axis=0)]

    grad_gate_up = [None] * n_e
    grad_gate_up[n_e - 1] = gate_up_grads(n_e - 1, back_sum)
    halves = deliver_first(grad_gate_up[n_e - 1])
    out_rows_f = []
    for k in range(n_e):
        hidden = after(hiddens[k], *(grad_gate_up[n_e - 1] if k < n_e - 1 else halves))
        out_rows_f.append(dot_tn(hidden, down_w[k]).astype(BF).reshape(n_s, capacity, width))
    out_sum = tokens_of(out_rows_f)
    ffn_out = scatter_shard(out_sum)
    back_f, out_sum = lax.optimization_barrier((back_f, out_sum))
    back_f = back_f.astype(F32)
    grad_gates_f = jnp.sum(
        shuffle(jnp.stack(grad_gate_f, axis=1).reshape(n_s, TOPK * tokens), "shard"), axis=0
    ).reshape(TOPK, tokens, 1)


    grad_out = cot.astype(F32)
    own_routes_f = ffn_routes[0]
    own_gates_f = pair_softmax(pick(dot(h_ffn, router_f.astype(BF)), own_routes_f, ids))

    def logit_grads(gates, grads, routes):
        centre = sum(gates[j] * grads[j] for j in range(TOPK))
        return place([gates[j] * (grads[j] - centre) for j in range(TOPK)], routes, ids)

    grad_logits_f = logit_grads(own_gates_f, grad_gates_f, own_routes_f)
    grad_router_f = dot_tn(h_ffn.astype(F32), grad_logits_f, PRECISE)
    grad_h_ffn = back_f + jnp.dot(grad_logits_f, router_f.T, precision=PRECISE)
    grad_norm, grad_gain_f = norm_back(grad_h_ffn, middle, inv_f, gain_f)
    grad_middle = grad_out + grad_norm
    grad_bias_f = jnp.sum(grad_out, axis=0)
    grad_bias_a = jnp.sum(grad_middle, axis=0)

    grad_middle_low = grad_middle.astype(BF)
    for k in range(n_e - 1):
        grad_gate_up[k] = gate_up_grads(k, back_f)
    seq_grad = spread(grad_middle_low)
    seq_grad, grad_gate_up = lax.optimization_barrier((seq_grad, grad_gate_up))
    near = deliver_near(grad_gate_up)
    last = deliver_last(grad_gate_up, halves)
    grad_mixed = dot(seq_grad, out_wt)
    grad_out_wt = dot_tn(seq_grad, mixed_all).astype(BF)
    grad_mixed, grad_out_wt = lax.optimization_barrier((grad_mixed, grad_out_wt))
    grad_query_all, grad_key_value, gate_notes = attend_back(
        grad_mixed, routes_a, gate_pair, queries, keys, values, mixed, log_total, cosine, sine, row_blocks, key_blocks
    )
    grad_query_all, *near = lax.optimization_barrier((grad_query_all, *near))
    key_value_grad, query_grad = dot_tn(h_attn, grad_key_value).astype(BF), dot_tn(h_attn, grad_query_all).astype(BF)
    grad_query_all, key_value_grad, query_grad = lax.optimization_barrier((grad_query_all, key_value_grad, query_grad))
    back_a = (dot_nt(grad_query_all, query_w) + dot_nt(grad_key_value, key_value_w)).astype(BF)
    back_a = jnp.concatenate([back_a, gate_notes], axis=1)
    back_a, ffn_out, *last = lax.optimization_barrier((back_a, ffn_out, *last))
    gate_up_total = [v.astype(BF) for v in total(grad_gate_up[0], near, last)]
    outputs = (middle + ffn_out.astype(F32) + bias_f).astype(BF)[None]
    value = scatter_shard(grad_out_wt)
    key_value_grad = key_value_grad.reshape(n_e, n_s, small_rows, 2 * group).transpose(1, 0, 2, 3)
    key_value_grad = scatter_shard(key_value_grad.reshape(n_s * n_e * small_rows, 2 * group))
    query_grad = scatter_shard(query_grad)
    value = from_heads(value).reshape(width // n_s, n_s, out_rows).transpose(1, 0, 2)

    def to_rows(value):
        value = shuffle(value.reshape(hidden_units, n_s, width // n_s).transpose(1, 0, 2), "shard")
        return value.reshape(n_s * hidden_units, width // n_s)

    grad_out_w = shuffle(value, "shard").reshape(width, out_rows)
    grad_out_w, gate_total = lax.optimization_barrier((grad_out_w, gate_up_total[0]))
    grad_out_w = grad_out_w.T.astype(F32)[None]
    gate_turned = to_rows(gate_total)
    grad_down = []
    for k in range(n_e):
        hidden = after(hiddens[k], back_a)
        grad_down.append([dot(v, grad_pieces[k][1]).astype(BF) for v in jnp.split(hidden, 2, axis=0)])
    halves = deliver_first(grad_down[n_e - 1])
    back_a = collect(back_a)
    near, last = deliver_near(grad_down), deliver_last(grad_down, halves)
    back_a, gate_turned, *near = lax.optimization_barrier((back_a, gate_turned, *near))
    up_total, key_value_grad = lax.optimization_barrier((after(gate_up_total[1], gate_turned), key_value_grad))
    up_turned = to_rows(up_total)
    grad_down_w = jnp.concatenate(total(grad_down[0], near, last), axis=0)[None]
    key_value_grad = trade(key_value_grad.reshape(n_e, small_rows, -1))
    grad_key_w = key_value_grad[:, :, :group].transpose(1, 0, 2).reshape(small_rows, -1).astype(F32)
    grad_value_w = key_value_grad[:, :, group:].transpose(1, 0, 2).reshape(small_rows, -1).astype(F32)
    gate_grads = back_a[:, width:width + TOPK] + back_a[:, width + TOPK:width + 2 * TOPK]
    grad_gates_a = [gate_grads[:, j:j + 1] for j in range(TOPK)]
    back_a = back_a[:, :width]
    grad_query_w = from_heads(query_grad)
    grad_gate_w = gate_turned.T.astype(F32)[None]

    h_own = h_attn[:tokens]
    own_routes_a = attn_routes[0]
    own_gates_a = [v[:tokens] for v in gates_a]
    grad_logits_a = logit_grads(own_gates_a, grad_gates_a, own_routes_a)
    grad_router_a = dot_tn(h_own.astype(F32), grad_logits_a, PRECISE)
    grad_h_attn = back_a + jnp.dot(grad_logits_a, router_a.T, precision=PRECISE)
    grad_norm, grad_gain_a = norm_back(grad_h_attn, own, inverse_rms(own), gain_a)
    input_grad = (grad_middle + grad_norm).astype(BF)[None]

    shared = jnp.concatenate(
        [grad_router_a, grad_router_f]
        + [v[:, None] for v in (grad_gain_a, grad_gain_f, grad_bias_a, grad_bias_f)],
        axis=1,
    )
    shared, up_turned, grad_query_w = lax.optimization_barrier((shared, up_turned, grad_query_w))
    grad_query_w = grad_query_w.astype(F32)[None]
    grad_up_w = up_turned.T.astype(F32)[None]
    shared = shuffle(shared.reshape(n_e * n_s, -1), ("expert", "shard"))
    shared = jnp.sum(shared, axis=0).reshape(small_rows, small_width)
    return (
        outputs,
        input_grad,
        grad_key_w,
        grad_value_w,
        shared[:, :n_e],
        shared[:, n_e:2 * n_e],
        shared[:, 2 * n_e],
        shared[:, 2 * n_e + 1],
        shared[:, 2 * n_e + 2],
        shared[:, 2 * n_e + 3],
        grad_query_w,
        grad_out_w,
        grad_gate_w,
        grad_up_w,
        grad_down_w,
    )


def solution(mesh):
    rows = P("shard", "expert", None)
    shared, vector = P(("expert", "shard"), None), P(("expert", "shard"))
    weight = P("expert", "shard", None)
    in_specs = (rows, rows, P("shard", "expert"), rows, rows) + (shared,) * 4 + (vector,) * 4 + (weight,) * 5
    out_specs = (rows, rows) + (shared,) * 4 + (vector,) * 4 + (weight,) * 5
    return jax.shard_map(local, mesh=mesh, in_specs=in_specs, out_specs=out_specs, check_vma=False)
```

```python
import functools
import math

import jax
import jax.numpy as jnp
from jax import lax
from jax.experimental import pallas as pl
from jax.experimental.pallas import tpu as pltpu
from jax.sharding import PartitionSpec as P

HD = 128
TOPK = 2
EPSILON = 1e-06
NEGATIVE = -1e30
ROPE_BASE = 10000.0
PRECISE = lax.Precision.HIGHEST
BF = jnp.bfloat16
F32 = jnp.float32
LOG2E = 1.4426950408889634


def dot(a, b):
    return jnp.dot(a, b, preferred_element_type=F32)


def dot_tn(a, b, precision=None):
    return lax.dot_general(a, b, (((0,), (0,)), ((), ())), precision=precision, preferred_element_type=F32)


def dot_nt(a, b):
    return lax.dot_general(a, b, (((1,), (1,)), ((), ())), preferred_element_type=F32)


def inverse_rms(values):
    return lax.rsqrt(jnp.mean(values * values, axis=-1, keepdims=True) + EPSILON)


def norm_back(grad, values, inv, gain):
    u = grad * gain
    centre = jnp.mean(u * values, axis=-1, keepdims=True)
    return inv * (u - values * (inv * inv) * centre), jnp.sum(grad * values * inv, axis=0)


def rope_tables(position):
    half = HD // 2
    frequency = jnp.exp(-math.log(ROPE_BASE) * jnp.arange(half, dtype=F32) / half)
    angles = position[:, None] * frequency
    cosine, sine = jnp.cos(angles), jnp.sin(angles)
    return jnp.concatenate([cosine, cosine], -1), jnp.concatenate([-sine, sine], -1)


def turn(tile, cosine, sine):
    return tile * cosine + pltpu.roll(tile, HD // 2, 1) * sine


def chosen(ref, route, n_e, width, at):
    parts = [jnp.where(route == e, ref[:, e * width + at:e * width + at + HD], 0.0) for e in range(n_e)]
    return functools.reduce(lambda a, b: a + b, parts)


def attend_kernel(
    n_e, scale, q_ref, kv_ref, route_ref, gate_ref, cos_ref, sin_ref, qb_ref, kb_ref,
    query_ref, key_ref, value_ref, o_ref, l_ref, mixed_ref,
):
    width = key_ref.shape[1]
    tile = q_ref.shape[0]
    step = pl.program_id(0)

    @pl.when(step == 0)
    def _():
        for at in range(0, width, HD):
            key_ref[:, at:at + HD] = turn(kv_ref[:, at:at + HD], cos_ref[...], sin_ref[...]).astype(BF)
        value_ref[...] = kv_ref[:, width:].astype(BF)

    here = pl.ds(pl.multiple_of(step * tile, tile), tile)
    cosine, sine = cos_ref[here, :], sin_ref[here, :]
    routes = [route_ref[:, j:j + 1] for j in range(TOPK)]
    gates = [gate_ref[:, j:j + 1] for j in range(TOPK)]
    allowed = kb_ref[...] <= jnp.concatenate([qb_ref[...]] * TOPK, axis=1)
    for head in range(width // HD):
        at = head * HD
        q = [turn(chosen(q_ref, routes[j], n_e, width, at), cosine, sine).astype(BF) for j in range(TOPK)]
        for j in range(TOPK):
            query_ref[j, :, at:at + HD] = q[j]
        s = dot_nt(key_ref[:, at:at + HD], jnp.concatenate(q, axis=0))
        s = jnp.where(allowed, s * (scale * LOG2E), NEGATIVE)
        peak = jnp.max(s, axis=0, keepdims=True)
        p = jnp.exp2(s - peak)
        total = jnp.sum(p, axis=0, keepdims=True)
        o = (dot_tn(value_ref[:, at:at + HD], p.astype(BF)) / total).T.astype(BF)
        l_ref[0, head:head + 1, :] = peak + jnp.log2(total)
        o = [o[j * tile:(j + 1) * tile] for j in range(TOPK)]
        for j in range(TOPK):
            o_ref[j, :, at:at + HD] = o[j]
        o = [gates[j] * o[j].astype(F32) for j in range(TOPK)]
        for e in range(n_e):
            parts = [jnp.where(routes[j] == e, o[j], 0.0) for j in range(TOPK)]
            mixed_ref[:, e * width + at:e * width + at + HD] = (parts[0] + parts[1]).astype(BF)


def attend(q_raw, kv_raw, routes, gates, cosine, sine, q_blocks, k_blocks):
    length, wide = q_raw.shape
    width = kv_raw.shape[1] // 2
    n_e, heads = wide // width, width // HD
    tile = 256
    whole = lambda *shape: pl.BlockSpec(shape, lambda i: (0,) * len(shape))
    tiled = lambda cols: pl.BlockSpec((tile, cols), lambda i: (i, 0))
    pair = pl.BlockSpec((TOPK, tile, width), lambda i: (0, i, 0))
    return pl.pallas_call(
        functools.partial(attend_kernel, n_e, HD ** -0.5),
        grid=(length // tile,),
        in_specs=[
            tiled(wide), whole(length, 2 * width), tiled(TOPK), tiled(TOPK), whole(length, HD), whole(length, HD),
            pl.BlockSpec((1, tile), lambda i: (0, i)), whole(length, 1),
        ],
        out_specs=[
            pair, whole(length, width), whole(length, width), pair,
            pl.BlockSpec((1, heads, TOPK * tile), lambda i: (i, 0, 0)), tiled(wide),
        ],
        out_shape=[
            jax.ShapeDtypeStruct((TOPK, length, width), BF),
            jax.ShapeDtypeStruct((length, width), BF),
            jax.ShapeDtypeStruct((length, width), BF),
            jax.ShapeDtypeStruct((TOPK, length, width), BF),
            jax.ShapeDtypeStruct((length // tile, heads, TOPK * tile), F32),
            jax.ShapeDtypeStruct((length, wide), BF),
        ],
        cost_estimate=pl.CostEstimate(flops=length * length, transcendentals=0, bytes_accessed=8 * length * width),
        name="attend",
    )(q_raw, kv_raw, routes, gates, cosine, sine, q_blocks, k_blocks)


def attend_back_kernel(
    n_e, scale, g_ref, route_ref, gate_ref, query_ref, key_ref, value_ref, o_ref, l_ref, cos_ref, sin_ref, qb_ref,
    kb_ref, dq_ref, dkv_ref, note_ref, dk_ref, dv_ref,
):
    width = key_ref.shape[1]
    tile = g_ref.shape[0]
    step = pl.program_id(0)

    @pl.when(step == 0)
    def _():
        dk_ref[...] = jnp.zeros_like(dk_ref)
        dv_ref[...] = jnp.zeros_like(dv_ref)

    here = pl.ds(pl.multiple_of(step * tile, tile), tile)
    cosine, sine = cos_ref[here, :], sin_ref[here, :]
    routes = [route_ref[:, j:j + 1] for j in range(TOPK)]
    gates = [gate_ref[:, j:j + 1] for j in range(TOPK)]
    allowed = kb_ref[...] <= jnp.concatenate([qb_ref[...]] * TOPK, axis=1)
    gate_grads = [jnp.zeros((tile, 1), F32) for _ in range(TOPK)]
    for head in range(width // HD):
        at = head * HD
        k, v = key_ref[:, at:at + HD], value_ref[:, at:at + HD]
        g = [chosen(g_ref, routes[j], n_e, width, at) for j in range(TOPK)]
        o = [o_ref[j, :, at:at + HD].astype(F32) for j in range(TOPK)]
        gate_grads = [gate_grads[j] + jnp.sum(g[j] * o[j], axis=1, keepdims=True) for j in range(TOPK)]
        d = jnp.concatenate([(gates[j] * g[j]).astype(BF) for j in range(TOPK)], axis=0)
        q = jnp.concatenate([query_ref[j, :, at:at + HD] for j in range(TOPK)], axis=0)
        centre = jnp.sum((d.astype(F32) * jnp.concatenate(o, axis=0)).T, axis=0, keepdims=True)
        s = dot_nt(k, q)
        p = jnp.where(allowed, jnp.exp2(s * (scale * LOG2E) - l_ref[0, head:head + 1, :]), 0.0)
        grad_s = (p * (dot_nt(v, d) - centre)).astype(BF)
        dq = (dot_tn(k, grad_s) * scale).T
        dq = [turn(dq[j * tile:(j + 1) * tile], cosine, -sine) for j in range(TOPK)]
        for e in range(n_e):
            parts = [jnp.where(routes[j] == e, dq[j], 0.0) for j in range(TOPK)]
            dq_ref[:, e * width + at:e * width + at + HD] = (parts[0] + parts[1]).astype(BF)
        dk_ref[:, at:at + HD] += dot(grad_s, q) * scale
        dv_ref[:, at:at + HD] += dot(p.astype(BF), d)
    lane = lax.broadcasted_iota(jnp.int32, (tile, HD), 1)
    note = jnp.zeros((tile, HD), F32)
    for j in range(TOPK):
        high = gate_grads[j].astype(BF).astype(F32)
        note = jnp.where(lane == j, high, note)
        note = jnp.where(lane == TOPK + j, gate_grads[j] - high, note)
    note_ref[...] = note.astype(BF)

    @pl.when(step == pl.num_programs(0) - 1)
    def _():
        for at in range(0, width, HD):
            dkv_ref[:, at:at + HD] = turn(dk_ref[:, at:at + HD], cos_ref[...], -sin_ref[...]).astype(BF)
        dkv_ref[:, width:] = dv_ref[...].astype(BF)


def attend_back(g_raw, routes, gates, queries, keys, values, mixed, log_total, cosine, sine, q_blocks, k_blocks):
    length, wide = g_raw.shape
    width = keys.shape[1]
    n_e, heads = wide // width, width // HD
    tile = 256
    whole = lambda *shape: pl.BlockSpec(shape, lambda i: (0,) * len(shape))
    tiled = lambda cols: pl.BlockSpec((tile, cols), lambda i: (i, 0))
    pair = pl.BlockSpec((TOPK, tile, width), lambda i: (0, i, 0))
    return pl.pallas_call(
        functools.partial(attend_back_kernel, n_e, HD ** -0.5),
        grid=(length // tile,),
        in_specs=[
            tiled(wide), tiled(TOPK), tiled(TOPK), pair, whole(length, width), whole(length, width), pair,
            pl.BlockSpec((1, heads, TOPK * tile), lambda i: (i, 0, 0)), whole(length, HD), whole(length, HD),
            pl.BlockSpec((1, tile), lambda i: (0, i)), whole(length, 1),
        ],
        out_specs=[tiled(wide), whole(length, 2 * width), tiled(HD)],
        out_shape=[
            jax.ShapeDtypeStruct((length, wide), BF),
            jax.ShapeDtypeStruct((length, 2 * width), BF),
            jax.ShapeDtypeStruct((length, HD), BF),
        ],
        scratch_shapes=[pltpu.VMEM((length, width), F32), pltpu.VMEM((length, width), F32)],
        cost_estimate=pl.CostEstimate(flops=length * length, transcendentals=0, bytes_accessed=8 * length * width),
        name="attend_back",
    )(g_raw, routes, gates, queries, keys, values, mixed, log_total, cosine, sine, q_blocks, k_blocks)


def expert_kernel(ready, cot_ref, slot_gate_ref, gate_w_ref, up_w_ref, down_ref, *refs):
    half = down_ref.shape[0]
    if ready:
        gate_pre, up_pre = refs[0][...], refs[1][...]
        hidden_ref, grad_ref, back_ref, slot_ref = refs[2:]
    else:
        rows = refs[0][...]
        gate_pre, up_pre = dot_nt(gate_w_ref[...], rows), dot_nt(up_w_ref[...], rows)
        hidden_ref, grad_ref, back_ref, slot_ref = refs[1:]
    grad_hidden = dot_nt(down_ref[...], cot_ref[...])
    sigma = 1.0 / (1.0 + jnp.exp(-gate_pre))
    silu = gate_pre * sigma
    hidden = silu * up_pre
    slot_ref[...] = jnp.sum(grad_hidden * hidden, axis=0, keepdims=True)
    gate = slot_gate_ref[...]
    grad_hidden = grad_hidden * gate
    hidden_ref[...] = (hidden * gate).astype(BF)
    grad_ref[:half] = (grad_hidden * up_pre * sigma * (1.0 + gate_pre * (1.0 - sigma))).astype(BF)
    grad_ref[half:] = (grad_hidden * silu).astype(BF)
    back_ref[...] = (dot_tn(grad_ref[:half], gate_w_ref[...]) + dot_tn(grad_ref[half:], up_w_ref[...])).astype(BF)


def expert_pass(cot_rows, gates, weights, down, sources):
    count, width = cot_rows.shape
    half = down.shape[0]
    tile = 256
    kept = lambda shape: pl.BlockSpec(shape, lambda i: (0, 0), pipeline_mode=pl.Buffered(1))
    tiled = pl.BlockSpec((tile, width), lambda i: (i, 0))
    turned = lambda size: pl.BlockSpec((size, tile), lambda i: (0, i))
    ready = len(sources) == 2
    return pl.pallas_call(
        functools.partial(expert_kernel, ready),
        grid=(count // tile,),
        in_specs=[tiled, turned(1)] + [kept(down.shape)] * 3 + ([turned(half)] * 2 if ready else [tiled]),
        out_specs=[turned(half), turned(2 * half), tiled, turned(1)],
        out_shape=[
            jax.ShapeDtypeStruct((half, count), BF),
            jax.ShapeDtypeStruct((2 * half, count), BF),
            jax.ShapeDtypeStruct((count, width), BF),
            jax.ShapeDtypeStruct((1, count), F32),
        ],
        cost_estimate=pl.CostEstimate(
            flops=10 * count * width * half, transcendentals=count * half, bytes_accessed=6 * count * width + 6 * half * width
        ),
        name="expert_pass",
    )(cot_rows, gates, *weights, down, *sources)


def pick(table, routes, ids):
    parts = jnp.split(table, len(ids), axis=1)
    return [sum(jnp.where(routes[:, j:j + 1] == e, part, 0.0) for e, part in zip(ids, parts)) for j in range(TOPK)]


def place(pieces, routes, ids):
    return jnp.concatenate(
        [sum(jnp.where(routes[:, j:j + 1] == e, pieces[j], 0.0) for j in range(TOPK)) for e in ids], axis=1
    )


def pair_softmax(logits):
    peak = jnp.maximum(logits[0], logits[1])
    powers = [jnp.exp(v - peak) for v in logits]
    total = powers[0] + powers[1]
    return [v / total for v in powers]


def local(
    inputs, cotangent, blocks, attn_routes, ffn_routes, w_key, w_value, attn_router, ffn_router, attn_gain, ffn_gain,
    attn_bias, ffn_bias, w_query, w_out, w_gate, w_up, w_down,
):
    n_e, n_s = lax.axis_size("expert"), lax.axis_size("shard")
    me = lax.axis_index("expert")
    tokens, width = inputs.shape[1:]
    ids = list(range(n_e))
    capacity = 5 * tokens * TOPK // (4 * n_e)
    group = w_key.shape[1] // n_e
    length = n_e * tokens
    small_rows = w_key.shape[0]

    def swap(value, k):
        return lax.ppermute(value, "expert", [(i, i ^ k) for i in range(n_e)])

    def after(value, *others):
        return lax.optimization_barrier((value,) + others)[0]

    def spread(value):
        return jnp.concatenate([value] + [swap(value, k) for k in range(1, n_e)], axis=0)

    def fetch(block):
        return [block] + [swap(block, k) for k in range(1, 3 if n_e == 4 else n_e)]

    def fetch_rest(blocks, *others):
        if n_e != 4:
            return blocks
        half = blocks[0].shape[0] // 2
        one, two = after(blocks[1], *others), after(blocks[2], *others)
        return blocks + [jnp.concatenate([swap(one[:half], 2), swap(two[half:], 1)], axis=0)]

    def add_low(a, b):
        return (a.astype(F32) + b.astype(F32)).astype(BF)

    def deliver_first(far):
        return [swap(far[0], 1), swap(far[1], 2)] if n_e == 4 else []

    def deliver_near(parts):
        if n_e != 4:
            return [swap(parts[k][i], k) for i in range(2) for k in range(1, n_e)]
        return [swap(parts[1][0], 1), swap(parts[2][1], 2)]

    def deliver_last(parts, halves):
        if n_e != 4:
            return []
        return [swap(add_low(parts[2][0], halves[0]), 2), swap(add_low(parts[1][1], halves[1]), 1)]

    def total(own, near, last):
        count = len(near) // 2
        return [
            sum(v.astype(F32) for v in [own[i]] + near[i * count:(i + 1) * count] + last[i:i + 1]) for i in range(2)
        ]

    def collect(value):
        parts = jnp.split(value, n_e, axis=0)
        return sum([parts[0].astype(F32)] + [swap(parts[k], k).astype(F32) for k in range(1, n_e)])

    def shuffle(value, axis):
        return lax.all_to_all(value, axis, split_axis=0, concat_axis=0, tiled=True)

    def trade(value):
        out = jnp.zeros_like(value)
        for k in range(n_e):
            piece = lax.dynamic_index_in_dim(value, me ^ k, 0, False)
            out = lax.dynamic_update_index_in_dim(out, swap(piece, k) if k else piece, me ^ k, 0)
        return out

    def gather_shard(value):
        return lax.all_gather(value, "shard", axis=0, tiled=True)

    def scatter_shard(value):
        return lax.psum_scatter(value, "shard", scatter_dimension=0, tiled=True)

    small = jnp.concatenate(
        [attn_router, ffn_router, attn_gain[:, None], ffn_gain[:, None], attn_bias[:, None], ffn_bias[:, None]], axis=1
    )
    small_width = small.shape[1]
    route_width = tokens * TOPK // (n_e * small_rows)
    small = jnp.pad(small, ((0, 0), (0, 128 - small_width)))
    packed = jnp.concatenate(
        [
            w_key.reshape(small_rows, n_e, group).transpose(1, 0, 2),
            w_value.reshape(small_rows, n_e, group).transpose(1, 0, 2),
            jnp.broadcast_to(small[None], (n_e,) + small.shape),
        ],
        axis=2,
    )
    packed = shuffle(packed, "expert")
    route_at = 2 * group + small_width
    packed = packed.at[:, :, route_at:route_at + route_width].set(
        ffn_routes[0].astype(BF).reshape(n_e, small_rows, route_width)
    )
    packed = gather_shard(packed[None])
    routes_f = packed[:, :, :, route_at:route_at + route_width].reshape(n_s * tokens, TOPK).astype(jnp.int32)
    packed = packed.transpose(1, 0, 2, 3).reshape(width, -1)
    key_value_w = packed[:, :2 * group]
    small = packed[:, 2 * group:2 * group + small_width].astype(F32)
    router_a, router_f = small[:, :n_e], small[:, n_e:2 * n_e]
    gain_a, gain_f, bias_a, bias_f = (small[:, 2 * n_e + i] for i in range(4))

    def to_heads(value):
        rows = value.shape[0]
        value = shuffle(value.reshape(rows, n_e, group).transpose(1, 0, 2), "expert")
        return value.transpose(1, 0, 2).reshape(rows, n_e * group)

    def from_heads(value):
        rows = value.shape[0]
        value = trade(value.reshape(rows, n_e, group).transpose(1, 0, 2))
        return value.transpose(1, 0, 2).reshape(rows, n_e * group)

    notes = jnp.concatenate([blocks[0][:, None], attn_routes[0]], axis=1).astype(BF)
    carried = jnp.concatenate([inputs[0], jnp.pad(notes, ((0, 0), (0, 128 - 1 - TOPK)))], axis=1)
    carried, down_w = lax.optimization_barrier((spread(carried), w_down[0]))
    query_w = gather_shard(to_heads(w_query[0]))

    hidden_units = w_down.shape[1]
    turned = jnp.stack([w_gate[0].T.reshape(n_s, hidden_units, -1), w_up[0].T.reshape(n_s, hidden_units, -1)], axis=1)
    down_w = fetch(down_w)
    turned, query_w = lax.optimization_barrier((turned, query_w))
    turned = shuffle(turned, "shard").reshape(n_s, 2 * hidden_units, -1)
    gate_up_own = [
        turned[:, i * hidden_units:(i + 1) * hidden_units].transpose(1, 0, 2).reshape(hidden_units, width) for i in range(2)
    ]

    own = inputs[0].astype(F32)
    cot = cotangent[0]
    seq_in = carried[:, :width].astype(F32)
    notes = carried[:, width:width + 1 + TOPK].astype(jnp.int32)
    seq_blocks, routes_a = notes[:, 0], notes[:, 1:]
    position = jnp.concatenate([(me ^ k) * tokens + jnp.arange(tokens, dtype=jnp.int32) for k in range(n_e)]).astype(F32)
    cosine, sine = rope_tables(position)
    h_attn = (seq_in * inverse_rms(seq_in) * gain_a).astype(BF)
    logits_a = dot(h_attn, router_a.astype(BF))
    gates_a = pair_softmax(pick(logits_a, routes_a, ids))
    key_value = dot(h_attn, key_value_w)
    key_value, out_w = lax.optimization_barrier((key_value, w_out[0]))
    out_rows = out_w.shape[0]
    turned = shuffle(out_w.T, "shard").reshape(n_s, width // n_s, out_rows).transpose(1, 0, 2)
    turned = to_heads(turned.reshape(width // n_s, n_s * out_rows))
    turned, *down_w = lax.optimization_barrier((turned, *down_w))
    down_w = fetch_rest(down_w)
    out_wt = gather_shard(turned)
    gate_pair = jnp.concatenate(gates_a, axis=1)
    row_blocks, key_blocks = seq_blocks.reshape(1, -1), seq_blocks.reshape(-1, 1)
    query_raw = dot(h_attn, query_w)
    queries, keys, values, mixed, log_total, mixed_all = attend(
        query_raw, key_value, routes_a, gate_pair, cosine, sine, row_blocks, key_blocks
    )
    mixed_out, *down_w = lax.optimization_barrier((mixed_all, *down_w))
    middle = own + collect(dot_nt(mixed_out, out_wt).astype(BF)) + bias_a

    inv_f = inverse_rms(middle)
    h_ffn = (middle * inv_f * gain_f).astype(BF)
    h_ffn, gate_up_own = lax.optimization_barrier((h_ffn, gate_up_own))
    gate_w, up_w = fetch(gate_up_own[0]), fetch(gate_up_own[1])
    h_all = gather_shard(h_ffn)
    cot_all = gather_shard(after(cot, h_ffn))
    logits_f = dot(h_all, router_f.astype(BF))
    gates_f = pair_softmax(pick(logits_f, routes_f, ids))
    routes_blocks = routes_f.reshape(n_s, tokens, TOPK)
    h_blocks = h_all.reshape(n_s, tokens, width)
    triangle = (jnp.arange(tokens)[:, None] <= jnp.arange(tokens)[None, :]).astype(BF)

    def rows_of(select, source):
        return lax.dot_general(
            select, source, (((2,), (1,)), ((0,), (0,))), preferred_element_type=F32
        ).astype(BF).reshape(n_s * capacity, width)

    selects, hiddens, back_rows_f = [], [], []
    grad_gate_f = [0.0] * TOPK
    grad_pieces = []
    all_rows = []
    for k in range(n_e):
        expert = me ^ k
        named = [routes_blocks[:, :, j] == expert for j in range(TOPK)]
        any_named = named[0] | named[1]
        rank = dot(any_named.astype(BF), triangle).astype(jnp.int32) - 1
        hit = (rank[:, None, :] == jnp.arange(capacity, dtype=jnp.int32)[None, :, None]) & any_named[:, None, :]
        gate_token = sum(jnp.where(named[j], gates_f[j].reshape(n_s, tokens), 0.0) for j in range(TOPK))
        gate_slot = jnp.sum(jnp.where(hit, gate_token[:, None, :], 0.0), axis=2).reshape(1, -1)
        all_rows.append((named, hit, gate_slot, rows_of(hit.astype(BF), h_blocks)))
    ahead = [[dot_nt(gate_w[k], all_rows[k][3]), dot_nt(up_w[k], all_rows[k][3])] for k in range(2)]
    cot_all, all_rows, gate_w, up_w, ahead = lax.optimization_barrier((cot_all, all_rows, gate_w, up_w, ahead))
    cot_blocks = cot_all.reshape(n_s, tokens, width)
    if n_e == 4:
        gate_w, up_w = gate_w + [swap(gate_w[1], 2)], up_w + [swap(up_w[2], 1)]
    for k in range(n_e):
        named, hit, gate_slot, rows = all_rows[k]
        select = hit.astype(BF)
        cot_rows = rows_of(select, cot_blocks)
        if k == 2 and n_e == 4:
            cot_rows, gate_w[3], up_w[3] = lax.optimization_barrier((cot_rows, gate_w[3], up_w[3]))
        hidden, grad_pre, back, grad_slot = expert_pass(
            cot_rows, gate_slot, (gate_w[k], up_w[k]), down_w[k], ahead[k] if k < len(ahead) else [rows]
        )
        grad_slot = grad_slot.reshape(n_s, capacity)
        selects.append(select)
        back_rows_f.append(back.reshape(n_s, capacity, width))
        hiddens.append(hidden)
        grad_token = jnp.sum(jnp.where(hit, grad_slot[:, :, None], 0.0), axis=1)
        grad_gate_f = [grad_gate_f[j] + jnp.where(named[j], grad_token, 0.0) for j in range(TOPK)]
        grad_pieces.append((rows, cot_rows, grad_pre))
    select = jnp.concatenate(selects, axis=1)

    def tokens_of(row_list):
        return lax.dot_general(
            select, jnp.concatenate(row_list, axis=1), (((1,), (1,)), ((0,), (0,))), preferred_element_type=F32
        ).astype(BF).reshape(n_s * tokens, width)

    back_sum = tokens_of(back_rows_f)
    back_f = scatter_shard(back_sum)

    def gate_up_grads(k, *others):
        rows, _, grad_pre = grad_pieces[k]
        rows = after(rows, *others)
        return [dot(v, rows).astype(BF) for v in jnp.split(grad_pre, 2, axis=0)]

    grad_gate_up = [None] * n_e
    grad_gate_up[n_e - 1] = gate_up_grads(n_e - 1, back_sum)
    halves = deliver_first(grad_gate_up[n_e - 1])
    out_rows_f = []
    for k in range(n_e):
        if k < n_e - 1:
            hidden = after(hiddens[k], *grad_gate_up[n_e - 1])
        else:
            for j in reversed(range(n_e - 1)):
                grad_gate_up[j] = gate_up_grads(j, back_sum)
            hidden, halves, grad_gate_up = lax.optimization_barrier((hiddens[k], halves, grad_gate_up))
        out_rows_f.append(dot_tn(hidden, down_w[k]).astype(BF).reshape(n_s, capacity, width))
    out_sum = tokens_of(out_rows_f)
    ffn_out = scatter_shard(out_sum)
    back_f, out_sum = lax.optimization_barrier((back_f, out_sum))
    back_f = back_f.astype(F32)
    grad_gates_f = jnp.sum(
        shuffle(jnp.stack(grad_gate_f, axis=1).reshape(n_s, TOPK * tokens), "shard"), axis=0
    ).reshape(TOPK, tokens, 1)


    grad_out = cot.astype(F32)
    own_routes_f = ffn_routes[0]
    own_gates_f = pair_softmax(pick(dot(h_ffn, router_f.astype(BF)), own_routes_f, ids))

    def logit_grads(gates, grads, routes):
        centre = sum(gates[j] * grads[j] for j in range(TOPK))
        return place([gates[j] * (grads[j] - centre) for j in range(TOPK)], routes, ids)

    grad_logits_f = logit_grads(own_gates_f, grad_gates_f, own_routes_f)
    grad_router_f = dot_tn(h_ffn.astype(F32), grad_logits_f, PRECISE)
    grad_h_ffn = back_f + jnp.dot(grad_logits_f, router_f.T, precision=PRECISE)
    grad_norm, grad_gain_f = norm_back(grad_h_ffn, middle, inv_f, gain_f)
    grad_middle = grad_out + grad_norm
    grad_bias_f = jnp.sum(grad_out, axis=0)
    grad_bias_a = jnp.sum(grad_middle, axis=0)

    grad_middle_low = grad_middle.astype(BF)
    seq_grad = spread(grad_middle_low)
    seq_grad, grad_gate_up = lax.optimization_barrier((seq_grad, grad_gate_up))
    near = deliver_near(grad_gate_up)
    last = deliver_last(grad_gate_up, halves)
    grad_mixed = dot(seq_grad, out_wt)
    grad_out_wt = dot_tn(seq_grad, mixed_all).astype(BF)
    grad_mixed, grad_out_wt = lax.optimization_barrier((grad_mixed, grad_out_wt))
    grad_query_all, grad_key_value, gate_notes = attend_back(
        grad_mixed, routes_a, gate_pair, queries, keys, values, mixed, log_total, cosine, sine, row_blocks, key_blocks
    )
    key_value_grad, query_grad = dot_tn(h_attn, grad_key_value).astype(BF), dot_tn(h_attn, grad_query_all).astype(BF)
    grad_query_all, key_value_grad, query_grad, *near = lax.optimization_barrier(
        (grad_query_all, key_value_grad, query_grad, *near)
    )
    back_a = (dot_nt(grad_query_all, query_w) + dot_nt(grad_key_value, key_value_w)).astype(BF)
    back_a = jnp.concatenate([back_a, gate_notes], axis=1)
    value = scatter_shard(grad_out_wt)
    back_a, ffn_out, value, *last = lax.optimization_barrier((back_a, ffn_out, value, *last))
    gate_up_total = [v.astype(BF) for v in total(grad_gate_up[0], near, last)]
    outputs = (middle + ffn_out.astype(F32) + bias_f).astype(BF)[None]
    key_value_grad = key_value_grad.reshape(n_e, n_s, small_rows, 2 * group).transpose(1, 0, 2, 3)
    key_value_grad = scatter_shard(key_value_grad.reshape(n_s * n_e * small_rows, 2 * group))
    query_grad = scatter_shard(query_grad)
    out_part = from_heads(value).reshape(width // n_s, n_s, out_rows).transpose(1, 0, 2)

    def to_rows(value):
        value = shuffle(value.reshape(hidden_units, n_s, width // n_s).transpose(1, 0, 2), "shard")
        return value.reshape(n_s * hidden_units, width // n_s)

    gate_turned = to_rows(gate_up_total[0])
    grad_down = []
    for k in range(n_e):
        hidden = after(hiddens[k], back_a)
        grad_down.append([dot(v, grad_pieces[k][1]).astype(BF) for v in jnp.split(hidden, 2, axis=0)])
    halves = deliver_first(grad_down[n_e - 1])
    back_a = collect(back_a)
    near, last = deliver_near(grad_down), deliver_last(grad_down, halves)
    back_a, gate_turned, *near = lax.optimization_barrier((back_a, gate_turned, *near))
    up_total, key_value_grad = lax.optimization_barrier((after(gate_up_total[1], gate_turned), key_value_grad))
    up_turned = to_rows(up_total)
    grad_down_w = jnp.concatenate(total(grad_down[0], near, last), axis=0)[None]
    key_value_grad = trade(key_value_grad.reshape(n_e, small_rows, -1))
    grad_key_w = key_value_grad[:, :, :group].transpose(1, 0, 2).reshape(small_rows, -1).astype(F32)
    grad_value_w = key_value_grad[:, :, group:].transpose(1, 0, 2).reshape(small_rows, -1).astype(F32)
    gate_grads = back_a[:, width:width + TOPK] + back_a[:, width + TOPK:width + 2 * TOPK]
    grad_gates_a = [gate_grads[:, j:j + 1] for j in range(TOPK)]
    back_a = back_a[:, :width]
    grad_query_w = from_heads(query_grad)
    grad_gate_w = gate_turned.T.astype(F32)[None]

    h_own = h_attn[:tokens]
    own_routes_a = attn_routes[0]
    own_gates_a = [v[:tokens] for v in gates_a]
    grad_logits_a = logit_grads(own_gates_a, grad_gates_a, own_routes_a)
    grad_router_a = dot_tn(h_own.astype(F32), grad_logits_a, PRECISE)
    grad_h_attn = back_a + jnp.dot(grad_logits_a, router_a.T, precision=PRECISE)
    grad_norm, grad_gain_a = norm_back(grad_h_attn, own, inverse_rms(own), gain_a)
    input_grad = (grad_middle + grad_norm).astype(BF)[None]

    shared = jnp.concatenate(
        [grad_router_a, grad_router_f]
        + [v[:, None] for v in (grad_gain_a, grad_gain_f, grad_bias_a, grad_bias_f)],
        axis=1,
    )
    shared, up_turned, grad_query_w, value = lax.optimization_barrier((shared, up_turned, grad_query_w, out_part))
    grad_out_w = shuffle(value, "shard").reshape(width, out_rows).T.astype(F32)[None]
    grad_query_w = grad_query_w.astype(F32)[None]
    grad_up_w = up_turned.T.astype(F32)[None]
    shared = shuffle(shared.reshape(n_e * n_s, -1), ("expert", "shard"))
    shared = jnp.sum(shared, axis=0).reshape(small_rows, small_width)
    return (
        outputs,
        input_grad,
        grad_key_w,
        grad_value_w,
        shared[:, :n_e],
        shared[:, n_e:2 * n_e],
        shared[:, 2 * n_e],
        shared[:, 2 * n_e + 1],
        shared[:, 2 * n_e + 2],
        shared[:, 2 * n_e + 3],
        grad_query_w,
        grad_out_w,
        grad_gate_w,
        grad_up_w,
        grad_down_w,
    )


def solution(mesh):
    rows = P("shard", "expert", None)
    shared, vector = P(("expert", "shard"), None), P(("expert", "shard"))
    weight = P("expert", "shard", None)
    in_specs = (rows, rows, P("shard", "expert"), rows, rows) + (shared,) * 4 + (vector,) * 4 + (weight,) * 5
    out_specs = (rows, rows) + (shared,) * 4 + (vector,) * 4 + (weight,) * 5
    return jax.shard_map(local, mesh=mesh, in_specs=in_specs, out_specs=out_specs, check_vma=False)
```

```python
import functools
import math

import jax
import jax.numpy as jnp
from jax import lax
from jax.experimental import pallas as pl
from jax.experimental.pallas import tpu as pltpu
from jax.sharding import PartitionSpec as P

HD = 128
TOPK = 2
EPSILON = 1e-06
NEGATIVE = -1e30
ROPE_BASE = 10000.0
PRECISE = lax.Precision.HIGHEST
BF = jnp.bfloat16
F32 = jnp.float32
LOG2E = 1.4426950408889634


def dot(a, b):
    return jnp.dot(a, b, preferred_element_type=F32)


def dot_tn(a, b, precision=None):
    return lax.dot_general(a, b, (((0,), (0,)), ((), ())), precision=precision, preferred_element_type=F32)


def dot_nt(a, b):
    return lax.dot_general(a, b, (((1,), (1,)), ((), ())), preferred_element_type=F32)


def inverse_rms(values):
    return lax.rsqrt(jnp.mean(values * values, axis=-1, keepdims=True) + EPSILON)


def norm_back(grad, values, inv, gain):
    u = grad * gain
    centre = jnp.mean(u * values, axis=-1, keepdims=True)
    return inv * (u - values * (inv * inv) * centre), jnp.sum(grad * values * inv, axis=0)


def rope_tables(position):
    half = HD // 2
    frequency = jnp.exp(-math.log(ROPE_BASE) * jnp.arange(half, dtype=F32) / half)
    angles = position[:, None] * frequency
    cosine, sine = jnp.cos(angles), jnp.sin(angles)
    return jnp.concatenate([cosine, cosine], -1), jnp.concatenate([-sine, sine], -1)


def turn(tile, cosine, sine):
    return tile * cosine + pltpu.roll(tile, HD // 2, 1) * sine


def chosen(ref, route, n_e, width, at):
    parts = [jnp.where(route == e, ref[:, e * width + at:e * width + at + HD], 0.0) for e in range(n_e)]
    return functools.reduce(lambda a, b: a + b, parts)


def attend_kernel(
    n_e, scale, q_ref, kv_ref, route_ref, gate_ref, cos_ref, sin_ref, qb_ref, kb_ref,
    query_ref, key_ref, value_ref, o_ref, l_ref, mixed_ref,
):
    width = key_ref.shape[1]
    tile = q_ref.shape[0]
    step = pl.program_id(0)

    @pl.when(step == 0)
    def _():
        for at in range(0, width, HD):
            key_ref[:, at:at + HD] = turn(kv_ref[:, at:at + HD], cos_ref[...], sin_ref[...]).astype(BF)
        value_ref[...] = kv_ref[:, width:].astype(BF)

    here = pl.ds(pl.multiple_of(step * tile, tile), tile)
    cosine, sine = cos_ref[here, :], sin_ref[here, :]
    routes = [route_ref[:, j:j + 1] for j in range(TOPK)]
    gates = [gate_ref[:, j:j + 1] for j in range(TOPK)]
    allowed = kb_ref[...] <= jnp.concatenate([qb_ref[...]] * TOPK, axis=1)
    for head in range(width // HD):
        at = head * HD
        q = [turn(chosen(q_ref, routes[j], n_e, width, at), cosine, sine).astype(BF) for j in range(TOPK)]
        for j in range(TOPK):
            query_ref[j, :, at:at + HD] = q[j]
        s = dot_nt(key_ref[:, at:at + HD], jnp.concatenate(q, axis=0))
        s = jnp.where(allowed, s * (scale * LOG2E), NEGATIVE)
        peak = jnp.max(s, axis=0, keepdims=True)
        p = jnp.exp2(s - peak)
        total = jnp.sum(p, axis=0, keepdims=True)
        o = (dot_tn(value_ref[:, at:at + HD], p.astype(BF)) / total).T.astype(BF)
        l_ref[0, head:head + 1, :] = peak + jnp.log2(total)
        o = [o[j * tile:(j + 1) * tile] for j in range(TOPK)]
        for j in range(TOPK):
            o_ref[j, :, at:at + HD] = o[j]
        o = [gates[j] * o[j].astype(F32) for j in range(TOPK)]
        for e in range(n_e):
            parts = [jnp.where(routes[j] == e, o[j], 0.0) for j in range(TOPK)]
            mixed_ref[:, e * width + at:e * width + at + HD] = (parts[0] + parts[1]).astype(BF)


def attend(q_raw, kv_raw, routes, gates, cosine, sine, q_blocks, k_blocks):
    length, wide = q_raw.shape
    width = kv_raw.shape[1] // 2
    n_e, heads = wide // width, width // HD
    tile = 256
    whole = lambda *shape: pl.BlockSpec(shape, lambda i: (0,) * len(shape))
    tiled = lambda cols: pl.BlockSpec((tile, cols), lambda i: (i, 0))
    pair = pl.BlockSpec((TOPK, tile, width), lambda i: (0, i, 0))
    return pl.pallas_call(
        functools.partial(attend_kernel, n_e, HD ** -0.5),
        grid=(length // tile,),
        in_specs=[
            tiled(wide), whole(length, 2 * width), tiled(TOPK), tiled(TOPK), whole(length, HD), whole(length, HD),
            pl.BlockSpec((1, tile), lambda i: (0, i)), whole(length, 1),
        ],
        out_specs=[
            pair, whole(length, width), whole(length, width), pair,
            pl.BlockSpec((1, heads, TOPK * tile), lambda i: (i, 0, 0)), tiled(wide),
        ],
        out_shape=[
            jax.ShapeDtypeStruct((TOPK, length, width), BF),
            jax.ShapeDtypeStruct((length, width), BF),
            jax.ShapeDtypeStruct((length, width), BF),
            jax.ShapeDtypeStruct((TOPK, length, width), BF),
            jax.ShapeDtypeStruct((length // tile, heads, TOPK * tile), F32),
            jax.ShapeDtypeStruct((length, wide), BF),
        ],
        cost_estimate=pl.CostEstimate(flops=length * length, transcendentals=0, bytes_accessed=8 * length * width),
        name="attend",
    )(q_raw, kv_raw, routes, gates, cosine, sine, q_blocks, k_blocks)


def attend_back_kernel(
    n_e, scale, g_ref, route_ref, gate_ref, query_ref, key_ref, value_ref, o_ref, l_ref, cos_ref, sin_ref, qb_ref,
    kb_ref, dq_ref, dkv_ref, note_ref, dk_ref, dv_ref,
):
    width = key_ref.shape[1]
    tile = g_ref.shape[0]
    step = pl.program_id(0)

    @pl.when(step == 0)
    def _():
        dk_ref[...] = jnp.zeros_like(dk_ref)
        dv_ref[...] = jnp.zeros_like(dv_ref)

    here = pl.ds(pl.multiple_of(step * tile, tile), tile)
    cosine, sine = cos_ref[here, :], sin_ref[here, :]
    routes = [route_ref[:, j:j + 1] for j in range(TOPK)]
    gates = [gate_ref[:, j:j + 1] for j in range(TOPK)]
    allowed = kb_ref[...] <= jnp.concatenate([qb_ref[...]] * TOPK, axis=1)
    gate_grads = [jnp.zeros((tile, 1), F32) for _ in range(TOPK)]
    for head in range(width // HD):
        at = head * HD
        k, v = key_ref[:, at:at + HD], value_ref[:, at:at + HD]
        g = [chosen(g_ref, routes[j], n_e, width, at) for j in range(TOPK)]
        o = [o_ref[j, :, at:at + HD].astype(F32) for j in range(TOPK)]
        gate_grads = [gate_grads[j] + jnp.sum(g[j] * o[j], axis=1, keepdims=True) for j in range(TOPK)]
        d = jnp.concatenate([(gates[j] * g[j]).astype(BF) for j in range(TOPK)], axis=0)
        q = jnp.concatenate([query_ref[j, :, at:at + HD] for j in range(TOPK)], axis=0)
        centre = jnp.sum((d.astype(F32) * jnp.concatenate(o, axis=0)).T, axis=0, keepdims=True)
        s = dot_nt(k, q)
        p = jnp.where(allowed, jnp.exp2(s * (scale * LOG2E) - l_ref[0, head:head + 1, :]), 0.0)
        grad_s = (p * (dot_nt(v, d) - centre)).astype(BF)
        dq = (dot_tn(k, grad_s) * scale).T
        dq = [turn(dq[j * tile:(j + 1) * tile], cosine, -sine) for j in range(TOPK)]
        for e in range(n_e):
            parts = [jnp.where(routes[j] == e, dq[j], 0.0) for j in range(TOPK)]
            dq_ref[:, e * width + at:e * width + at + HD] = (parts[0] + parts[1]).astype(BF)
        dk_ref[:, at:at + HD] += dot(grad_s, q) * scale
        dv_ref[:, at:at + HD] += dot(p.astype(BF), d)
    lane = lax.broadcasted_iota(jnp.int32, (tile, HD), 1)
    note = jnp.zeros((tile, HD), F32)
    for j in range(TOPK):
        high = gate_grads[j].astype(BF).astype(F32)
        note = jnp.where(lane == j, high, note)
        note = jnp.where(lane == TOPK + j, gate_grads[j] - high, note)
    note_ref[...] = note.astype(BF)

    @pl.when(step == pl.num_programs(0) - 1)
    def _():
        for at in range(0, width, HD):
            dkv_ref[:, at:at + HD] = turn(dk_ref[:, at:at + HD], cos_ref[...], -sin_ref[...]).astype(BF)
        dkv_ref[:, width:] = dv_ref[...].astype(BF)


def attend_back(g_raw, routes, gates, queries, keys, values, mixed, log_total, cosine, sine, q_blocks, k_blocks):
    length, wide = g_raw.shape
    width = keys.shape[1]
    n_e, heads = wide // width, width // HD
    tile = 256
    whole = lambda *shape: pl.BlockSpec(shape, lambda i: (0,) * len(shape))
    tiled = lambda cols: pl.BlockSpec((tile, cols), lambda i: (i, 0))
    pair = pl.BlockSpec((TOPK, tile, width), lambda i: (0, i, 0))
    return pl.pallas_call(
        functools.partial(attend_back_kernel, n_e, HD ** -0.5),
        grid=(length // tile,),
        in_specs=[
            tiled(wide), tiled(TOPK), tiled(TOPK), pair, whole(length, width), whole(length, width), pair,
            pl.BlockSpec((1, heads, TOPK * tile), lambda i: (i, 0, 0)), whole(length, HD), whole(length, HD),
            pl.BlockSpec((1, tile), lambda i: (0, i)), whole(length, 1),
        ],
        out_specs=[tiled(wide), whole(length, 2 * width), tiled(HD)],
        out_shape=[
            jax.ShapeDtypeStruct((length, wide), BF),
            jax.ShapeDtypeStruct((length, 2 * width), BF),
            jax.ShapeDtypeStruct((length, HD), BF),
        ],
        scratch_shapes=[pltpu.VMEM((length, width), F32), pltpu.VMEM((length, width), F32)],
        cost_estimate=pl.CostEstimate(flops=length * length, transcendentals=0, bytes_accessed=8 * length * width),
        name="attend_back",
    )(g_raw, routes, gates, queries, keys, values, mixed, log_total, cosine, sine, q_blocks, k_blocks)


def expert_kernel(ready, cot_ref, slot_gate_ref, gate_w_ref, up_w_ref, down_ref, *refs):
    half = down_ref.shape[0]
    *refs, wide_ref, sems = refs

    @pl.when(pl.program_id(0) == 0)
    def _():
        copies = [
            pltpu.make_async_copy(ref, wide_ref.at[pl.ds(i * half, half)], sems.at[i])
            for i, ref in enumerate((gate_w_ref, up_w_ref))
        ]
        for copy in copies:
            copy.start()
        for copy in copies:
            copy.wait()

    if ready:
        gate_pre, up_pre = refs[0][...], refs[1][...]
        hidden_ref, grad_ref, back_ref, slot_ref = refs[2:]
    else:
        pre = dot_nt(wide_ref[...], refs[0][...])
        gate_pre, up_pre = pre[:half], pre[half:]
        hidden_ref, grad_ref, back_ref, slot_ref = refs[1:]
    grad_hidden = dot_nt(down_ref[...], cot_ref[...])
    sigma = 1.0 / (1.0 + jnp.exp(-gate_pre))
    silu = gate_pre * sigma
    hidden = silu * up_pre
    slot_ref[...] = jnp.sum(grad_hidden * hidden, axis=0, keepdims=True)
    gate = slot_gate_ref[...]
    grad_hidden = grad_hidden * gate
    hidden_ref[...] = (hidden * gate).astype(BF)
    grad_ref[:half] = (grad_hidden * up_pre * sigma * (1.0 + gate_pre * (1.0 - sigma))).astype(BF)
    grad_ref[half:] = (grad_hidden * silu).astype(BF)
    back_ref[...] = dot_tn(grad_ref[...], wide_ref[...]).astype(BF)


def expert_pass(cot_rows, gates, weights, down, sources):
    count, width = cot_rows.shape
    half = down.shape[0]
    tile = 256
    kept = lambda shape: pl.BlockSpec(shape, lambda i: (0, 0), pipeline_mode=pl.Buffered(1))
    tiled = pl.BlockSpec((tile, width), lambda i: (i, 0))
    turned = lambda size: pl.BlockSpec((size, tile), lambda i: (0, i))
    ready = len(sources) == 2
    return pl.pallas_call(
        functools.partial(expert_kernel, ready),
        grid=(count // tile,),
        in_specs=[tiled, turned(1)] + [pl.BlockSpec(memory_space=pl.ANY)] * 2 + [kept(down.shape)]
        + ([turned(half)] * 2 if ready else [tiled]),
        out_specs=[turned(half), turned(2 * half), tiled, turned(1)],
        out_shape=[
            jax.ShapeDtypeStruct((half, count), BF),
            jax.ShapeDtypeStruct((2 * half, count), BF),
            jax.ShapeDtypeStruct((count, width), BF),
            jax.ShapeDtypeStruct((1, count), F32),
        ],
        scratch_shapes=[pltpu.VMEM((2 * half, width), BF), pltpu.SemaphoreType.DMA((2,))],
        cost_estimate=pl.CostEstimate(
            flops=10 * count * width * half, transcendentals=count * half, bytes_accessed=6 * count * width + 6 * half * width
        ),
        name="expert_pass",
    )(cot_rows, gates, *weights, down, *sources)


def pick(table, routes, ids):
    parts = jnp.split(table, len(ids), axis=1)
    return [sum(jnp.where(routes[:, j:j + 1] == e, part, 0.0) for e, part in zip(ids, parts)) for j in range(TOPK)]


def place(pieces, routes, ids):
    return jnp.concatenate(
        [sum(jnp.where(routes[:, j:j + 1] == e, pieces[j], 0.0) for j in range(TOPK)) for e in ids], axis=1
    )


def pair_softmax(logits):
    peak = jnp.maximum(logits[0], logits[1])
    powers = [jnp.exp(v - peak) for v in logits]
    total = powers[0] + powers[1]
    return [v / total for v in powers]


def local(
    inputs, cotangent, blocks, attn_routes, ffn_routes, w_key, w_value, attn_router, ffn_router, attn_gain, ffn_gain,
    attn_bias, ffn_bias, w_query, w_out, w_gate, w_up, w_down,
):
    n_e, n_s = lax.axis_size("expert"), lax.axis_size("shard")
    me = lax.axis_index("expert")
    tokens, width = inputs.shape[1:]
    ids = list(range(n_e))
    capacity = 5 * tokens * TOPK // (4 * n_e)
    group = w_key.shape[1] // n_e
    length = n_e * tokens
    small_rows = w_key.shape[0]

    def swap(value, k):
        return lax.ppermute(value, "expert", [(i, i ^ k) for i in range(n_e)])

    def after(value, *others):
        return lax.optimization_barrier((value,) + others)[0]

    def spread(value):
        return jnp.concatenate([value] + [swap(value, k) for k in range(1, n_e)], axis=0)

    def fetch(block):
        return [block] + [swap(block, k) for k in range(1, 3 if n_e == 4 else n_e)]

    def fetch_rest(blocks, *others):
        if n_e != 4:
            return blocks
        half = blocks[0].shape[0] // 2
        one, two = after(blocks[1], *others), after(blocks[2], *others)
        return blocks + [jnp.concatenate([swap(one[:half], 2), swap(two[half:], 1)], axis=0)]

    def add_low(a, b):
        return (a.astype(F32) + b.astype(F32)).astype(BF)

    def deliver_first(far):
        return [swap(far[0], 1), swap(far[1], 2)] if n_e == 4 else []

    def deliver_near(parts):
        if n_e != 4:
            return [swap(parts[k][i], k) for i in range(2) for k in range(1, n_e)]
        return [swap(parts[1][0], 1), swap(parts[2][1], 2)]

    def deliver_last(parts, halves):
        if n_e != 4:
            return []
        return [swap(add_low(parts[2][0], halves[0]), 2), swap(add_low(parts[1][1], halves[1]), 1)]

    def total(own, near, last):
        count = len(near) // 2
        return [
            sum(v.astype(F32) for v in [own[i]] + near[i * count:(i + 1) * count] + last[i:i + 1]) for i in range(2)
        ]

    def collect(value):
        parts = jnp.split(value, n_e, axis=0)
        return sum([parts[0].astype(F32)] + [swap(parts[k], k).astype(F32) for k in range(1, n_e)])

    def shuffle(value, axis):
        return lax.all_to_all(value, axis, split_axis=0, concat_axis=0, tiled=True)

    def trade(value):
        out = jnp.zeros_like(value)
        for k in range(n_e):
            piece = lax.dynamic_index_in_dim(value, me ^ k, 0, False)
            out = lax.dynamic_update_index_in_dim(out, swap(piece, k) if k else piece, me ^ k, 0)
        return out

    def gather_shard(value):
        return lax.all_gather(value, "shard", axis=0, tiled=True)

    def scatter_shard(value):
        return lax.psum_scatter(value, "shard", scatter_dimension=0, tiled=True)

    small = jnp.concatenate(
        [attn_router, ffn_router, attn_gain[:, None], ffn_gain[:, None], attn_bias[:, None], ffn_bias[:, None]], axis=1
    )
    small_width = small.shape[1]
    route_width = tokens * TOPK // (n_e * small_rows)
    small = jnp.pad(small, ((0, 0), (0, 128 - small_width)))
    packed = jnp.concatenate(
        [
            w_key.reshape(small_rows, n_e, group).transpose(1, 0, 2),
            w_value.reshape(small_rows, n_e, group).transpose(1, 0, 2),
            jnp.broadcast_to(small[None], (n_e,) + small.shape),
        ],
        axis=2,
    )
    packed = shuffle(packed, "expert")
    route_at = 2 * group + small_width
    packed = packed.at[:, :, route_at:route_at + route_width].set(
        ffn_routes[0].astype(BF).reshape(n_e, small_rows, route_width)
    )
    packed = gather_shard(packed[None])
    routes_f = packed[:, :, :, route_at:route_at + route_width].reshape(n_s * tokens, TOPK).astype(jnp.int32)
    packed = packed.transpose(1, 0, 2, 3).reshape(width, -1)
    key_value_w = packed[:, :2 * group]
    small = packed[:, 2 * group:2 * group + small_width].astype(F32)
    router_a, router_f = small[:, :n_e], small[:, n_e:2 * n_e]
    gain_a, gain_f, bias_a, bias_f = (small[:, 2 * n_e + i] for i in range(4))

    def to_heads(value):
        rows = value.shape[0]
        value = shuffle(value.reshape(rows, n_e, group).transpose(1, 0, 2), "expert")
        return value.transpose(1, 0, 2).reshape(rows, n_e * group)

    def from_heads(value):
        rows = value.shape[0]
        value = trade(value.reshape(rows, n_e, group).transpose(1, 0, 2))
        return value.transpose(1, 0, 2).reshape(rows, n_e * group)

    notes = jnp.concatenate([blocks[0][:, None], attn_routes[0]], axis=1).astype(BF)
    carried = jnp.concatenate([inputs[0], jnp.pad(notes, ((0, 0), (0, 128 - 1 - TOPK)))], axis=1)
    carried, down_w = lax.optimization_barrier((spread(carried), w_down[0]))
    query_w = gather_shard(to_heads(w_query[0]))

    hidden_units = w_down.shape[1]
    turned = jnp.stack([w_gate[0].T.reshape(n_s, hidden_units, -1), w_up[0].T.reshape(n_s, hidden_units, -1)], axis=1)
    down_w = fetch(down_w)
    turned, query_w = lax.optimization_barrier((turned, query_w))
    turned = shuffle(turned, "shard").reshape(n_s, 2 * hidden_units, -1)
    gate_up_own = [
        turned[:, i * hidden_units:(i + 1) * hidden_units].transpose(1, 0, 2).reshape(hidden_units, width) for i in range(2)
    ]

    own = inputs[0].astype(F32)
    cot = cotangent[0]
    seq_in = carried[:, :width].astype(F32)
    notes = carried[:, width:width + 1 + TOPK].astype(jnp.int32)
    seq_blocks, routes_a = notes[:, 0], notes[:, 1:]
    position = jnp.concatenate([(me ^ k) * tokens + jnp.arange(tokens, dtype=jnp.int32) for k in range(n_e)]).astype(F32)
    cosine, sine = rope_tables(position)
    h_attn = (seq_in * inverse_rms(seq_in) * gain_a).astype(BF)
    logits_a = dot(h_attn, router_a.astype(BF))
    gates_a = pair_softmax(pick(logits_a, routes_a, ids))
    key_value = dot(h_attn, key_value_w)
    key_value, out_w = lax.optimization_barrier((key_value, w_out[0]))
    out_rows = out_w.shape[0]
    turned = shuffle(out_w.T, "shard").reshape(n_s, width // n_s, out_rows).transpose(1, 0, 2)
    turned = to_heads(turned.reshape(width // n_s, n_s * out_rows))
    turned, *down_w = lax.optimization_barrier((turned, *down_w))
    down_w = fetch_rest(down_w)
    out_wt = gather_shard(turned)
    gate_pair = jnp.concatenate(gates_a, axis=1)
    row_blocks, key_blocks = seq_blocks.reshape(1, -1), seq_blocks.reshape(-1, 1)
    query_raw = dot(h_attn, query_w)
    queries, keys, values, mixed, log_total, mixed_all = attend(
        query_raw, key_value, routes_a, gate_pair, cosine, sine, row_blocks, key_blocks
    )
    mixed_out, *down_w = lax.optimization_barrier((mixed_all, *down_w))
    middle = own + collect(dot_nt(mixed_out, out_wt).astype(BF)) + bias_a

    inv_f = inverse_rms(middle)
    h_ffn = (middle * inv_f * gain_f).astype(BF)
    h_ffn, gate_up_own = lax.optimization_barrier((h_ffn, gate_up_own))
    gate_w, up_w = fetch(gate_up_own[0]), fetch(gate_up_own[1])
    h_all = gather_shard(h_ffn)
    cot_all = gather_shard(after(cot, h_ffn))
    logits_f = dot(h_all, router_f.astype(BF))
    gates_f = pair_softmax(pick(logits_f, routes_f, ids))
    routes_blocks = routes_f.reshape(n_s, tokens, TOPK)
    h_blocks = h_all.reshape(n_s, tokens, width)
    triangle = (jnp.arange(tokens)[:, None] <= jnp.arange(tokens)[None, :]).astype(BF)

    def rows_of(select, source):
        return lax.dot_general(
            select, source, (((2,), (1,)), ((0,), (0,))), preferred_element_type=F32
        ).astype(BF).reshape(n_s * capacity, width)

    selects, hiddens, back_rows_f = [], [], []
    grad_gate_f = [0.0] * TOPK
    grad_pieces = []
    all_rows = []
    for k in range(n_e):
        expert = me ^ k
        named = [routes_blocks[:, :, j] == expert for j in range(TOPK)]
        any_named = named[0] | named[1]
        rank = dot(any_named.astype(BF), triangle).astype(jnp.int32) - 1
        hit = (rank[:, None, :] == jnp.arange(capacity, dtype=jnp.int32)[None, :, None]) & any_named[:, None, :]
        gate_token = sum(jnp.where(named[j], gates_f[j].reshape(n_s, tokens), 0.0) for j in range(TOPK))
        gate_slot = jnp.sum(jnp.where(hit, gate_token[:, None, :], 0.0), axis=2).reshape(1, -1)
        all_rows.append((named, hit, gate_slot, rows_of(hit.astype(BF), h_blocks)))
    ahead = [[dot_nt(gate_w[k], all_rows[k][3]), dot_nt(up_w[k], all_rows[k][3])] for k in range(2)]
    cot_all, all_rows, gate_w, up_w, ahead = lax.optimization_barrier((cot_all, all_rows, gate_w, up_w, ahead))
    cot_blocks = cot_all.reshape(n_s, tokens, width)
    if n_e == 4:
        gate_w, up_w = gate_w + [swap(gate_w[1], 2)], up_w + [swap(up_w[2], 1)]
    for k in range(n_e):
        named, hit, gate_slot, rows = all_rows[k]
        select = hit.astype(BF)
        cot_rows = rows_of(select, cot_blocks)
        if k == 2 and n_e == 4:
            cot_rows, gate_w[3], up_w[3] = lax.optimization_barrier((cot_rows, gate_w[3], up_w[3]))
        hidden, grad_pre, back, grad_slot = expert_pass(
            cot_rows, gate_slot, (gate_w[k], up_w[k]), down_w[k], ahead[k] if k < len(ahead) else [rows]
        )
        grad_slot = grad_slot.reshape(n_s, capacity)
        selects.append(select)
        back_rows_f.append(back.reshape(n_s, capacity, width))
        hiddens.append(hidden)
        grad_token = jnp.sum(jnp.where(hit, grad_slot[:, :, None], 0.0), axis=1)
        grad_gate_f = [grad_gate_f[j] + jnp.where(named[j], grad_token, 0.0) for j in range(TOPK)]
        grad_pieces.append((rows, cot_rows, grad_pre))
    select = jnp.concatenate(selects, axis=1)

    def tokens_of(row_list):
        return lax.dot_general(
            select, jnp.concatenate(row_list, axis=1), (((1,), (1,)), ((0,), (0,))), preferred_element_type=F32
        ).astype(BF).reshape(n_s * tokens, width)

    back_sum = tokens_of(back_rows_f)
    back_f = scatter_shard(back_sum)

    def gate_up_grads(k, *others):
        rows, _, grad_pre = grad_pieces[k]
        rows = after(rows, *others)
        return [dot(v, rows).astype(BF) for v in jnp.split(grad_pre, 2, axis=0)]

    grad_gate_up = [None] * n_e
    grad_gate_up[n_e - 1] = gate_up_grads(n_e - 1, back_sum)
    halves = deliver_first(grad_gate_up[n_e - 1])
    gate_grads_f = shuffle(jnp.stack(grad_gate_f, axis=1).reshape(n_s, TOPK * tokens), "shard")
    out_rows_f = []
    for k in range(n_e):
        if k < n_e - 1:
            hidden = after(hiddens[k], *grad_gate_up[n_e - 1])
        else:
            for j in reversed(range(n_e - 1)):
                grad_gate_up[j] = gate_up_grads(j, back_sum)
            hidden, halves, grad_gate_up, gate_grads_f = lax.optimization_barrier(
                (hiddens[k], halves, grad_gate_up, gate_grads_f)
            )
        out_rows_f.append(dot_tn(hidden, down_w[k]).astype(BF).reshape(n_s, capacity, width))
    out_sum = tokens_of(out_rows_f)
    ffn_out = scatter_shard(out_sum)
    back_f, out_sum = lax.optimization_barrier((back_f, out_sum))
    back_f = back_f.astype(F32)
    grad_gates_f = jnp.sum(gate_grads_f, axis=0).reshape(TOPK, tokens, 1)

    grad_out = cot.astype(F32)
    own_routes_f = ffn_routes[0]
    own_gates_f = pair_softmax(pick(dot(h_ffn, router_f.astype(BF)), own_routes_f, ids))

    def logit_grads(gates, grads, routes):
        centre = sum(gates[j] * grads[j] for j in range(TOPK))
        return place([gates[j] * (grads[j] - centre) for j in range(TOPK)], routes, ids)

    grad_logits_f = logit_grads(own_gates_f, grad_gates_f, own_routes_f)
    grad_router_f = dot_tn(h_ffn.astype(F32), grad_logits_f, PRECISE)
    grad_h_ffn = back_f + jnp.dot(grad_logits_f, router_f.T, precision=PRECISE)
    grad_norm, grad_gain_f = norm_back(grad_h_ffn, middle, inv_f, gain_f)
    grad_middle = grad_out + grad_norm
    grad_bias_f = jnp.sum(grad_out, axis=0)
    grad_bias_a = jnp.sum(grad_middle, axis=0)

    grad_middle_low = grad_middle.astype(BF)
    seq_grad = spread(grad_middle_low)
    seq_grad, grad_gate_up = lax.optimization_barrier((seq_grad, grad_gate_up))
    near = deliver_near(grad_gate_up)
    last = deliver_last(grad_gate_up, halves)
    grad_mixed = dot(seq_grad, out_wt)
    grad_out_wt = dot_tn(seq_grad, mixed_all).astype(BF)
    grad_mixed, grad_out_wt = lax.optimization_barrier((grad_mixed, grad_out_wt))
    grad_query_all, grad_key_value, gate_notes = attend_back(
        grad_mixed, routes_a, gate_pair, queries, keys, values, mixed, log_total, cosine, sine, row_blocks, key_blocks
    )
    key_value_grad, query_grad = dot_tn(h_attn, grad_key_value).astype(BF), dot_tn(h_attn, grad_query_all).astype(BF)
    grad_query_all, key_value_grad, query_grad, *near = lax.optimization_barrier(
        (grad_query_all, key_value_grad, query_grad, *near)
    )
    back_a = (dot_nt(grad_query_all, query_w) + dot_nt(grad_key_value, key_value_w)).astype(BF)
    back_a = jnp.concatenate([back_a, gate_notes], axis=1)
    value = scatter_shard(grad_out_wt)
    back_a, ffn_out, value, key_value_grad, *last = lax.optimization_barrier(
        (back_a, ffn_out, value, key_value_grad, *last)
    )
    gate_up_total = [v.astype(BF) for v in total(grad_gate_up[0], near, last)]
    outputs = (middle + ffn_out.astype(F32) + bias_f).astype(BF)[None]
    key_value_grad = key_value_grad.reshape(n_e, n_s, small_rows, 2 * group).transpose(1, 0, 2, 3)
    key_value_grad = scatter_shard(key_value_grad.reshape(n_s * n_e * small_rows, 2 * group))
    query_grad = scatter_shard(query_grad)
    out_part = from_heads(value).reshape(width // n_s, n_s, out_rows).transpose(1, 0, 2)

    def to_rows(value):
        value = shuffle(value.reshape(hidden_units, n_s, width // n_s).transpose(1, 0, 2), "shard")
        return value.reshape(n_s * hidden_units, width // n_s)

    gate_turned = to_rows(gate_up_total[0])
    grad_down = []
    for k in range(n_e):
        hidden = after(hiddens[k], back_a)
        grad_down.append([dot(v, grad_pieces[k][1]).astype(BF) for v in jnp.split(hidden, 2, axis=0)])
    halves = deliver_first(grad_down[n_e - 1])
    back_a = collect(back_a)
    near, last = deliver_near(grad_down), deliver_last(grad_down, halves)
    back_a, gate_turned, up_total = lax.optimization_barrier((back_a, gate_turned, gate_up_total[1]))
    up_turned = to_rows(up_total)
    key_value_grad = trade(key_value_grad.reshape(n_e, small_rows, -1))
    gate_grads = back_a[:, width:width + TOPK] + back_a[:, width + TOPK:width + 2 * TOPK]
    grad_gates_a = [gate_grads[:, j:j + 1] for j in range(TOPK)]
    back_a = back_a[:, :width]
    grad_query_w = from_heads(query_grad)
    grad_gate_w = gate_turned.T.astype(F32)[None]

    h_own = h_attn[:tokens]
    own_routes_a = attn_routes[0]
    own_gates_a = [v[:tokens] for v in gates_a]
    grad_logits_a = logit_grads(own_gates_a, grad_gates_a, own_routes_a)
    grad_router_a = dot_tn(h_own.astype(F32), grad_logits_a, PRECISE)
    grad_h_attn = back_a + jnp.dot(grad_logits_a, router_a.T, precision=PRECISE)
    grad_norm, grad_gain_a = norm_back(grad_h_attn, own, inverse_rms(own), gain_a)
    input_grad = (grad_middle + grad_norm).astype(BF)[None]

    shared = jnp.concatenate(
        [grad_router_a, grad_router_f]
        + [v[:, None] for v in (grad_gain_a, grad_gain_f, grad_bias_a, grad_bias_f)],
        axis=1,
    )
    shared, up_turned, grad_query_w, value, key_value_grad, near, last = lax.optimization_barrier(
        (shared, up_turned, grad_query_w, out_part, key_value_grad, near, last)
    )
    grad_down_w = jnp.concatenate(total(grad_down[0], near, last), axis=0)[None]
    grad_key_w = key_value_grad[:, :, :group].transpose(1, 0, 2).reshape(small_rows, -1).astype(F32)
    grad_value_w = key_value_grad[:, :, group:].transpose(1, 0, 2).reshape(small_rows, -1).astype(F32)
    grad_out_w = shuffle(value, "shard").reshape(width, out_rows).T.astype(F32)[None]
    grad_query_w = grad_query_w.astype(F32)[None]
    grad_up_w = up_turned.T.astype(F32)[None]
    shared = shuffle(shared.reshape(n_e * n_s, -1), ("expert", "shard"))
    shared = jnp.sum(shared, axis=0).reshape(small_rows, small_width)
    return (
        outputs,
        input_grad,
        grad_key_w,
        grad_value_w,
        shared[:, :n_e],
        shared[:, n_e:2 * n_e],
        shared[:, 2 * n_e],
        shared[:, 2 * n_e + 1],
        shared[:, 2 * n_e + 2],
        shared[:, 2 * n_e + 3],
        grad_query_w,
        grad_out_w,
        grad_gate_w,
        grad_up_w,
        grad_down_w,
    )


def solution(mesh):
    rows = P("shard", "expert", None)
    shared, vector = P(("expert", "shard"), None), P(("expert", "shard"))
    weight = P("expert", "shard", None)
    in_specs = (rows, rows, P("shard", "expert"), rows, rows) + (shared,) * 4 + (vector,) * 4 + (weight,) * 5
    out_specs = (rows, rows) + (shared,) * 4 + (vector,) * 4 + (weight,) * 5
    return jax.shard_map(local, mesh=mesh, in_specs=in_specs, out_specs=out_specs, check_vma=False)
```

```python
import functools
import math

import jax
import jax.numpy as jnp
from jax import lax
from jax.experimental import pallas as pl
from jax.experimental.pallas import tpu as pltpu
from jax.sharding import PartitionSpec as P

HD = 128
TOPK = 2
EPSILON = 1e-06
NEGATIVE = -1e30
ROPE_BASE = 10000.0
PRECISE = lax.Precision.HIGHEST
BF = jnp.bfloat16
F32 = jnp.float32
LOG2E = 1.4426950408889634


def dot(a, b):
    return jnp.dot(a, b, preferred_element_type=F32)


def dot_tn(a, b, precision=None):
    return lax.dot_general(a, b, (((0,), (0,)), ((), ())), precision=precision, preferred_element_type=F32)


def dot_nt(a, b):
    return lax.dot_general(a, b, (((1,), (1,)), ((), ())), preferred_element_type=F32)


def inverse_rms(values):
    return lax.rsqrt(jnp.mean(values * values, axis=-1, keepdims=True) + EPSILON)


def norm_back(grad, values, inv, gain):
    u = grad * gain
    centre = jnp.mean(u * values, axis=-1, keepdims=True)
    return inv * (u - values * (inv * inv) * centre), jnp.sum(grad * values * inv, axis=0)


def rope_tables(position):
    half = HD // 2
    frequency = jnp.exp(-math.log(ROPE_BASE) * jnp.arange(half, dtype=F32) / half)
    angles = position[:, None] * frequency
    cosine, sine = jnp.cos(angles), jnp.sin(angles)
    return jnp.concatenate([cosine, cosine], -1), jnp.concatenate([-sine, sine], -1)


def turn(tile, cosine, sine):
    return tile * cosine + pltpu.roll(tile, HD // 2, 1) * sine


def chosen(ref, route, n_e, width, at):
    parts = [jnp.where(route == e, ref[:, e * width + at:e * width + at + HD], 0.0) for e in range(n_e)]
    return functools.reduce(lambda a, b: a + b, parts)


def attend_kernel(
    n_e, scale, q_ref, kv_ref, route_ref, gate_ref, cos_ref, sin_ref, qb_ref, kb_ref,
    query_ref, key_ref, value_ref, o_ref, l_ref, mixed_ref,
):
    width = key_ref.shape[1]
    tile = q_ref.shape[0]
    step = pl.program_id(0)

    @pl.when(step == 0)
    def _():
        for at in range(0, width, HD):
            key_ref[:, at:at + HD] = turn(kv_ref[:, at:at + HD], cos_ref[...], sin_ref[...]).astype(BF)
        value_ref[...] = kv_ref[:, width:].astype(BF)

    here = pl.ds(pl.multiple_of(step * tile, tile), tile)
    cosine, sine = cos_ref[here, :], sin_ref[here, :]
    routes = [route_ref[:, j:j + 1] for j in range(TOPK)]
    gates = [gate_ref[:, j:j + 1] for j in range(TOPK)]
    allowed = kb_ref[...] <= jnp.concatenate([qb_ref[...]] * TOPK, axis=1)
    for head in range(width // HD):
        at = head * HD
        q = [turn(chosen(q_ref, routes[j], n_e, width, at), cosine, sine).astype(BF) for j in range(TOPK)]
        for j in range(TOPK):
            query_ref[j, :, at:at + HD] = q[j]
        s = dot_nt(key_ref[:, at:at + HD], jnp.concatenate(q, axis=0))
        s = jnp.where(allowed, s * (scale * LOG2E), NEGATIVE)
        peak = jnp.max(s, axis=0, keepdims=True)
        p = jnp.exp2(s - peak)
        total = jnp.sum(p, axis=0, keepdims=True)
        o = (dot_tn(value_ref[:, at:at + HD], p.astype(BF)) / total).T.astype(BF)
        l_ref[0, head:head + 1, :] = peak + jnp.log2(total)
        o = [o[j * tile:(j + 1) * tile] for j in range(TOPK)]
        for j in range(TOPK):
            o_ref[j, :, at:at + HD] = o[j]
        o = [gates[j] * o[j].astype(F32) for j in range(TOPK)]
        for e in range(n_e):
            parts = [jnp.where(routes[j] == e, o[j], 0.0) for j in range(TOPK)]
            mixed_ref[:, e * width + at:e * width + at + HD] = (parts[0] + parts[1]).astype(BF)


def attend(q_raw, kv_raw, routes, gates, cosine, sine, q_blocks, k_blocks):
    length, wide = q_raw.shape
    width = kv_raw.shape[1] // 2
    n_e, heads = wide // width, width // HD
    tile = 256
    whole = lambda *shape: pl.BlockSpec(shape, lambda i: (0,) * len(shape))
    tiled = lambda cols: pl.BlockSpec((tile, cols), lambda i: (i, 0))
    pair = pl.BlockSpec((TOPK, tile, width), lambda i: (0, i, 0))
    return pl.pallas_call(
        functools.partial(attend_kernel, n_e, HD ** -0.5),
        grid=(length // tile,),
        in_specs=[
            tiled(wide), whole(length, 2 * width), tiled(TOPK), tiled(TOPK), whole(length, HD), whole(length, HD),
            pl.BlockSpec((1, tile), lambda i: (0, i)), whole(length, 1),
        ],
        out_specs=[
            pair, whole(length, width), whole(length, width), pair,
            pl.BlockSpec((1, heads, TOPK * tile), lambda i: (i, 0, 0)), tiled(wide),
        ],
        out_shape=[
            jax.ShapeDtypeStruct((TOPK, length, width), BF),
            jax.ShapeDtypeStruct((length, width), BF),
            jax.ShapeDtypeStruct((length, width), BF),
            jax.ShapeDtypeStruct((TOPK, length, width), BF),
            jax.ShapeDtypeStruct((length // tile, heads, TOPK * tile), F32),
            jax.ShapeDtypeStruct((length, wide), BF),
        ],
        cost_estimate=pl.CostEstimate(flops=length * length, transcendentals=0, bytes_accessed=8 * length * width),
        name="attend",
    )(q_raw, kv_raw, routes, gates, cosine, sine, q_blocks, k_blocks)


def attend_back_kernel(
    n_e, scale, g_ref, route_ref, gate_ref, query_ref, key_ref, value_ref, o_ref, l_ref, cos_ref, sin_ref, qb_ref,
    kb_ref, dq_ref, dkv_ref, note_ref, dk_ref, dv_ref,
):
    width = key_ref.shape[1]
    tile = g_ref.shape[0]
    step = pl.program_id(0)

    @pl.when(step == 0)
    def _():
        dk_ref[...] = jnp.zeros_like(dk_ref)
        dv_ref[...] = jnp.zeros_like(dv_ref)

    here = pl.ds(pl.multiple_of(step * tile, tile), tile)
    cosine, sine = cos_ref[here, :], sin_ref[here, :]
    routes = [route_ref[:, j:j + 1] for j in range(TOPK)]
    gates = [gate_ref[:, j:j + 1] for j in range(TOPK)]
    allowed = kb_ref[...] <= jnp.concatenate([qb_ref[...]] * TOPK, axis=1)
    gate_grads = [jnp.zeros((tile, 1), F32) for _ in range(TOPK)]
    for head in range(width // HD):
        at = head * HD
        k, v = key_ref[:, at:at + HD], value_ref[:, at:at + HD]
        g = [chosen(g_ref, routes[j], n_e, width, at) for j in range(TOPK)]
        o = [o_ref[j, :, at:at + HD].astype(F32) for j in range(TOPK)]
        gate_grads = [gate_grads[j] + jnp.sum(g[j] * o[j], axis=1, keepdims=True) for j in range(TOPK)]
        d = jnp.concatenate([(gates[j] * g[j]).astype(BF) for j in range(TOPK)], axis=0)
        q = jnp.concatenate([query_ref[j, :, at:at + HD] for j in range(TOPK)], axis=0)
        centre = jnp.sum((d.astype(F32) * jnp.concatenate(o, axis=0)).T, axis=0, keepdims=True)
        s = dot_nt(k, q)
        p = jnp.where(allowed, jnp.exp2(s * (scale * LOG2E) - l_ref[0, head:head + 1, :]), 0.0)
        grad_s = (p * (dot_nt(v, d) - centre)).astype(BF)
        dq = (dot_tn(k, grad_s) * scale).T
        dq = [turn(dq[j * tile:(j + 1) * tile], cosine, -sine) for j in range(TOPK)]
        for e in range(n_e):
            parts = [jnp.where(routes[j] == e, dq[j], 0.0) for j in range(TOPK)]
            dq_ref[:, e * width + at:e * width + at + HD] = (parts[0] + parts[1]).astype(BF)
        dk_ref[:, at:at + HD] += dot(grad_s, q) * scale
        dv_ref[:, at:at + HD] += dot(p.astype(BF), d)
    lane = lax.broadcasted_iota(jnp.int32, (tile, HD), 1)
    note = jnp.zeros((tile, HD), F32)
    for j in range(TOPK):
        high = gate_grads[j].astype(BF).astype(F32)
        note = jnp.where(lane == j, high, note)
        note = jnp.where(lane == TOPK + j, gate_grads[j] - high, note)
    note_ref[...] = note.astype(BF)

    @pl.when(step == pl.num_programs(0) - 1)
    def _():
        for at in range(0, width, HD):
            dkv_ref[:, at:at + HD] = turn(dk_ref[:, at:at + HD], cos_ref[...], -sin_ref[...]).astype(BF)
        dkv_ref[:, width:] = dv_ref[...].astype(BF)


def attend_back(g_raw, routes, gates, queries, keys, values, mixed, log_total, cosine, sine, q_blocks, k_blocks):
    length, wide = g_raw.shape
    width = keys.shape[1]
    n_e, heads = wide // width, width // HD
    tile = 256
    whole = lambda *shape: pl.BlockSpec(shape, lambda i: (0,) * len(shape))
    tiled = lambda cols: pl.BlockSpec((tile, cols), lambda i: (i, 0))
    pair = pl.BlockSpec((TOPK, tile, width), lambda i: (0, i, 0))
    return pl.pallas_call(
        functools.partial(attend_back_kernel, n_e, HD ** -0.5),
        grid=(length // tile,),
        in_specs=[
            tiled(wide), tiled(TOPK), tiled(TOPK), pair, whole(length, width), whole(length, width), pair,
            pl.BlockSpec((1, heads, TOPK * tile), lambda i: (i, 0, 0)), whole(length, HD), whole(length, HD),
            pl.BlockSpec((1, tile), lambda i: (0, i)), whole(length, 1),
        ],
        out_specs=[tiled(wide), whole(length, 2 * width), tiled(HD)],
        out_shape=[
            jax.ShapeDtypeStruct((length, wide), BF),
            jax.ShapeDtypeStruct((length, 2 * width), BF),
            jax.ShapeDtypeStruct((length, HD), BF),
        ],
        scratch_shapes=[pltpu.VMEM((length, width), F32), pltpu.VMEM((length, width), F32)],
        cost_estimate=pl.CostEstimate(flops=length * length, transcendentals=0, bytes_accessed=8 * length * width),
        name="attend_back",
    )(g_raw, routes, gates, queries, keys, values, mixed, log_total, cosine, sine, q_blocks, k_blocks)


def expert_kernel(ready, cot_ref, slot_gate_ref, gate_w_ref, up_w_ref, down_ref, *refs):
    half = down_ref.shape[0]
    *refs, wide_ref, sems = refs

    @pl.when(pl.program_id(0) == 0)
    def _():
        copies = [
            pltpu.make_async_copy(ref, wide_ref.at[pl.ds(i * half, half)], sems.at[i])
            for i, ref in enumerate((gate_w_ref, up_w_ref))
        ]
        for copy in copies:
            copy.start()
        for copy in copies:
            copy.wait()

    if ready:
        gate_pre, up_pre = refs[0][...], refs[1][...]
        hidden_ref, grad_ref, back_ref, slot_ref = refs[2:]
    else:
        pre = dot_nt(wide_ref[...], refs[0][...])
        gate_pre, up_pre = pre[:half], pre[half:]
        hidden_ref, grad_ref, back_ref, slot_ref = refs[1:]
    grad_hidden = dot_nt(down_ref[...], cot_ref[...])
    sigma = 1.0 / (1.0 + jnp.exp(-gate_pre))
    silu = gate_pre * sigma
    hidden = silu * up_pre
    slot_ref[...] = jnp.sum(grad_hidden * hidden, axis=0, keepdims=True)
    gate = slot_gate_ref[...]
    grad_hidden = grad_hidden * gate
    hidden_ref[...] = (hidden * gate).astype(BF)
    grad_ref[:half] = (grad_hidden * up_pre * sigma * (1.0 + gate_pre * (1.0 - sigma))).astype(BF)
    grad_ref[half:] = (grad_hidden * silu).astype(BF)
    back_ref[...] = dot_tn(grad_ref[...], wide_ref[...]).astype(BF)


def expert_pass(cot_rows, gates, weights, down, sources):
    count, width = cot_rows.shape
    half = down.shape[0]
    tile = 256
    kept = lambda shape: pl.BlockSpec(shape, lambda i: (0, 0), pipeline_mode=pl.Buffered(1))
    tiled = pl.BlockSpec((tile, width), lambda i: (i, 0))
    turned = lambda size: pl.BlockSpec((size, tile), lambda i: (0, i))
    ready = len(sources) == 2
    return pl.pallas_call(
        functools.partial(expert_kernel, ready),
        grid=(count // tile,),
        in_specs=[tiled, turned(1)] + [pl.BlockSpec(memory_space=pl.ANY)] * 2 + [kept(down.shape)]
        + ([turned(half)] * 2 if ready else [tiled]),
        out_specs=[turned(half), turned(2 * half), tiled, turned(1)],
        out_shape=[
            jax.ShapeDtypeStruct((half, count), BF),
            jax.ShapeDtypeStruct((2 * half, count), BF),
            jax.ShapeDtypeStruct((count, width), BF),
            jax.ShapeDtypeStruct((1, count), F32),
        ],
        scratch_shapes=[pltpu.VMEM((2 * half, width), BF), pltpu.SemaphoreType.DMA((2,))],
        cost_estimate=pl.CostEstimate(
            flops=10 * count * width * half, transcendentals=count * half, bytes_accessed=6 * count * width + 6 * half * width
        ),
        name="expert_pass",
    )(cot_rows, gates, *weights, down, *sources)


def pick(table, routes, ids):
    parts = jnp.split(table, len(ids), axis=1)
    return [sum(jnp.where(routes[:, j:j + 1] == e, part, 0.0) for e, part in zip(ids, parts)) for j in range(TOPK)]


def place(pieces, routes, ids):
    return jnp.concatenate(
        [sum(jnp.where(routes[:, j:j + 1] == e, pieces[j], 0.0) for j in range(TOPK)) for e in ids], axis=1
    )


def pair_softmax(logits):
    peak = jnp.maximum(logits[0], logits[1])
    powers = [jnp.exp(v - peak) for v in logits]
    total = powers[0] + powers[1]
    return [v / total for v in powers]


def local(
    inputs, cotangent, blocks, attn_routes, ffn_routes, w_key, w_value, attn_router, ffn_router, attn_gain, ffn_gain,
    attn_bias, ffn_bias, w_query, w_out, w_gate, w_up, w_down,
):
    n_e, n_s = lax.axis_size("expert"), lax.axis_size("shard")
    me = lax.axis_index("expert")
    tokens, width = inputs.shape[1:]
    ids = list(range(n_e))
    capacity = 5 * tokens * TOPK // (4 * n_e)
    group = w_key.shape[1] // n_e
    length = n_e * tokens
    small_rows = w_key.shape[0]

    def swap(value, k):
        return lax.ppermute(value, "expert", [(i, i ^ k) for i in range(n_e)])

    def after(value, *others):
        return lax.optimization_barrier((value,) + others)[0]

    def spread(value):
        return jnp.concatenate([value] + [swap(value, k) for k in range(1, n_e)], axis=0)

    def fetch(block):
        return [block] + [swap(block, k) for k in range(1, 3 if n_e == 4 else n_e)]

    def fetch_rest(blocks, *others):
        if n_e != 4:
            return blocks
        half = blocks[0].shape[0] // 2
        one, two = after(blocks[1], *others), after(blocks[2], *others)
        return blocks + [jnp.concatenate([swap(one[:half], 2), swap(two[half:], 1)], axis=0)]

    def add_low(a, b):
        return (a.astype(F32) + b.astype(F32)).astype(BF)

    def deliver_first(far):
        return [swap(far[0], 1), swap(far[1], 2)] if n_e == 4 else []

    def deliver_near(parts):
        if n_e != 4:
            return [swap(parts[k][i], k) for i in range(2) for k in range(1, n_e)]
        return [swap(parts[1][0], 1), swap(parts[2][1], 2)]

    def deliver_last(parts, halves):
        if n_e != 4:
            return []
        return [swap(add_low(parts[2][0], halves[0]), 2), swap(add_low(parts[1][1], halves[1]), 1)]

    def total(own, near, last):
        count = len(near) // 2
        return [
            sum(v.astype(F32) for v in [own[i]] + near[i * count:(i + 1) * count] + last[i:i + 1]) for i in range(2)
        ]

    def collect(value):
        parts = jnp.split(value, n_e, axis=0)
        return sum([parts[0].astype(F32)] + [swap(parts[k], k).astype(F32) for k in range(1, n_e)])

    def shuffle(value, axis):
        return lax.all_to_all(value, axis, split_axis=0, concat_axis=0, tiled=True)

    def trade(value):
        out = jnp.zeros_like(value)
        for k in range(n_e):
            piece = lax.dynamic_index_in_dim(value, me ^ k, 0, False)
            out = lax.dynamic_update_index_in_dim(out, swap(piece, k) if k else piece, me ^ k, 0)
        return out

    def gather_shard(value):
        return lax.all_gather(value, "shard", axis=0, tiled=True)

    def scatter_shard(value):
        return lax.psum_scatter(value, "shard", scatter_dimension=0, tiled=True)

    small = jnp.concatenate(
        [attn_router, ffn_router, attn_gain[:, None], ffn_gain[:, None], attn_bias[:, None], ffn_bias[:, None]], axis=1
    )
    small_width = small.shape[1]
    route_width = tokens * TOPK // (n_e * small_rows)
    small = jnp.pad(small, ((0, 0), (0, 128 - small_width)))
    packed = jnp.concatenate(
        [
            w_key.reshape(small_rows, n_e, group).transpose(1, 0, 2),
            w_value.reshape(small_rows, n_e, group).transpose(1, 0, 2),
            jnp.broadcast_to(small[None], (n_e,) + small.shape),
        ],
        axis=2,
    )
    packed = shuffle(packed, "expert")
    route_at = 2 * group + small_width
    packed = packed.at[:, :, route_at:route_at + route_width].set(
        ffn_routes[0].astype(BF).reshape(n_e, small_rows, route_width)
    )
    packed = gather_shard(packed[None])
    routes_f = packed[:, :, :, route_at:route_at + route_width].reshape(n_s * tokens, TOPK).astype(jnp.int32)
    packed = packed.transpose(1, 0, 2, 3).reshape(width, -1)
    key_value_w = packed[:, :2 * group]
    small = packed[:, 2 * group:2 * group + small_width].astype(F32)
    router_a, router_f = small[:, :n_e], small[:, n_e:2 * n_e]
    gain_a, gain_f, bias_a, bias_f = (small[:, 2 * n_e + i] for i in range(4))

    def to_heads(value):
        rows = value.shape[0]
        value = shuffle(value.reshape(rows, n_e, group).transpose(1, 0, 2), "expert")
        return value.transpose(1, 0, 2).reshape(rows, n_e * group)

    def from_heads(value):
        rows = value.shape[0]
        value = trade(value.reshape(rows, n_e, group).transpose(1, 0, 2))
        return value.transpose(1, 0, 2).reshape(rows, n_e * group)

    notes = jnp.concatenate([blocks[0][:, None], attn_routes[0]], axis=1).astype(BF)
    carried = jnp.concatenate([inputs[0], jnp.pad(notes, ((0, 0), (0, 128 - 1 - TOPK)))], axis=1)
    carried, down_w = lax.optimization_barrier((spread(carried), w_down[0]))
    query_w = gather_shard(to_heads(w_query[0]))

    hidden_units = w_down.shape[1]
    turned = jnp.stack([w_gate[0].T.reshape(n_s, hidden_units, -1), w_up[0].T.reshape(n_s, hidden_units, -1)], axis=1)
    down_w = fetch(down_w)
    turned, query_w = lax.optimization_barrier((turned, query_w))
    turned = shuffle(turned, "shard").reshape(n_s, 2 * hidden_units, -1)
    gate_up_own = [
        turned[:, i * hidden_units:(i + 1) * hidden_units].transpose(1, 0, 2).reshape(hidden_units, width) for i in range(2)
    ]

    own = inputs[0].astype(F32)
    cot = cotangent[0]
    seq_in = carried[:, :width].astype(F32)
    notes = carried[:, width:width + 1 + TOPK].astype(jnp.int32)
    seq_blocks, routes_a = notes[:, 0], notes[:, 1:]
    position = jnp.concatenate([(me ^ k) * tokens + jnp.arange(tokens, dtype=jnp.int32) for k in range(n_e)]).astype(F32)
    cosine, sine = rope_tables(position)
    h_attn = (seq_in * inverse_rms(seq_in) * gain_a).astype(BF)
    logits_a = dot(h_attn, router_a.astype(BF))
    gates_a = pair_softmax(pick(logits_a, routes_a, ids))
    key_value = dot(h_attn, key_value_w)
    key_value, out_w = lax.optimization_barrier((key_value, w_out[0]))
    out_rows = out_w.shape[0]
    turned = shuffle(out_w.T, "shard").reshape(n_s, width // n_s, out_rows).transpose(1, 0, 2)
    turned = to_heads(turned.reshape(width // n_s, n_s * out_rows))
    turned, *down_w = lax.optimization_barrier((turned, *down_w))
    down_w = fetch_rest(down_w)
    out_wt = gather_shard(turned)
    gate_pair = jnp.concatenate(gates_a, axis=1)
    row_blocks, key_blocks = seq_blocks.reshape(1, -1), seq_blocks.reshape(-1, 1)
    query_raw = dot(h_attn, query_w)
    queries, keys, values, mixed, log_total, mixed_all = attend(
        query_raw, key_value, routes_a, gate_pair, cosine, sine, row_blocks, key_blocks
    )
    mixed_out, *down_w = lax.optimization_barrier((mixed_all, *down_w))
    middle = own + collect(dot_nt(mixed_out, out_wt).astype(BF)) + bias_a

    inv_f = inverse_rms(middle)
    h_ffn = (middle * inv_f * gain_f).astype(BF)
    h_ffn, gate_up_own = lax.optimization_barrier((h_ffn, gate_up_own))
    gate_w, up_w = fetch(gate_up_own[0]), fetch(gate_up_own[1])
    h_all = gather_shard(h_ffn)
    cot_all = gather_shard(after(cot, h_ffn))
    logits_f = dot(h_all, router_f.astype(BF))
    gates_f = pair_softmax(pick(logits_f, routes_f, ids))
    routes_blocks = routes_f.reshape(n_s, tokens, TOPK)
    h_blocks = h_all.reshape(n_s, tokens, width)
    triangle = (jnp.arange(tokens)[:, None] <= jnp.arange(tokens)[None, :]).astype(BF)

    def rows_of(select, source):
        return lax.dot_general(
            select, source, (((2,), (1,)), ((0,), (0,))), preferred_element_type=F32
        ).astype(BF).reshape(n_s * capacity, width)

    selects, hiddens, back_rows_f = [], [], []
    grad_gate_f = [0.0] * TOPK
    grad_pieces = []
    all_rows = []
    for k in range(n_e):
        expert = me ^ k
        named = [routes_blocks[:, :, j] == expert for j in range(TOPK)]
        any_named = named[0] | named[1]
        rank = dot(any_named.astype(BF), triangle).astype(jnp.int32) - 1
        hit = (rank[:, None, :] == jnp.arange(capacity, dtype=jnp.int32)[None, :, None]) & any_named[:, None, :]
        gate_token = sum(jnp.where(named[j], gates_f[j].reshape(n_s, tokens), 0.0) for j in range(TOPK))
        gate_slot = jnp.sum(jnp.where(hit, gate_token[:, None, :], 0.0), axis=2).reshape(1, -1)
        all_rows.append((named, hit, gate_slot, rows_of(hit.astype(BF), h_blocks)))
    ahead = [[dot_nt(gate_w[k], all_rows[k][3]), dot_nt(up_w[k], all_rows[k][3])] for k in range(2)]
    cot_all, all_rows, gate_w, up_w, ahead = lax.optimization_barrier((cot_all, all_rows, gate_w, up_w, ahead))
    cot_blocks = cot_all.reshape(n_s, tokens, width)
    if n_e == 4:
        gate_w, up_w = gate_w + [swap(gate_w[1], 2)], up_w + [swap(up_w[2], 1)]
    for k in range(n_e):
        named, hit, gate_slot, rows = all_rows[k]
        select = hit.astype(BF)
        cot_rows = rows_of(select, cot_blocks)
        if k == 2 and n_e == 4:
            cot_rows, gate_w[3], up_w[3] = lax.optimization_barrier((cot_rows, gate_w[3], up_w[3]))
        hidden, grad_pre, back, grad_slot = expert_pass(
            cot_rows, gate_slot, (gate_w[k], up_w[k]), down_w[k], ahead[k] if k < len(ahead) else [rows]
        )
        grad_slot = grad_slot.reshape(n_s, capacity)
        selects.append(select)
        back_rows_f.append(back.reshape(n_s, capacity, width))
        hiddens.append(hidden)
        grad_token = jnp.sum(jnp.where(hit, grad_slot[:, :, None], 0.0), axis=1)
        grad_gate_f = [grad_gate_f[j] + jnp.where(named[j], grad_token, 0.0) for j in range(TOPK)]
        grad_pieces.append((rows, cot_rows, grad_pre))
    select = jnp.concatenate(selects, axis=1)

    def tokens_of(row_list):
        return lax.dot_general(
            select, jnp.concatenate(row_list, axis=1), (((1,), (1,)), ((0,), (0,))), preferred_element_type=F32
        ).astype(BF).reshape(n_s * tokens, width)

    back_sum = tokens_of(back_rows_f)
    back_f = scatter_shard(back_sum)

    def gate_up_grads(k, *others):
        rows, _, grad_pre = grad_pieces[k]
        rows = after(rows, *others)
        return [dot(v, rows).astype(BF) for v in jnp.split(grad_pre, 2, axis=0)]

    grad_gate_up = [None] * n_e
    grad_gate_up[n_e - 1] = gate_up_grads(n_e - 1, back_sum)
    halves = deliver_first(grad_gate_up[n_e - 1])
    gate_grads_f = shuffle(jnp.stack(grad_gate_f, axis=1).reshape(n_s, TOPK * tokens), "shard")
    out_rows_f = []
    for k in range(n_e):
        hidden = after(hiddens[k], *grad_gate_up[n_e - 1])
        out_rows_f.append(dot_tn(hidden, down_w[k]).astype(BF).reshape(n_s, capacity, width))
    for j in range(1, n_e - 1):
        grad_gate_up[j] = gate_up_grads(j, back_sum)

    def logit_grads(gates, grads, routes):
        centre = sum(gates[j] * grads[j] for j in range(TOPK))
        return place([gates[j] * (grads[j] - centre) for j in range(TOPK)], routes, ids)

    own_routes_f = ffn_routes[0]
    own_gates_f = pair_softmax(pick(dot(h_ffn, router_f.astype(BF)), own_routes_f, ids))
    grad_gates_f = jnp.sum(gate_grads_f, axis=0).reshape(TOPK, tokens, 1)
    grad_logits_f = logit_grads(own_gates_f, grad_gates_f, own_routes_f)
    out_rows_f, halves, grad_gate_up[1:], grad_logits_f = lax.optimization_barrier(
        (out_rows_f, halves, grad_gate_up[1:], grad_logits_f)
    )
    out_sum = tokens_of(out_rows_f)
    ffn_out = scatter_shard(out_sum)
    back_f, out_sum = lax.optimization_barrier((back_f, out_sum))
    back_f = back_f.astype(F32)
    grad_out = cot.astype(F32)
    grad_router_f = dot_tn(h_ffn.astype(F32), grad_logits_f, PRECISE)
    grad_h_ffn = back_f + jnp.dot(grad_logits_f, router_f.T, precision=PRECISE)
    grad_norm, grad_gain_f = norm_back(grad_h_ffn, middle, inv_f, gain_f)
    grad_middle = grad_out + grad_norm
    grad_bias_f = jnp.sum(grad_out, axis=0)
    grad_bias_a = jnp.sum(grad_middle, axis=0)

    grad_middle_low = grad_middle.astype(BF)
    grad_gate_up[0] = gate_up_grads(0, back_f)
    seq_grad = spread(grad_middle_low)
    seq_grad, grad_gate_up = lax.optimization_barrier((seq_grad, grad_gate_up))
    near = deliver_near(grad_gate_up)
    last = deliver_last(grad_gate_up, halves)
    grad_mixed = dot(seq_grad, out_wt)
    grad_out_wt = dot_tn(seq_grad, mixed_all).astype(BF)
    grad_mixed, grad_out_wt = lax.optimization_barrier((grad_mixed, grad_out_wt))
    grad_query_all, grad_key_value, gate_notes = attend_back(
        grad_mixed, routes_a, gate_pair, queries, keys, values, mixed, log_total, cosine, sine, row_blocks, key_blocks
    )
    key_value_grad, query_grad = dot_tn(h_attn, grad_key_value).astype(BF), dot_tn(h_attn, grad_query_all).astype(BF)
    grad_query_all, key_value_grad, query_grad, *near = lax.optimization_barrier(
        (grad_query_all, key_value_grad, query_grad, *near)
    )
    back_a = (dot_nt(grad_query_all, query_w) + dot_nt(grad_key_value, key_value_w)).astype(BF)
    back_a = jnp.concatenate([back_a, gate_notes], axis=1)
    value = scatter_shard(grad_out_wt)
    back_a, ffn_out, value, *last = lax.optimization_barrier((back_a, ffn_out, value, *last))
    gate_up_total = [v.astype(BF) for v in total(grad_gate_up[0], near, last)]
    outputs = (middle + ffn_out.astype(F32) + bias_f).astype(BF)[None]
    key_value_grad = key_value_grad.reshape(n_e, n_s, small_rows, 2 * group).transpose(1, 0, 2, 3)
    key_value_grad = scatter_shard(key_value_grad.reshape(n_s * n_e * small_rows, 2 * group))
    query_grad = scatter_shard(query_grad)
    out_part = from_heads(value).reshape(width // n_s, n_s, out_rows).transpose(1, 0, 2)

    def to_rows(value):
        value = shuffle(value.reshape(hidden_units, n_s, width // n_s).transpose(1, 0, 2), "shard")
        return value.reshape(n_s * hidden_units, width // n_s)

    gate_turned = to_rows(gate_up_total[0])
    grad_down = []
    for k in range(n_e):
        hidden = after(hiddens[k], back_a)
        grad_down.append([dot(v, grad_pieces[k][1]).astype(BF) for v in jnp.split(hidden, 2, axis=0)])
    halves = deliver_first(grad_down[n_e - 1])
    back_a = collect(back_a)
    near, last = deliver_near(grad_down), deliver_last(grad_down, halves)
    back_a, gate_turned, *near = lax.optimization_barrier((back_a, gate_turned, *near))
    up_total, key_value_grad = lax.optimization_barrier((after(gate_up_total[1], gate_turned), key_value_grad))
    up_turned = to_rows(up_total)
    grad_down_w = jnp.concatenate(total(grad_down[0], near, last), axis=0)[None]
    key_value_grad = trade(key_value_grad.reshape(n_e, small_rows, -1))
    grad_key_w = key_value_grad[:, :, :group].transpose(1, 0, 2).reshape(small_rows, -1).astype(F32)
    grad_value_w = key_value_grad[:, :, group:].transpose(1, 0, 2).reshape(small_rows, -1).astype(F32)
    gate_grads = back_a[:, width:width + TOPK] + back_a[:, width + TOPK:width + 2 * TOPK]
    grad_gates_a = [gate_grads[:, j:j + 1] for j in range(TOPK)]
    back_a = back_a[:, :width]
    grad_query_w = from_heads(query_grad)
    grad_gate_w = gate_turned.T.astype(F32)[None]

    h_own = h_attn[:tokens]
    own_routes_a = attn_routes[0]
    own_gates_a = [v[:tokens] for v in gates_a]
    grad_logits_a = logit_grads(own_gates_a, grad_gates_a, own_routes_a)
    grad_router_a = dot_tn(h_own.astype(F32), grad_logits_a, PRECISE)
    grad_h_attn = back_a + jnp.dot(grad_logits_a, router_a.T, precision=PRECISE)
    grad_norm, grad_gain_a = norm_back(grad_h_attn, own, inverse_rms(own), gain_a)
    input_grad = (grad_middle + grad_norm).astype(BF)[None]

    shared = jnp.concatenate(
        [grad_router_a, grad_router_f]
        + [v[:, None] for v in (grad_gain_a, grad_gain_f, grad_bias_a, grad_bias_f)],
        axis=1,
    )
    shared, up_turned, grad_query_w, value = lax.optimization_barrier((shared, up_turned, grad_query_w, out_part))
    grad_out_w = shuffle(value, "shard").reshape(width, out_rows).T.astype(F32)[None]
    grad_query_w = grad_query_w.astype(F32)[None]
    grad_up_w = up_turned.T.astype(F32)[None]
    shared = shuffle(shared.reshape(n_e * n_s, -1), ("expert", "shard"))
    shared = jnp.sum(shared, axis=0).reshape(small_rows, small_width)
    return (
        outputs,
        input_grad,
        grad_key_w,
        grad_value_w,
        shared[:, :n_e],
        shared[:, n_e:2 * n_e],
        shared[:, 2 * n_e],
        shared[:, 2 * n_e + 1],
        shared[:, 2 * n_e + 2],
        shared[:, 2 * n_e + 3],
        grad_query_w,
        grad_out_w,
        grad_gate_w,
        grad_up_w,
        grad_down_w,
    )


def solution(mesh):
    rows = P("shard", "expert", None)
    shared, vector = P(("expert", "shard"), None), P(("expert", "shard"))
    weight = P("expert", "shard", None)
    in_specs = (rows, rows, P("shard", "expert"), rows, rows) + (shared,) * 4 + (vector,) * 4 + (weight,) * 5
    out_specs = (rows, rows) + (shared,) * 4 + (vector,) * 4 + (weight,) * 5
    return jax.shard_map(local, mesh=mesh, in_specs=in_specs, out_specs=out_specs, check_vma=False)
```
